32 devices in a mesh: seq: 8 (over z, x), exp: 4 (over y, core).
Axes of the slice: x: 2, y: 2, z: 4, core: 2. Of those that a mesh axis runs over, the one named last changes fastest.
Arguments:
- residual: bfloat16 [4096, 8192], P('seq', 'exp'), may hold values from -16 to 16
- queries: bfloat16 [4096, 4096], P('seq', 'exp'), may hold values from -6 to 6
- keys: bfloat16 [4096, 4096], P('seq', 'exp'), may hold values from -10 to 10
- values: bfloat16 [4096, 4096], P('seq', 'exp'), may hold values from -6 to 6
- documents: int32 [4096], replicated, may hold values from 0 to 1, as said below
- out_proj: bfloat16 [4096, 8192], P(None, 'exp'), may hold values from -0.09375 to 0.09375
- modality: int32 [4096], P('seq'), may hold values from 0 to 1, as said below
- norm_gain: float32 [2, 8192], P(None, 'exp'), may hold values from 0.25 to 1.75
- picks: int32 [4, 64], replicated, may hold values from 0 to 4095, as said below
- router: bfloat16 [8192, 4], P(None, 'exp'), may hold values from -0.0625 to 0.0625
- w_gate: bfloat16 [4, 8192, 4096], P('exp', None, 'seq'), may hold values from -0.0625 to 0.0625
- w_up: bfloat16 [4, 8192, 4096], P('exp', None, 'seq'), may hold values from -0.0625 to 0.0625
- w_down: bfloat16 [4, 4096, 8192], P('exp', 'seq'), may hold values from -0.09375 to 0.09375
Outputs:
- layer_out: bfloat16 [4096, 8192], P('seq', 'exp')
The draws below stay inside these ranges and needn't reach their ends.
Inputs may be any that keep to these rules, and one draw needn't show every extreme that they name: `modality`: 0 marks a text token, 1 an image token. `documents`: 0 for the first document, 1 for the second; the second begins between position 1024 and 3072. `picks`: row e lists 64 different positions in ascending order; all carry modality 0 for e < 2 and modality 1 otherwise. Within each aligned block of 512 positions (the tokens of one index of seq) a row lists at most 16 positions, and every row lists exactly 16 in some block.
All inputs are finite; a program needn't handle non-finite values.
Results may differ from the reference program's by a relative error of at most 0.0035.
Values may be sent and summed in bfloat16 or wider, within the bound.
A program may use at most 128 MiB of HBM per device.

```python
import math
import jax
import jax.numpy as jnp
from jax import lax

D = 8192
HEADS = 32
HD = 128
FF = 4096
TOK_DEV = 512
TOKENS = 4096
EXPERTS = 4
CB = 16
CAP = 64
N_SEQ = 8


def layout_draw(base_key):
    own_key = jax.random.fold_in(base_key, 11)
    span_key, force_key, pick_key = jax.random.split(own_key, 3)
    spans = 8
    span_len = TOK_DEV // spans
    span_bits = jax.random.randint(span_key, (N_SEQ, spans), 0, 2)
    one_key, two_key = jax.random.split(force_key)
    fixed_one = jax.random.randint(one_key, (N_SEQ,), 0, spans)
    offset = jax.random.randint(two_key, (N_SEQ,), 1, spans)
    second = (fixed_one + offset) % spans
    span_pos = jnp.arange(spans)
    span_bits = jnp.where(span_pos[None, :] == fixed_one[:, None], 0, span_bits)
    span_bits = jnp.where(span_pos[None, :] == second[:, None], 1, span_bits)
    modal_tags = jnp.repeat(span_bits, span_len, axis=1).astype(jnp.int32)
    flat_index = jnp.arange(TOKENS, dtype=jnp.int32)
    half_cap = CB // 2
    chosen_lists = []
    for expert in range(EXPERTS):
        modal_kind = 0 if expert < EXPERTS // 2 else 1
        order_key, shift_key, rank_key = jax.random.split(jax.random.fold_in(pick_key, expert), 3)
        shard_order = jax.random.permutation(order_key, N_SEQ)
        shift_size = jax.random.randint(shift_key, (N_SEQ // 2,), 0, half_cap + 1)
        shift_size = shift_size.at[0].set(half_cap)
        quota_rows = jnp.zeros((N_SEQ,), jnp.int32)
        quota_rows = quota_rows.at[shard_order[0::2]].set(half_cap + shift_size)
        quota_rows = quota_rows.at[shard_order[1::2]].set(half_cap - shift_size)
        shuffled = jax.vmap(lambda sub_key: jax.random.permutation(sub_key, TOK_DEV))(jax.random.split(rank_key, N_SEQ))
        sort_keys = jnp.where(modal_tags == modal_kind, shuffled, TOK_DEV + shuffled)
        rank_in = jnp.argsort(jnp.argsort(sort_keys, axis=1), axis=1)
        chosen = (rank_in < quota_rows[:, None]).reshape(TOKENS)
        listed = jnp.argsort(jnp.where(chosen, flat_index, TOKENS + flat_index))[:CAP]
        chosen_lists.append(listed.astype(jnp.int32))
    return (modal_tags.reshape(TOKENS), jnp.stack(chosen_lists))


def draw_modality(key, part):
    return layout_draw(key)[0]


def draw_picks(key, part):
    return layout_draw(key)[1]


def draw_documents(key, part):
    boundary = jax.random.randint(jax.random.fold_in(key, 5), (), TOKENS // 4, 3 * TOKENS // 4 + 1)
    return (jnp.arange(TOKENS) >= boundary).astype(jnp.int32)


def draw_queries(key, part):
    base_key = jax.random.fold_in(key, 31)
    base_draw = jnp.clip(jax.random.normal(base_key, (TOKENS, HEADS * HD), jnp.float32), -6.0, 6.0)
    return base_draw.astype(jnp.bfloat16)


def draw_keys(key, part):
    base_key = jax.random.fold_in(key, 41)
    base_draw = jnp.clip(2.5 * jax.random.normal(base_key, (TOKENS, HEADS * HD), jnp.float32), -10.0, 10.0)
    return base_draw.astype(jnp.bfloat16)


def draw_residual(key, part):
    base_key = jax.random.fold_in(jax.random.fold_in(key, 51), 0)
    rising = 0.6 + 1.2 * jnp.arange(D, dtype=jnp.float32) / D
    base_draw = jnp.clip(jax.random.normal(base_key, (TOKENS, D), jnp.float32), -4.0, 4.0)
    result = base_draw * rising[None, :]
    return jnp.clip(result, -16.0, 16.0).astype(jnp.bfloat16)


def shard_levels(key, extent, shards, smallest, top_value):
    def one(position, blocks):
        heights = jax.random.uniform(jax.random.fold_in(jax.random.fold_in(key, 6), position), (blocks,), jnp.float32, smallest / len(shards), top_value / len(shards))
        return jnp.repeat(jnp.exp(heights), extent[position] // blocks).reshape((-1,) + (1,) * (len(extent) - position - 1))

    gain = one(*shards[0])
    for cut in shards[1:]:
        gain = gain * one(*cut)
    return gain


def bell_draw(key, extent, deviation, limit, cuts=(), kind=jnp.bfloat16):
    level = shard_levels(key, extent, cuts, -0.22, 0.18) if cuts else 1.0
    entries = jax.random.normal(key, extent, jnp.float32) * deviation * level
    return jnp.minimum(jnp.maximum(entries, -limit), limit).astype(kind)


def setup_inputs(seed: int = 0) -> dict:
    arg_keys = jax.random.split(jax.random.key(seed), 14)
    return {
        "residual": draw_residual(jax.random.fold_in(arg_keys[13], 71), 0),
        "queries": draw_queries(jax.random.fold_in(arg_keys[13], 71), 0),
        "keys": draw_keys(jax.random.fold_in(arg_keys[13], 71), 0),
        "values": bell_draw(arg_keys[3], (TOKENS, HEADS * HD), 1.0, 6.0, ((0, 8), (1, 4))),
        "documents": draw_documents(jax.random.fold_in(arg_keys[13], 71), 0),
        "out_proj": bell_draw(arg_keys[5], (HEADS * HD, D), (HEADS * HD) ** -0.5, 0.09375, ((1, 4),)),
        "modality": draw_modality(jax.random.fold_in(arg_keys[13], 71), 0),
        "norm_gain": jnp.clip(1.0 + 0.15 * jax.random.normal(arg_keys[7], (2, D), jnp.float32), 0.25, 1.75),
        "picks": draw_picks(jax.random.fold_in(arg_keys[13], 71), 0),
        "router": bell_draw(arg_keys[9], (D, EXPERTS), D ** -0.5, 0.0625, ((1, 4),)),
        "w_gate": bell_draw(arg_keys[10], (EXPERTS, D, FF), D ** -0.5, 0.0625, ((0, 4), (2, 8))),
        "w_up": bell_draw(arg_keys[11], (EXPERTS, D, FF), D ** -0.5, 0.0625, ((0, 4), (2, 8))),
        "w_down": bell_draw(arg_keys[12], (EXPERTS, FF, D), FF ** -0.5, 0.09375, ((0, 4), (1, 8))),
    }


def reference(residual, queries, keys, values, documents, out_proj, modality, norm_gain, picks, router, w_gate, w_up, w_down):
    length = queries.shape[0]
    q_heads = queries.reshape(length, HEADS, HD).transpose(1, 0, 2)
    k_heads = keys.reshape(length, HEADS, HD).transpose(1, 0, 2)
    v_heads = values.reshape(length, HEADS, HD).transpose(1, 0, 2)
    positions = jnp.arange(length, dtype=jnp.int32)
    allowed = (positions[None, :] <= positions[:, None]) & (documents[None, :] == documents[:, None])

    def one_head(item):
        q_one, k_one, v_one = item
        scores = jnp.dot(q_one, k_one.T, preferred_element_type=jnp.float32) / math.sqrt(HD)
        scores = jnp.where(allowed, scores, -jnp.inf)
        row_max = lax.optimization_barrier(jnp.max(scores, axis=1))
        probs = jnp.exp(scores - row_max[:, None])
        denominator = lax.optimization_barrier(jnp.sum(probs, axis=1))
        numerator = jnp.dot(probs.astype(jnp.bfloat16), v_one, preferred_element_type=jnp.float32)
        return (numerator / denominator[:, None]).astype(jnp.bfloat16)
    attended = lax.map(one_head, (q_heads, k_heads, v_heads))
    attended = attended.transpose(1, 0, 2).reshape(length, HEADS * HD)
    hidden_state = (residual.astype(jnp.float32) + jnp.dot(attended, out_proj, preferred_element_type=jnp.float32)).astype(jnp.bfloat16)
    hidden_wide = hidden_state.astype(jnp.float32)
    mean_square = lax.optimization_barrier(jnp.mean(hidden_wide * hidden_wide, axis=1))
    gain_rows = norm_gain[modality]
    normed = (hidden_wide * lax.rsqrt(mean_square + 1e-05)[:, None] * gain_rows).astype(jnp.bfloat16)
    expert_add = jnp.zeros((length, D), jnp.float32)
    for expert in range(EXPERTS):
        chosen = normed[picks[expert]]
        gate_part = jnp.dot(chosen, w_gate[expert], preferred_element_type=jnp.float32)
        up_part = jnp.dot(chosen, w_up[expert], preferred_element_type=jnp.float32)
        inner_act = (jax.nn.silu(gate_part) * up_part).astype(jnp.bfloat16)
        summed = jnp.dot(inner_act, w_down[expert], preferred_element_type=jnp.float32)
        logits = jnp.dot(chosen, router[:, expert:expert + 1], preferred_element_type=jnp.float32)[:, 0]
        weighted = (jax.nn.sigmoid(logits)[:, None] * summed).astype(jnp.bfloat16)
        expert_add = expert_add.at[picks[expert]].add(weighted.astype(jnp.float32))
    return (hidden_wide + expert_add).astype(jnp.bfloat16)
```

```python
import functools
import math

import jax
import jax.numpy as jnp
from jax import lax
from jax.experimental import pallas as pl
from jax.experimental.pallas import tpu as pltpu
from jax.sharding import PartitionSpec as P

D = 8192
HD = 128


block_rows = 512


MESH = pl.DeviceIdType.MESH


def greet(peers):
    barrier = pltpu.get_barrier_semaphore()
    for peer in peers:
        pl.semaphore_signal(barrier, inc=1, device_id=peer, device_id_type=MESH)
    pl.semaphore_wait(barrier, len(peers))


def cut(start, size):
    return pl.ds(pl.multiple_of(start, size), size)


def heads_out_kernel(n, width, q_ref, k_ref, v_ref, qo, ko, vo, send, recv, own):
    me = lax.axis_index("seq")
    tokens = q_ref.shape[0]
    greet([{"seq": lax.rem(me + i, n)} for i in range(1, n)])
    pairs = ((k_ref, ko), (v_ref, vo), (q_ref, qo))
    copies = []
    for i in range(1, n):
        to = lax.rem(me + i, n)
        for t, (src, dst) in enumerate(pairs):
            copies.append(
                pltpu.make_async_remote_copy(
                    src_ref=src.at[:, cut(to * width, width)],
                    dst_ref=dst.at[cut(me * tokens, tokens), :],
                    send_sem=send.at[t * n + i],
                    recv_sem=recv.at[t * n + i],
                    device_id={"seq": to},
                    device_id_type=MESH,
                )
            )
            copies[-1].start()
    for t, (src, dst) in enumerate(pairs):
        copies.append(
            pltpu.make_async_copy(
                src.at[:, cut(me * width, width)], dst.at[cut(me * tokens, tokens), :], own.at[t]
            )
        )
        copies[-1].start()
    for copy in copies:
        copy.wait()


def heads_out(queries, keys, values, n):
    tokens, columns = queries.shape
    width = columns // n
    whole = jax.ShapeDtypeStruct((n * tokens, width), queries.dtype)
    anywhere = pl.BlockSpec(memory_space=pl.ANY)
    return pl.pallas_call(
        functools.partial(heads_out_kernel, n, width),
        out_shape=(whole, whole, whole),
        in_specs=[anywhere] * 3,
        out_specs=(anywhere,) * 3,
        scratch_shapes=[
            pltpu.SemaphoreType.DMA((3 * n,)),
            pltpu.SemaphoreType.DMA((3 * n,)),
            pltpu.SemaphoreType.DMA((3,)),
        ],
        compiler_params=pltpu.CompilerParams(collective_id=0, has_side_effects=True),
    )(queries, keys, values)


def heads_back_kernel(n, ny, width, a_ref, o_ref, s_send, s_recv, y_send, y_recv, c_send, c_recv, own):
    me = lax.axis_index("seq")
    place = lax.axis_index("exp")
    y, core = place // 2, lax.rem(place, 2)
    sibling = {"exp": y * 2 + 1 - core}
    across = [{"exp": lax.rem(y + k, ny) * 2 + core} for k in range(1, ny)]
    tokens = o_ref.shape[0]
    span = n * width
    greet([{"seq": lax.rem(me + i, n)} for i in range(1, n)] + across + [sibling])

    def piece(exp_at, seq_at):
        return o_ref.at[:, cut(exp_at * span + seq_at * width, width)]

    local = pltpu.make_async_copy(a_ref.at[cut(me * tokens, tokens), :], piece(place, me), own)
    local.start()
    first = []
    for i in range(1, n):
        to = lax.rem(me + i, n)
        first.append(
            push(
                a_ref.at[cut(to * tokens, tokens), :],
                piece(place, me),
                s_send.at[i],
                s_recv.at[i],
                {"seq": to},
            )
        )
    second = []
    third = []
    for i in range(n):
        if i == 0:
            local.wait()
        else:
            first[i - 1].wait_recv()
        part = piece(place, lax.rem(me + n - i, n))
        for k in range(1, ny):
            at = i * ny + k
            second.append(push(part, part, y_send.at[at], y_recv.at[at], across[k - 1]))
        third.append(push(part, part, c_send.at[i * ny], c_recv.at[i * ny], sibling))
    for i in range(n):
        for k in range(1, ny):
            second[i * (ny - 1) + k - 1].wait_recv()
            at = i * ny + k
            part = piece(lax.rem(y + ny - k, ny) * 2 + core, lax.rem(me + n - i, n))
            third.append(push(part, part, c_send.at[at], c_recv.at[at], sibling))
    for copy in third:
        copy.wait_recv()
    for copy in first + second + third:
        copy.wait_send()


def heads_back(attended, n, n_exp):
    rows, width = attended.shape
    ny = n_exp // 2
    anywhere = pl.BlockSpec(memory_space=pl.ANY)
    return pl.pallas_call(
        functools.partial(heads_back_kernel, n, ny, width),
        out_shape=jax.ShapeDtypeStruct((rows // n, n_exp * n * width), attended.dtype),
        in_specs=[anywhere],
        out_specs=anywhere,
        scratch_shapes=[
            pltpu.SemaphoreType.DMA((n,)),
            pltpu.SemaphoreType.DMA((n,)),
            pltpu.SemaphoreType.DMA((n * ny,)),
            pltpu.SemaphoreType.DMA((n * ny,)),
            pltpu.SemaphoreType.DMA((n * ny,)),
            pltpu.SemaphoreType.DMA((n * ny,)),
            pltpu.SemaphoreType.DMA(()),
        ],
        compiler_params=pltpu.CompilerParams(collective_id=1, has_side_effects=True),
    )(attended)


def push(src, dst, send, recv, peer):
    copy = pltpu.make_async_remote_copy(
        src_ref=src, dst_ref=dst, send_sem=send, recv_sem=recv, device_id=peer, device_id_type=MESH
    )
    copy.start()
    return copy


def lines(me, nz):
    z, x = me // 2, lax.rem(me, 2)
    along = [{"seq": lax.rem(z + k, nz) * 2 + x} for k in range(1, nz)]
    return z, x, along, {"seq": z * 2 + 1 - x}


def ring_device(pos, n):
    half = pos // (n // 2)
    return (1 - half) * pos * 2 + half * ((n - 1 - pos) * 2 + 1)


def rows_kernel(n, ne, cap, width, r_ref, o_ref, e_send, e_recv, s_send, s_recv, own):
    me = lax.axis_index("seq")
    place = lax.axis_index("exp")
    z, x = me // 2, lax.rem(me, 2)
    pos = (1 - x) * z + x * (n - 1 - z)
    ways = (1, n - 1)
    nexts = [{"seq": ring_device(lax.rem(pos + way, n), n)} for way in ways]
    others = [{"exp": lax.rem(place + i, ne)} for i in range(1, ne)]
    greet(others + nexts)

    def piece(seq_at, exp_at):
        return o_ref.at[cut(seq_at * cap, cap), cut(exp_at * width, width)]

    local = pltpu.make_async_copy(r_ref.at[cut(place * cap, cap), :], piece(me, place), own)
    local.start()
    first = []
    for i in range(1, ne):
        src = r_ref.at[cut(lax.rem(place + i, ne) * cap, cap), :]
        first.append(push(src, piece(me, place), e_send.at[i], e_recv.at[i], others[i - 1]))
    hops = {}
    for t in range(n // 2):
        for i in range(ne):
            if t == 0:
                local.wait() if i == 0 else first[i - 1].wait_recv()
            for d in range(2):
                if t:
                    hops[i, d, t - 1].wait_recv()
                if t == n // 2 - 1 and i % 2 != d:
                    continue
                seq_at = ring_device(lax.rem(pos + n + t * (ways[1 - d]), n), n)
                part = piece(seq_at, lax.rem(place + ne - i, ne))
                at = (i * 2 + d) * (n // 2) + t
                hops[i, d, t] = push(part, part, s_send.at[at], s_recv.at[at], nexts[d])
    for i in range(ne):
        hops[i, i % 2, n // 2 - 1].wait_recv()
    for copy in first + list(hops.values()):
        copy.wait_send()


def share_rows(rows, n, ne):
    cap, width = rows.shape[0] // ne, rows.shape[1]
    anywhere = pl.BlockSpec(memory_space=pl.ANY)
    return pl.pallas_call(
        functools.partial(rows_kernel, n, ne, cap, width),
        out_shape=jax.ShapeDtypeStruct((n * cap, ne * width), rows.dtype),
        in_specs=[anywhere],
        out_specs=anywhere,
        scratch_shapes=[pltpu.SemaphoreType.DMA((ne,))] * 2
        + [pltpu.SemaphoreType.DMA((ne * n,))] * 2
        + [pltpu.SemaphoreType.DMA(())],
        compiler_params=pltpu.CompilerParams(collective_id=2, has_side_effects=True),
    )(rows)


def sums_kernel(
    nz, ne, cap, p_ref, g_ref, o_ref, x_buf, s_buf, z_buf, total, w_buf,
    x_send, x_recv, z_send, z_recv, e_send, e_recv, own,
):
    me = lax.axis_index("seq")
    z, x, along, partner = lines(me, nz)
    place = lax.axis_index("exp")
    others = [{"exp": lax.rem(place + i, ne)} for i in range(1, ne)]
    greet(along + [partner] + others)

    def rows_of(k, side):
        return cut((lax.rem(z + k, nz) * 2 + side) * cap, cap)

    order = list(range(1, nz)) + [0]
    pairs = {}
    for k in order:
        pairs[k] = push(p_ref.at[rows_of(k, 1 - x), :], x_buf.at[k], x_send.at[k], x_recv.at[k], partner)
    sent = []
    for k in order:
        pairs[k].wait_recv()
        both = p_ref[rows_of(k, x), :].astype(jnp.float32) + x_buf[k].astype(jnp.float32)
        if k:
            s_buf[k] = both.astype(jnp.bfloat16)
            sent.append(push(s_buf.at[k], z_buf.at[k], z_send.at[k], z_recv.at[k], along[k - 1]))
        else:
            total[...] = both
    for k in range(1, nz):
        sent[k - 1].wait_recv()
        total[...] += z_buf[k].astype(jnp.float32)
    w_buf[...] = (g_ref[...] * total[...]).astype(jnp.bfloat16)
    width = w_buf.shape[1] // ne
    mine = o_ref.at[cut(place * cap, cap), :]
    local = pltpu.make_async_copy(w_buf.at[:, cut(place * width, width)], mine, own)
    local.start()
    spread = []
    for i in range(1, ne):
        src = w_buf.at[:, cut(lax.rem(place + i, ne) * width, width)]
        spread.append(push(src, mine, e_send.at[i], e_recv.at[i], others[i - 1]))
    local.wait()
    for copy in spread:
        copy.wait_recv()
    for copy in list(pairs.values()) + sent + spread:
        copy.wait_send()


def sum_rows(partial, gate, n, ne):
    cap, width = partial.shape[0] // n, partial.shape[1]
    nz = n // 2
    slots = pltpu.VMEM((nz, cap, width), jnp.bfloat16)
    return pl.pallas_call(
        functools.partial(sums_kernel, nz, ne, cap),
        out_shape=jax.ShapeDtypeStruct((ne * cap, width // ne), jnp.bfloat16),
        in_specs=[pl.BlockSpec(memory_space=pltpu.VMEM)] * 2,
        out_specs=pl.BlockSpec(memory_space=pl.ANY),
        scratch_shapes=[slots, slots, slots]
        + [pltpu.VMEM((cap, width), jnp.float32), pltpu.VMEM((cap, width), jnp.bfloat16)]
        + [pltpu.SemaphoreType.DMA((nz,))] * 4
        + [pltpu.SemaphoreType.DMA((ne,))] * 2
        + [pltpu.SemaphoreType.DMA(())],
        compiler_params=pltpu.CompilerParams(collective_id=3, has_side_effects=True),
    )(partial, gate)


def flash_kernel(block, border_ref, q_ref, k_ref, v_ref, o_ref):
    at = pl.program_id(1)
    border = border_ref[0]
    q_start = at * block
    rows = q_start + lax.broadcasted_iota(jnp.int32, (block, 1), 0)
    low = jnp.where(rows >= border, border, 0)
    steps = lax.broadcasted_iota(jnp.int32, (block, block), 1)
    q = q_ref[...]
    scale = math.log2(math.e) / math.sqrt(HD)

    def scored(j):
        start = pl.multiple_of(j * block, block)
        s = lax.dot_general(
            q, k_ref[pl.ds(start, block), :], (((1,), (1,)), ((), ())), preferred_element_type=jnp.float32
        )
        return s * scale, start

    def mix(p, start):
        return jnp.dot(
            p.astype(jnp.bfloat16), v_ref[pl.ds(start, block), :], preferred_element_type=jnp.float32
        )

    s, start = scored(at)
    s = jnp.where((steps >= low - start) & (steps <= rows - start), s, -jnp.inf)
    top = jnp.max(s, axis=1, keepdims=True)
    p = jnp.exp2(s - top)
    state = (top, jnp.sum(p, axis=1, keepdims=True), mix(p, start))

    def step(j, state):
        top, total, out = state
        s, start = scored(j)
        s = jnp.where(steps >= low - start, s, -jnp.inf)
        new_top = jnp.maximum(top, jnp.max(s, axis=1, keepdims=True))
        factor = jnp.exp2(top - new_top)
        p = jnp.exp2(s - new_top)
        return (
            new_top,
            total * factor + jnp.sum(p, axis=1, keepdims=True),
            out * factor + mix(p, start),
        )

    begin = jnp.where(q_start >= border, border // block, 0)
    top, total, out = lax.fori_loop(begin, at, step, state)
    o_ref[...] = (out / total).astype(o_ref.dtype)


def flash(queries, keys, values, border):
    rows, width = queries.shape
    block = block_rows
    return pl.pallas_call(
        functools.partial(flash_kernel, block),
        out_shape=jax.ShapeDtypeStruct((rows, width), queries.dtype),
        grid_spec=pltpu.PrefetchScalarGridSpec(
            num_scalar_prefetch=1,
            grid=(width // HD, rows // block),
            in_specs=[
                pl.BlockSpec((block, HD), lambda h, i, b: (i, h)),
                pl.BlockSpec((rows, HD), lambda h, i, b: (0, h)),
                pl.BlockSpec((rows, HD), lambda h, i, b: (0, h)),
            ],
            out_specs=pl.BlockSpec((block, HD), lambda h, i, b: (i, h)),
        ),
    )(border, queries, keys, values)


def attend_by_head(queries, keys, values, documents, n, n_exp):
    border = jnp.sum((documents == 0).astype(jnp.int32)).reshape(1)
    q_all, k_all, v_all = heads_out(queries, keys, values, n)
    return heads_back(flash(q_all, k_all, v_all, border), n, n_exp)


def chain_kernel(
    nz, ne, group, causal_span, border_ref, q_ref, k_ref, v_ref, o_ref,
    q0, q1, q2, kb, vb, o0, o1, c0, c1, s2, s1, p2, p1, ls2, ls1, lp2, lp1, fin, back,
    load, x_send, x_recv, d0_send, d0_recv, d1_send, d1_recv, u2_send, u2_recv, g2_send, g2_recv,
    u1_send, u1_recv, g1_send, g1_recv, b_send, b_recv, y_send, y_recv, m_send, m_recv,
    r_send, r_recv, own,
):
    me = lax.axis_index("seq")
    place = lax.axis_index("exp")
    z, x = me // 2, lax.rem(me, 2)
    y, core = place // 2, lax.rem(place, 2)
    ny = ne // 2
    tokens = q_ref.shape[0]
    steps = 2 * group
    up = {"seq": lax.rem(z + 1, nz) * 2 + x}
    down = {"seq": lax.rem(z + nz - 1, nz) * 2 + x}
    partner = {"seq": z * 2 + 1 - x}
    sibling = {"exp": y * 2 + 1 - core}
    far_place = lax.rem(y + 1, ny) * 2 + core
    far = {"exp": far_place}
    has1, has2, low1 = z + 1 < nz, z + 2 < nz, z >= 1
    border = border_ref[0]
    scale = math.log2(math.e) / math.sqrt(HD)
    greet([up, down, partner, sibling, far])

    def remote(src, dst, send, recv, peer):
        return pltpu.make_async_remote_copy(
            src_ref=src, dst_ref=dst, send_sem=send, recv_sem=recv, device_id=peer, device_id_type=MESH
        )

    def half(ref, h, side):
        return ref.at[h, cut(side * tokens, tokens), :]

    def columns(ref, h, side):
        return ref.at[:, cut((side * group + h) * HD, HD)]

    def loads(h):
        return (
            pltpu.make_async_copy(columns(q_ref, h, x), q0.at[2 * h], load.at[3 * h]),
            pltpu.make_async_copy(columns(k_ref, h, x), half(kb, h, x), load.at[3 * h + 1]),
            pltpu.make_async_copy(columns(v_ref, h, x), half(vb, h, x), load.at[3 * h + 2]),
        )

    def swaps(h):
        side = 1 - x
        return tuple(
            remote(columns(src, h, side), dst, x_send.at[3 * h + t], x_recv.at[3 * h + t], partner)
            for t, (src, dst) in enumerate(
                ((q_ref, q0.at[2 * h + 1]), (k_ref, half(kb, h, x)), (v_ref, half(vb, h, x)))
            )
        )

    def q_down(t):
        return remote(q0.at[t], q1.at[t], d0_send.at[t], d0_recv.at[t], down)

    def q_further(t):
        return remote(q1.at[t], q2.at[t], d1_send.at[t], d1_recv.at[t], down)

    def part2_up(t):
        return (
            remote(s2.at[t], p2.at[t], u2_send.at[t], u2_recv.at[t], up),
            remote(ls2.at[t], lp2.at[t], g2_send.at[t], g2_recv.at[t], up),
        )

    def part1_up(t):
        return (
            remote(s1.at[t], p1.at[t], u1_send.at[t], u1_recv.at[t], up),
            remote(ls1.at[t], lp1.at[t], g1_send.at[t], g1_recv.at[t], up),
        )

    def give_back(t):
        return remote(back.at[t // 2], fin.at[t], b_send.at[t // 2], b_recv.at[t // 2], partner)

    def spot(at, t):
        j = lax.rem(t, 2)
        side = x + j * (1 - 2 * x)
        return o_ref.at[:, cut(((at * 2 + side) * group + t // 2) * HD, HD)]

    def keep(t):
        return pltpu.make_async_copy(fin.at[t], spot(place, t), own.at[t])

    def to_far(t):
        return remote(fin.at[t], spot(place, t), y_send.at[t], y_recv.at[t], far)

    def to_sibling(t):
        return remote(fin.at[t], spot(place, t), m_send.at[t], m_recv.at[t], sibling)

    def relay(t):
        return remote(spot(far_place, t), spot(far_place, t), r_send.at[t], r_recv.at[t], sibling)

    tile = HD
    tiles = tokens // tile
    span = kb.shape[1]
    key_base = z * span
    diagonal = lax.broadcasted_iota(jnp.int32, (tile, tile), 0) == lax.broadcasted_iota(
        jnp.int32, (tile, tile), 1
    )

    def attend(q_of, h, level, t, put):
        j = lax.rem(t, 2)
        side = x + j * (1 - 2 * x)
        base = ((z + level) * 2 + side) * tokens - key_base
        edge = border - key_base
        keys, vals = kb[h], vb[h]
        at = lax.broadcasted_iota(jnp.int32, (tile, span), 1)
        for r in range(tiles):
            rows = base + r * tile + lax.broadcasted_iota(jnp.int32, (tile, 1), 0)
            low = jnp.where(rows >= edge, edge, -key_base)
            s = lax.dot_general(
                q_of[r * tile : (r + 1) * tile, :], keys, (((1,), (1,)), ((), ())),
                preferred_element_type=jnp.float32,
            )
            seen = at >= low
            if level == 0:
                seen = seen & (at <= rows)
            s = jnp.where(seen, s, -1e30)
            top = jnp.max(s, axis=1, keepdims=True) * scale
            p = jnp.exp2(s * scale - top)
            total = jnp.sum(p, axis=1, keepdims=True)
            out = jnp.dot(p.astype(jnp.bfloat16), vals, preferred_element_type=jnp.float32)
            put(r, out / total, top + jnp.log2(total))

    def flat(level):
        return jnp.sum(jnp.where(diagonal, level, 0.0), axis=0, keepdims=True)

    def upright(ref, r):
        return jnp.sum(jnp.where(diagonal, ref[r : r + 1, :], 0.0), axis=1, keepdims=True)

    def joined(out, level, p_of, l_of, r):
        other = upright(l_of, r)
        top = jnp.maximum(level, other)
        mine, theirs = jnp.exp2(level - top), jnp.exp2(other - top)
        both = mine + theirs
        out = (out * mine + p_of[r * tile : (r + 1) * tile, :].astype(jnp.float32) * theirs) / both
        return out, top + jnp.log2(both)

    for h in range(group):
        for copy in swaps(h):
            copy.start()
        for copy in loads(h):
            copy.start()

    def send_own(t):
        @pl.when(lax.rem(t, 2) == 0)
        def _():
            loads(t // 2)[0].wait()

        @pl.when(lax.rem(t, 2) == 1)
        def _():
            swaps(t // 2)[0].wait_recv()

        @pl.when(low1)
        def _():
            q_down(t).start()

    def forward(t):
        @pl.when(has1)
        def _():
            q_down(t).wait_recv()

            @pl.when(low1)
            def _():
                q_further(t).start()

    def spread(t):
        keep(t).start()
        to_far(t).start()
        to_sibling(t).start()

    send_own(jnp.int32(0))
    send_own(jnp.int32(1))
    forward(jnp.int32(0))

    def step(i, carry):
        live = i < steps

        @pl.when(i + 2 < steps)
        def _():
            send_own(i + 2)

        @pl.when(i + 1 < steps)
        def _():
            forward(i + 1)

        @pl.when(live & (lax.rem(i, 2) == 0))
        def _():
            for copy in loads(i // 2)[1:]:
                copy.wait()
            for copy in swaps(i // 2)[1:]:
                copy.wait_recv()

        @pl.when(live & has2)
        def _():
            q_further(i).wait_recv()

            def put(r, out, level):
                s2[i, r * tile : (r + 1) * tile, :] = out.astype(jnp.bfloat16)
                ls2[i, r : r + 1, :] = flat(level)

            attend(q2.at[i], i // 2, 2, i, put)
            for copy in part2_up(i):
                copy.start()

        t1 = i - 1

        @pl.when((t1 >= 0) & (t1 < steps) & has1)
        def _():
            def put(r, out, level):
                s1[t1, r * tile : (r + 1) * tile, :] = out.astype(jnp.bfloat16)
                ls1[t1, r : r + 1, :] = flat(level)

            @pl.when(low1)
            def _():
                for copy in part2_up(t1):
                    copy.wait_recv()
                for r in range(tiles):
                    put(r, *joined(o1[t1, r * tile : (r + 1) * tile, :], c1[t1, r * tile : (r + 1) * tile, :], p2.at[t1], lp2.at[t1], r))

            @pl.when(jnp.logical_not(low1))
            def _():
                for r in range(tiles):
                    put(r, o1[t1, r * tile : (r + 1) * tile, :], c1[t1, r * tile : (r + 1) * tile, :])

            for copy in part1_up(t1):
                copy.start()

        @pl.when(live & has1)
        def _():
            def put(r, out, level):
                o1[i, r * tile : (r + 1) * tile, :] = out
                c1[i, r * tile : (r + 1) * tile, :] = level

            attend(q1.at[i], i // 2, 1, i, put)

        t0 = i - 2

        @pl.when((t0 >= 0) & (t0 < steps))
        def _():
            def finish(put):
                @pl.when(low1)
                def _():
                    for copy in part1_up(t0):
                        copy.wait_recv()
                    for r in range(tiles):
                        out, level = joined(o0[t0, r * tile : (r + 1) * tile, :], c0[t0, r * tile : (r + 1) * tile, :], p1.at[t0], lp1.at[t0], r)
                        put(r, out)

                @pl.when(jnp.logical_not(low1))
                def _():
                    for r in range(tiles):
                        put(r, o0[t0, r * tile : (r + 1) * tile, :])

            @pl.when(lax.rem(t0, 2) == 0)
            def _():
                def put(r, out):
                    fin[t0, r * tile : (r + 1) * tile, :] = out.astype(jnp.bfloat16)

                finish(put)
                spread(t0)

            @pl.when(lax.rem(t0, 2) == 1)
            def _():
                def put(r, out):
                    back[t0 // 2, r * tile : (r + 1) * tile, :] = out.astype(jnp.bfloat16)

                finish(put)
                give_back(t0).start()

        @pl.when(live)
        def _():
            def put(r, out, level):
                o0[i, r * tile : (r + 1) * tile, :] = out
                c0[i, r * tile : (r + 1) * tile, :] = level

            attend(q0.at[i], i // 2, 0, i, put)

        t4 = i - 3

        @pl.when((t4 >= 0) & (t4 < steps) & (lax.rem(t4, 2) == 1))
        def _():
            give_back(t4).wait_recv()
            spread(t4)

        t5 = i - 5

        @pl.when((t5 >= 0) & (t5 < steps))
        def _():
            to_far(t5).wait_recv()
            relay(t5).start()

        return carry

    lax.fori_loop(0, steps + 5, step, 0)

    def settle(t, carry):
        to_sibling(t).wait_recv()
        relay(t).wait_recv()
        keep(t).wait()
        to_far(t).wait_send()
        to_sibling(t).wait_send()
        relay(t).wait_send()

        @pl.when(low1)
        def _():
            q_down(t).wait_send()

            @pl.when(has1)
            def _():
                q_further(t).wait_send()

        @pl.when(has1)
        def _():
            for copy in part1_up(t):
                copy.wait_send()

        @pl.when(has2)
        def _():
            for copy in part2_up(t):
                copy.wait_send()

        @pl.when(lax.rem(t, 2) == 1)
        def _():
            give_back(t).wait_send()
            for copy in swaps(t // 2):
                copy.wait_send()

        return carry

    lax.fori_loop(0, steps, settle, 0)


def attend_by_chain(queries, keys, values, documents, n, n_exp):
    tokens, width = queries.shape
    group = width // HD // 2
    steps = 2 * group
    nz = n // 2
    border = jnp.sum((documents == 0).astype(jnp.int32)).reshape(1)
    anywhere = pl.BlockSpec(memory_space=pl.ANY)
    bf, f32 = jnp.bfloat16, jnp.float32
    chunks = pltpu.VMEM((steps, tokens, HD), bf)
    side = pltpu.VMEM((group, 2 * tokens, HD), bf)
    wide = pltpu.VMEM((steps, tokens, HD), f32)
    thin = pltpu.VMEM((steps, tokens, 1), f32)
    flats = pltpu.VMEM((steps, max(8, tokens // HD), HD), f32)
    sems = lambda count: pltpu.SemaphoreType.DMA((count,))
    return pl.pallas_call(
        functools.partial(chain_kernel, nz, n_exp, group, None),
        out_shape=jax.ShapeDtypeStruct((tokens, n_exp * width), queries.dtype),
        in_specs=[pl.BlockSpec(memory_space=pltpu.SMEM)] + [anywhere] * 3,
        out_specs=anywhere,
        scratch_shapes=[chunks] * 3 + [side] * 2 + [wide] * 2 + [thin] * 2 + [chunks] * 4 + [flats] * 4
        + [chunks, pltpu.VMEM((group, tokens, HD), bf)]
        + [sems(3 * group)] * 3 + [sems(steps)] * 12 + [sems(group)] * 2 + [sems(steps)] * 6 + [sems(steps)],
        compiler_params=pltpu.CompilerParams(
            collective_id=0, has_side_effects=True, vmem_limit_bytes=48 * 1024 * 1024
        ),
    )(border, queries, keys, values)


def attend_by_token(queries, keys, values, documents):
    tokens = queries.shape[0]
    heads_here = queries.shape[1] // HD
    seq_pos = lax.axis_index("seq")
    start_row = seq_pos * tokens
    query_pos = start_row + jnp.arange(tokens, dtype=jnp.int32)
    query_doc = lax.dynamic_slice_in_dim(documents, start_row, tokens, 0)
    query_heads = queries.reshape(tokens, heads_here, HD)
    score_scale = 1.0 / math.sqrt(HD)

    def attend(state, key_rows, value_rows, key_start):
        row_count = key_rows.shape[0]
        key_pos = key_start + jnp.arange(row_count, dtype=jnp.int32)
        key_doc = lax.dynamic_slice_in_dim(documents, key_start, row_count, 0)
        scores = (
            jnp.einsum(
                "qhd,khd->qhk",
                query_heads,
                key_rows.reshape(row_count, heads_here, HD),
                preferred_element_type=jnp.float32,
            )
            * score_scale
        )
        allowed = (key_pos[None, :] <= query_pos[:, None]) & (
            key_doc[None, :] == query_doc[:, None]
        )
        scores = jnp.where(allowed[:, None, :], scores, -jnp.inf)
        running_max, running_sum, running_out = state
        new_max = jnp.maximum(running_max, jnp.max(scores, axis=2))
        factor = jnp.exp(running_max - new_max)
        weights = jnp.exp(scores - new_max[:, :, None])
        running_sum = running_sum * factor + jnp.sum(weights, axis=2)
        running_out = running_out * factor[:, :, None] + jnp.einsum(
            "qhk,khd->qhd",
            weights.astype(jnp.bfloat16),
            value_rows.reshape(row_count, heads_here, HD),
            preferred_element_type=jnp.float32,
        )
        return (new_max, running_sum, running_out)

    def visit_block(state, key_rows, value_rows, key_start):
        row_count = key_rows.shape[0]
        last_doc = lax.dynamic_index_in_dim(documents, key_start + row_count - 1, 0, keepdims=False)
        beyond = (key_start > query_pos[tokens - 1]) | (last_doc < query_doc[0])
        return lax.cond(
            beyond,
            lambda inner_state: inner_state,
            lambda inner_state: attend(inner_state, key_rows, value_rows, key_start),
            state,
        )

    initial = (
        jnp.full((tokens, heads_here), -1e30, jnp.float32),
        jnp.zeros((tokens, heads_here), jnp.float32),
        jnp.zeros((tokens, heads_here, HD), jnp.float32),
    )
    state = initial
    key_piece = lax.all_gather(keys, "seq", axis=0, tiled=True)
    value_piece = lax.all_gather(values, "seq", axis=0, tiled=True)
    row_count = key_piece.shape[0]
    blocks = row_count // block_rows
    key_stack = key_piece.reshape(blocks, block_rows, key_piece.shape[1])
    value_stack = value_piece.reshape(blocks, block_rows, value_piece.shape[1])

    def scan_step(inner_state, block_item):
        block_index, key_rows, value_rows = block_item
        return (visit_block(inner_state, key_rows, value_rows, block_index * block_rows), None)

    state, unused = lax.scan(
        scan_step, state, (jnp.arange(blocks, dtype=jnp.int32), key_stack, value_stack)
    )
    running_max, running_sum, running_out = state
    attended = (
        (running_out / running_sum[:, :, None])
        .reshape(tokens, heads_here * HD)
        .astype(jnp.bfloat16)
    )
    return lax.all_gather(attended, "exp", axis=1, tiled=True)


def shards(
    residual,
    queries,
    keys,
    values,
    documents,
    out_proj,
    modality,
    norm_gain,
    picks,
    router,
    w_gate,
    w_up,
    w_down,
):
    tokens = queries.shape[0]
    seq_pos = lax.axis_index("seq")
    start_row = seq_pos * tokens
    n_seq, n_exp = lax.axis_size("seq"), lax.axis_size("exp")
    if (queries.shape[1] // HD) % n_seq == 0 and n_exp % 2 == 0:
        attended = attend_by_chain(queries, keys, values, documents, n_seq, n_exp)
    else:
        attended = attend_by_token(queries, keys, values, documents)
    mixed = jnp.dot(
        attended,
        out_proj,
        preferred_element_type=jnp.float32,
    )
    hidden_state = (residual.astype(jnp.float32) + mixed).astype(jnp.bfloat16)
    hidden_wide = hidden_state.astype(jnp.float32)
    square_total = lax.psum(jnp.sum(hidden_wide * hidden_wide, axis=1), "exp")
    inverse = lax.rsqrt(square_total / D + 1e-05)
    gain_rows = jnp.where(modality[:, None] == 0, norm_gain[0][None, :], norm_gain[1][None, :])
    normed = (hidden_wide * inverse[:, None] * gain_rows).astype(jnp.bfloat16)
    capacity = tokens // 32
    inside = (picks >= start_row) & (picks < start_row + tokens)
    slot_index = jnp.cumsum(inside.astype(jnp.int32), axis=1) - 1
    matched = inside[:, None, :] & (
        slot_index[:, None, :] == jnp.arange(capacity, dtype=jnp.int32)[None, :, None]
    )
    local_index = jnp.sum(jnp.where(matched, picks[:, None, :] - start_row, 0), axis=2)
    filled = jnp.any(matched, axis=2)
    rows_out = jnp.take(normed, local_index.reshape(-1), axis=0)
    rows_out = jnp.where(filled.reshape(-1, 1), rows_out, jnp.zeros_like(rows_out))
    piece = share_rows(rows_out, n_seq, n_exp)
    expert_rows = lax.dynamic_slice_in_dim(piece, seq_pos * capacity, capacity, 0)
    logits = jnp.dot(expert_rows, router, preferred_element_type=jnp.float32)[:, 0]
    gate_part = jnp.dot(piece, w_gate[0], preferred_element_type=jnp.float32)
    up_part = jnp.dot(piece, w_up[0], preferred_element_type=jnp.float32)
    inner_act = (jax.nn.silu(gate_part) * up_part).astype(jnp.bfloat16)
    partial = jnp.dot(inner_act, w_down[0], preferred_element_type=jnp.float32).astype(jnp.bfloat16)
    returned = sum_rows(partial, jax.nn.sigmoid(logits)[:, None], n_seq, n_exp)
    placing = (
        (jnp.arange(tokens, dtype=jnp.int32)[:, None] == local_index.reshape(1, -1))
        & filled.reshape(1, -1)
    ).astype(jnp.bfloat16)
    expert_add = jnp.dot(placing, returned, preferred_element_type=jnp.float32)
    return (hidden_wide + expert_add).astype(jnp.bfloat16)


def solution(mesh):
    return jax.shard_map(
        shards,
        mesh=mesh,
        in_specs=(
            P("seq", "exp"),
            P("seq", "exp"),
            P("seq", "exp"),
            P("seq", "exp"),
            P(),
            P(None, "exp"),
            P("seq"),
            P(None, "exp"),
            P(),
            P(None, "exp"),
            P("exp", None, "seq"),
            P("exp", None, "seq"),
            P("exp", "seq", None),
        ),
        out_specs=P("seq", "exp"),
        check_vma=False,
    )
```

```python
import functools
import math

import jax
import jax.numpy as jnp
from jax import lax
from jax.experimental import pallas as pl
from jax.experimental.pallas import tpu as pltpu
from jax.sharding import PartitionSpec as P

D = 8192
HD = 128


block_rows = 512


MESH = pl.DeviceIdType.MESH


def greet(peers):
    barrier = pltpu.get_barrier_semaphore()
    for peer in peers:
        pl.semaphore_signal(barrier, inc=1, device_id=peer, device_id_type=MESH)
    pl.semaphore_wait(barrier, len(peers))


def cut(start, size):
    return pl.ds(pl.multiple_of(start, size), size)


def heads_out_kernel(n, width, q_ref, k_ref, v_ref, qo, ko, vo, send, recv, own):
    me = lax.axis_index("seq")
    tokens = q_ref.shape[0]
    greet([{"seq": lax.rem(me + i, n)} for i in range(1, n)])
    pairs = ((k_ref, ko), (v_ref, vo), (q_ref, qo))
    copies = []
    for i in range(1, n):
        to = lax.rem(me + i, n)
        for t, (src, dst) in enumerate(pairs):
            copies.append(
                pltpu.make_async_remote_copy(
                    src_ref=src.at[:, cut(to * width, width)],
                    dst_ref=dst.at[cut(me * tokens, tokens), :],
                    send_sem=send.at[t * n + i],
                    recv_sem=recv.at[t * n + i],
                    device_id={"seq": to},
                    device_id_type=MESH,
                )
            )
            copies[-1].start()
    for t, (src, dst) in enumerate(pairs):
        copies.append(
            pltpu.make_async_copy(
                src.at[:, cut(me * width, width)], dst.at[cut(me * tokens, tokens), :], own.at[t]
            )
        )
        copies[-1].start()
    for copy in copies:
        copy.wait()


def heads_out(queries, keys, values, n):
    tokens, columns = queries.shape
    width = columns // n
    whole = jax.ShapeDtypeStruct((n * tokens, width), queries.dtype)
    anywhere = pl.BlockSpec(memory_space=pl.ANY)
    return pl.pallas_call(
        functools.partial(heads_out_kernel, n, width),
        out_shape=(whole, whole, whole),
        in_specs=[anywhere] * 3,
        out_specs=(anywhere,) * 3,
        scratch_shapes=[
            pltpu.SemaphoreType.DMA((3 * n,)),
            pltpu.SemaphoreType.DMA((3 * n,)),
            pltpu.SemaphoreType.DMA((3,)),
        ],
        compiler_params=pltpu.CompilerParams(collective_id=0, has_side_effects=True),
    )(queries, keys, values)


def heads_back_kernel(n, ny, width, a_ref, o_ref, s_send, s_recv, y_send, y_recv, c_send, c_recv, own):
    me = lax.axis_index("seq")
    place = lax.axis_index("exp")
    y, core = place // 2, lax.rem(place, 2)
    sibling = {"exp": y * 2 + 1 - core}
    across = [{"exp": lax.rem(y + k, ny) * 2 + core} for k in range(1, ny)]
    tokens = o_ref.shape[0]
    span = n * width
    greet([{"seq": lax.rem(me + i, n)} for i in range(1, n)] + across + [sibling])

    def piece(exp_at, seq_at):
        return o_ref.at[:, cut(exp_at * span + seq_at * width, width)]

    local = pltpu.make_async_copy(a_ref.at[cut(me * tokens, tokens), :], piece(place, me), own)
    local.start()
    first = []
    for i in range(1, n):
        to = lax.rem(me + i, n)
        first.append(
            push(
                a_ref.at[cut(to * tokens, tokens), :],
                piece(place, me),
                s_send.at[i],
                s_recv.at[i],
                {"seq": to},
            )
        )
    second = []
    third = []
    for i in range(n):
        if i == 0:
            local.wait()
        else:
            first[i - 1].wait_recv()
        part = piece(place, lax.rem(me + n - i, n))
        for k in range(1, ny):
            at = i * ny + k
            second.append(push(part, part, y_send.at[at], y_recv.at[at], across[k - 1]))
        third.append(push(part, part, c_send.at[i * ny], c_recv.at[i * ny], sibling))
    for i in range(n):
        for k in range(1, ny):
            second[i * (ny - 1) + k - 1].wait_recv()
            at = i * ny + k
            part = piece(lax.rem(y + ny - k, ny) * 2 + core, lax.rem(me + n - i, n))
            third.append(push(part, part, c_send.at[at], c_recv.at[at], sibling))
    for copy in third:
        copy.wait_recv()
    for copy in first + second + third:
        copy.wait_send()


def heads_back(attended, n, n_exp):
    rows, width = attended.shape
    ny = n_exp // 2
    anywhere = pl.BlockSpec(memory_space=pl.ANY)
    return pl.pallas_call(
        functools.partial(heads_back_kernel, n, ny, width),
        out_shape=jax.ShapeDtypeStruct((rows // n, n_exp * n * width), attended.dtype),
        in_specs=[anywhere],
        out_specs=anywhere,
        scratch_shapes=[
            pltpu.SemaphoreType.DMA((n,)),
            pltpu.SemaphoreType.DMA((n,)),
            pltpu.SemaphoreType.DMA((n * ny,)),
            pltpu.SemaphoreType.DMA((n * ny,)),
            pltpu.SemaphoreType.DMA((n * ny,)),
            pltpu.SemaphoreType.DMA((n * ny,)),
            pltpu.SemaphoreType.DMA(()),
        ],
        compiler_params=pltpu.CompilerParams(collective_id=1, has_side_effects=True),
    )(attended)


def push(src, dst, send, recv, peer):
    copy = pltpu.make_async_remote_copy(
        src_ref=src, dst_ref=dst, send_sem=send, recv_sem=recv, device_id=peer, device_id_type=MESH
    )
    copy.start()
    return copy


def lines(me, nz):
    z, x = me // 2, lax.rem(me, 2)
    along = [{"seq": lax.rem(z + k, nz) * 2 + x} for k in range(1, nz)]
    return z, x, along, {"seq": z * 2 + 1 - x}


def ring_device(pos, n):
    half = pos // (n // 2)
    return (1 - half) * pos * 2 + half * ((n - 1 - pos) * 2 + 1)


def rows_kernel(n, ne, cap, width, r_ref, o_ref, e_send, e_recv, s_send, s_recv, own):
    me = lax.axis_index("seq")
    place = lax.axis_index("exp")
    z, x = me // 2, lax.rem(me, 2)
    pos = (1 - x) * z + x * (n - 1 - z)
    ways = (1, n - 1)
    nexts = [{"seq": ring_device(lax.rem(pos + way, n), n)} for way in ways]
    others = [{"exp": lax.rem(place + i, ne)} for i in range(1, ne)]
    greet(others + nexts)

    def piece(seq_at, exp_at):
        return o_ref.at[cut(seq_at * cap, cap), cut(exp_at * width, width)]

    local = pltpu.make_async_copy(r_ref.at[cut(place * cap, cap), :], piece(me, place), own)
    local.start()
    first = []
    for i in range(1, ne):
        src = r_ref.at[cut(lax.rem(place + i, ne) * cap, cap), :]
        first.append(push(src, piece(me, place), e_send.at[i], e_recv.at[i], others[i - 1]))
    hops = {}
    for t in range(n // 2):
        for i in range(ne):
            if t == 0:
                local.wait() if i == 0 else first[i - 1].wait_recv()
            for d in range(2):
                if t:
                    hops[i, d, t - 1].wait_recv()
                if t == n // 2 - 1 and i % 2 != d:
                    continue
                seq_at = ring_device(lax.rem(pos + n + t * (ways[1 - d]), n), n)
                part = piece(seq_at, lax.rem(place + ne - i, ne))
                at = (i * 2 + d) * (n // 2) + t
                hops[i, d, t] = push(part, part, s_send.at[at], s_recv.at[at], nexts[d])
    for i in range(ne):
        hops[i, i % 2, n // 2 - 1].wait_recv()
    for copy in first + list(hops.values()):
        copy.wait_send()


def share_rows(rows, n, ne):
    cap, width = rows.shape[0] // ne, rows.shape[1]
    anywhere = pl.BlockSpec(memory_space=pl.ANY)
    return pl.pallas_call(
        functools.partial(rows_kernel, n, ne, cap, width),
        out_shape=jax.ShapeDtypeStruct((n * cap, ne * width), rows.dtype),
        in_specs=[anywhere],
        out_specs=anywhere,
        scratch_shapes=[pltpu.SemaphoreType.DMA((ne,))] * 2
        + [pltpu.SemaphoreType.DMA((ne * n,))] * 2
        + [pltpu.SemaphoreType.DMA(())],
        compiler_params=pltpu.CompilerParams(collective_id=2, has_side_effects=True),
    )(rows)


def sums_kernel(
    nz, ne, cap, p_ref, g_ref, o_ref, x_buf, s_buf, z_buf, total, w_buf,
    x_send, x_recv, z_send, z_recv, e_send, e_recv, own,
):
    me = lax.axis_index("seq")
    z, x, along, partner = lines(me, nz)
    place = lax.axis_index("exp")
    others = [{"exp": lax.rem(place + i, ne)} for i in range(1, ne)]
    greet(along + [partner] + others)

    def rows_of(k, side):
        return cut((lax.rem(z + k, nz) * 2 + side) * cap, cap)

    order = list(range(1, nz)) + [0]
    pairs = {}
    for k in order:
        pairs[k] = push(p_ref.at[rows_of(k, 1 - x), :], x_buf.at[k], x_send.at[k], x_recv.at[k], partner)
    sent = []
    for k in order:
        pairs[k].wait_recv()
        both = p_ref[rows_of(k, x), :].astype(jnp.float32) + x_buf[k].astype(jnp.float32)
        if k:
            s_buf[k] = both.astype(jnp.bfloat16)
            sent.append(push(s_buf.at[k], z_buf.at[k], z_send.at[k], z_recv.at[k], along[k - 1]))
        else:
            total[...] = both
    for k in range(1, nz):
        sent[k - 1].wait_recv()
        total[...] += z_buf[k].astype(jnp.float32)
    w_buf[...] = (g_ref[...] * total[...]).astype(jnp.bfloat16)
    width = w_buf.shape[1] // ne
    mine = o_ref.at[cut(place * cap, cap), :]
    local = pltpu.make_async_copy(w_buf.at[:, cut(place * width, width)], mine, own)
    local.start()
    spread = []
    for i in range(1, ne):
        src = w_buf.at[:, cut(lax.rem(place + i, ne) * width, width)]
        spread.append(push(src, mine, e_send.at[i], e_recv.at[i], others[i - 1]))
    local.wait()
    for copy in spread:
        copy.wait_recv()
    for copy in list(pairs.values()) + sent + spread:
        copy.wait_send()


def sum_rows(partial, gate, n, ne):
    cap, width = partial.shape[0] // n, partial.shape[1]
    nz = n // 2
    slots = pltpu.VMEM((nz, cap, width), jnp.bfloat16)
    return pl.pallas_call(
        functools.partial(sums_kernel, nz, ne, cap),
        out_shape=jax.ShapeDtypeStruct((ne * cap, width // ne), jnp.bfloat16),
        in_specs=[pl.BlockSpec(memory_space=pltpu.VMEM)] * 2,
        out_specs=pl.BlockSpec(memory_space=pl.ANY),
        scratch_shapes=[slots, slots, slots]
        + [pltpu.VMEM((cap, width), jnp.float32), pltpu.VMEM((cap, width), jnp.bfloat16)]
        + [pltpu.SemaphoreType.DMA((nz,))] * 4
        + [pltpu.SemaphoreType.DMA((ne,))] * 2
        + [pltpu.SemaphoreType.DMA(())],
        compiler_params=pltpu.CompilerParams(collective_id=3, has_side_effects=True),
    )(partial, gate)


def experts_kernel(
    n, ne, cap, hid_ref, pick_ref, pack_ref, unpack_ref, gain_ref, router_ref, wg_ref, wu_ref, wd_ref, o_ref,
    wg, wu, wd, r_buf, rows, gains, normed, mine, p_buf, x_buf, s_buf, z_buf, w_buf,
    w_sem, e_send, e_recv, n_send, n_recv, s_send, s_recv, x_send, x_recv, z_send, z_recv,
    t_send, t_recv, own,
):
    me = lax.axis_index("seq")
    place = lax.axis_index("exp")
    nz, z, x = n // 2, me // 2, lax.rem(me, 2)
    loads = [
        pltpu.make_async_copy(src, dst, w_sem.at[t])
        for t, (src, dst) in enumerate(((wg_ref, wg), (wu_ref, wu), (wd_ref, wd)))
    ]
    for copy in loads:
        copy.start()
    pos = (1 - x) * z + x * (n - 1 - z)
    ways = (1, n - 1)
    nexts = [{"seq": ring_device(lax.rem(pos + way, n), n)} for way in ways]
    partner = {"seq": z * 2 + 1 - x}
    along = [{"seq": lax.rem(z + k, nz) * 2 + x} for k in range(1, nz)]
    others = [{"exp": lax.rem(place + i, ne)} for i in range(1, ne)]
    flat_at = me * ne + place
    everyone = n * ne

    barrier = pltpu.get_barrier_semaphore()

    def hello(i, carry):
        at = lax.rem(flat_at + i, everyone)
        pl.semaphore_signal(
            barrier, inc=1, device_id={"seq": at // ne, "exp": lax.rem(at, ne)}, device_id_type=MESH
        )
        return carry

    lax.fori_loop(1, everyone, hello, 0)
    r_buf[...] = jnp.dot(pick_ref[...], hid_ref[...], preferred_element_type=jnp.float32).astype(jnp.bfloat16)
    width = r_buf.shape[1]
    pl.semaphore_wait(barrier, everyone - 1)

    def piece(seq_at, exp_at):
        return rows.at[cut(seq_at * cap, cap), cut(exp_at * width, width)]

    def kind(e):
        return (2 * e) // ne

    local = pltpu.make_async_copy(r_buf.at[cut(place * cap, cap), :], piece(me, place), own.at[0])
    local.start()
    own_gain = pltpu.make_async_copy(
        gain_ref.at[pl.ds(kind(place), 1), :], gains.at[:, cut(place * width, width)], own.at[1]
    )
    own_gain.start()
    first = []
    scales = []
    for i in range(1, ne):
        to = lax.rem(place + i, ne)
        first.append(
            push(r_buf.at[cut(to * cap, cap), :], piece(me, place), e_send.at[i], e_recv.at[i], others[i - 1])
        )
    hops = {}
    for t in range(n // 2):
        for i in range(ne):
            if t == 0:
                local.wait() if i == 0 else first[i - 1].wait_recv()
            for d in range(2):
                if t:
                    hops[i, d, t - 1].wait_recv()
                if t == n // 2 - 1 and i % 2 != d:
                    continue
                seq_at = ring_device(lax.rem(pos + n + t * (ways[1 - d]), n), n)
                part = piece(seq_at, lax.rem(place + ne - i, ne))
                at = (i * 2 + d) * (n // 2) + t
                hops[i, d, t] = push(part, part, s_send.at[at], s_recv.at[at], nexts[d])
        if t == 0:
            for i in range(1, ne):
                to = lax.rem(place + i, ne)
                scales.append(
                    push(
                        gain_ref.at[pl.ds(kind(to), 1), :], gains.at[:, cut(place * width, width)],
                        n_send.at[i], n_recv.at[i], others[i - 1],
                    )
                )
    own_gain.wait()
    for copy in scales:
        copy.wait_recv()
    for i in range(ne):
        hops[i, i % 2, n // 2 - 1].wait_recv()

    count = pack_ref.shape[0]
    depth = ne * width
    square = jnp.zeros((count, 1), jnp.float32)
    for e in range(ne):
        span = slice(e * width, (e + 1) * width)
        packed = jnp.dot(pack_ref[...], rows[:, span], preferred_element_type=jnp.float32)
        square += jnp.sum(packed * packed, axis=1, keepdims=True)
        normed[:, span] = packed.astype(jnp.bfloat16)
    inverse = lax.rsqrt(square / depth + 1e-05)
    logits = jnp.zeros((count, 1), jnp.float32)
    for e in range(ne):
        span = slice(e * width, (e + 1) * width)
        scaled = (normed[:, span].astype(jnp.float32) * inverse * gains[:, span]).astype(jnp.bfloat16)
        normed[:, span] = scaled
        logits += jnp.sum(scaled.astype(jnp.float32) * router_ref[:, span], axis=1, keepdims=True)
    gate = jax.nn.sigmoid(logits)

    loads[0].wait()
    loads[1].wait()
    hidden = wg.shape[1]
    block = depth // n

    def expand(j, sums):
        at = cut(j * block, block)
        part = normed[:, at]
        return (
            sums[0] + jnp.dot(part, wg[at, :], preferred_element_type=jnp.float32),
            sums[1] + jnp.dot(part, wu[at, :], preferred_element_type=jnp.float32),
        )

    zero = jnp.zeros((count, hidden), jnp.float32)
    gate_part, up_part = lax.fori_loop(0, n, expand, (zero, zero))
    inner = (jax.nn.silu(gate_part) * up_part).astype(jnp.bfloat16)
    loads[2].wait()

    def partial(k, side):
        at = lax.rem(z + k, nz) * 2 + side
        return jnp.dot(inner, wd[:, cut(at * block, block)], preferred_element_type=jnp.float32)

    order = list(range(1, nz)) + [0]
    pairs = {}
    for k in order:
        p_buf[k] = partial(k, 1 - x).astype(jnp.bfloat16)
        pairs[k] = push(p_buf.at[k], x_buf.at[k], x_send.at[k], x_recv.at[k], partner)
    for k in order:
        mine[k] = partial(k, x)
    sent = []
    for k in order:
        pairs[k].wait_recv()
        if k:
            s_buf[k] = (mine[k] + x_buf[k].astype(jnp.float32)).astype(jnp.bfloat16)
            sent.append(push(s_buf.at[k], z_buf.at[k], z_send.at[k], z_recv.at[k], along[k - 1]))
    total = mine[0] + x_buf[0].astype(jnp.float32)
    for k in range(1, nz):
        sent[k - 1].wait_recv()
        total += z_buf[k].astype(jnp.float32)
    weighted = (gate * total).astype(jnp.bfloat16)
    w_buf[...] = jnp.dot(unpack_ref[...], weighted, preferred_element_type=jnp.float32).astype(jnp.bfloat16)

    per = n // ne
    target = me // per
    turn = lax.rem(me, per)

    def deliver(i):
        to = lax.rem(me + i, n)
        at = turn * ne + place
        return pltpu.make_async_remote_copy(
            src_ref=w_buf.at[cut(to * cap, cap), :],
            dst_ref=o_ref.at[cut(place * cap, cap), cut(turn * block, block)],
            send_sem=t_send.at[i], recv_sem=t_recv.at[at],
            device_id={"seq": to, "exp": target}, device_id_type=MESH,
        )

    home = pltpu.make_async_copy(
        w_buf.at[cut(me * cap, cap), :], o_ref.at[cut(place * cap, cap), cut(turn * block, block)], own.at[2]
    )
    stays = target == place
    for i in range(1, n):
        deliver(i).start()

    @pl.when(stays)
    def _():
        home.start()

    @pl.when(jnp.logical_not(stays))
    def _():
        deliver(0).start()

    for k in range(per):
        for e in range(ne):
            arrival = pltpu.make_async_remote_copy(
                src_ref=w_buf.at[cut(me * cap, cap), :],
                dst_ref=o_ref.at[e * cap : (e + 1) * cap, k * block : (k + 1) * block],
                send_sem=t_send.at[0], recv_sem=t_recv.at[k * ne + e],
                device_id=partner, device_id_type=MESH,
            )

            @pl.when(jnp.logical_not(stays & (turn == k) & (place == e)))
            def _():
                arrival.wait_recv()

    @pl.when(stays)
    def _():
        home.wait()

    @pl.when(jnp.logical_not(stays))
    def _():
        deliver(0).wait_send()

    for i in range(1, n):
        deliver(i).wait_send()
    for copy in first + scales + list(hops.values()) + list(pairs.values()) + sent:
        copy.wait_send()


def run_experts(hidden_state, pick_rows, pack, unpack, norm_gain, router_row, w_gate, w_up, w_down, n, ne):
    count, slots = pack.shape
    cap = slots // n
    width = hidden_state.shape[1]
    depth, hidden = w_gate.shape
    nz, block = n // 2, depth // n
    bf, f32 = jnp.bfloat16, jnp.float32
    inside = pl.BlockSpec(memory_space=pltpu.VMEM)
    anywhere = pl.BlockSpec(memory_space=pl.ANY)
    slab = pltpu.VMEM((nz, count, block), bf)
    sems = lambda size: pltpu.SemaphoreType.DMA((size,))
    return pl.pallas_call(
        functools.partial(experts_kernel, n, ne, cap),
        out_shape=jax.ShapeDtypeStruct((ne * cap, width), bf),
        in_specs=[inside] * 6 + [anywhere] * 3,
        out_specs=anywhere,
        scratch_shapes=[
            pltpu.VMEM((depth, hidden), bf), pltpu.VMEM((depth, hidden), bf), pltpu.VMEM((hidden, depth), bf),
            pltpu.VMEM((ne * cap, width), bf), pltpu.VMEM((slots, depth), bf), pltpu.VMEM((1, depth), f32),
            pltpu.VMEM((count, depth), bf), pltpu.VMEM((nz, count, block), f32),
            slab, slab, slab, slab, pltpu.VMEM((slots, block), bf),
            sems(3), sems(ne), sems(ne), sems(ne), sems(ne), sems(ne * n), sems(ne * n),
            sems(nz), sems(nz), sems(nz), sems(nz), sems(n), sems(n), sems(3),
        ],
        compiler_params=pltpu.CompilerParams(
            collective_id=2, has_side_effects=True, vmem_limit_bytes=56 * 1024 * 1024
        ),
    )(hidden_state, pick_rows, pack, unpack, norm_gain, router_row, w_gate, w_up, w_down)


def flash_kernel(block, border_ref, q_ref, k_ref, v_ref, o_ref):
    at = pl.program_id(1)
    border = border_ref[0]
    q_start = at * block
    rows = q_start + lax.broadcasted_iota(jnp.int32, (block, 1), 0)
    low = jnp.where(rows >= border, border, 0)
    steps = lax.broadcasted_iota(jnp.int32, (block, block), 1)
    q = q_ref[...]
    scale = math.log2(math.e) / math.sqrt(HD)

    def scored(j):
        start = pl.multiple_of(j * block, block)
        s = lax.dot_general(
            q, k_ref[pl.ds(start, block), :], (((1,), (1,)), ((), ())), preferred_element_type=jnp.float32
        )
        return s * scale, start

    def mix(p, start):
        return jnp.dot(
            p.astype(jnp.bfloat16), v_ref[pl.ds(start, block), :], preferred_element_type=jnp.float32
        )

    s, start = scored(at)
    s = jnp.where((steps >= low - start) & (steps <= rows - start), s, -jnp.inf)
    top = jnp.max(s, axis=1, keepdims=True)
    p = jnp.exp2(s - top)
    state = (top, jnp.sum(p, axis=1, keepdims=True), mix(p, start))

    def step(j, state):
        top, total, out = state
        s, start = scored(j)
        s = jnp.where(steps >= low - start, s, -jnp.inf)
        new_top = jnp.maximum(top, jnp.max(s, axis=1, keepdims=True))
        factor = jnp.exp2(top - new_top)
        p = jnp.exp2(s - new_top)
        return (
            new_top,
            total * factor + jnp.sum(p, axis=1, keepdims=True),
            out * factor + mix(p, start),
        )

    begin = jnp.where(q_start >= border, border // block, 0)
    top, total, out = lax.fori_loop(begin, at, step, state)
    o_ref[...] = (out / total).astype(o_ref.dtype)


def flash(queries, keys, values, border):
    rows, width = queries.shape
    block = block_rows
    return pl.pallas_call(
        functools.partial(flash_kernel, block),
        out_shape=jax.ShapeDtypeStruct((rows, width), queries.dtype),
        grid_spec=pltpu.PrefetchScalarGridSpec(
            num_scalar_prefetch=1,
            grid=(width // HD, rows // block),
            in_specs=[
                pl.BlockSpec((block, HD), lambda h, i, b: (i, h)),
                pl.BlockSpec((rows, HD), lambda h, i, b: (0, h)),
                pl.BlockSpec((rows, HD), lambda h, i, b: (0, h)),
            ],
            out_specs=pl.BlockSpec((block, HD), lambda h, i, b: (i, h)),
        ),
    )(border, queries, keys, values)


def attend_by_head(queries, keys, values, documents, n, n_exp):
    border = jnp.sum((documents == 0).astype(jnp.int32)).reshape(1)
    q_all, k_all, v_all = heads_out(queries, keys, values, n)
    return heads_back(flash(q_all, k_all, v_all, border), n, n_exp)


def chain_kernel(
    nz, ne, group, causal_span, border_ref, q_ref, k_ref, v_ref, o_ref,
    q0, q1, q2, kb, vb, o0, o1, c0, c1, s2, s1, p2, p1, ls2, ls1, lp2, lp1, fin, back,
    load, x_send, x_recv, d0_send, d0_recv, d1_send, d1_recv, u2_send, u2_recv, g2_send, g2_recv,
    u1_send, u1_recv, g1_send, g1_recv, b_send, b_recv, y_send, y_recv, m_send, m_recv,
    r_send, r_recv, own,
):
    me = lax.axis_index("seq")
    place = lax.axis_index("exp")
    z, x = me // 2, lax.rem(me, 2)
    y, core = place // 2, lax.rem(place, 2)
    ny = ne // 2
    tokens = q_ref.shape[0]
    steps = 2 * group
    up = {"seq": lax.rem(z + 1, nz) * 2 + x}
    down = {"seq": lax.rem(z + nz - 1, nz) * 2 + x}
    partner = {"seq": z * 2 + 1 - x}
    sibling = {"exp": y * 2 + 1 - core}
    far_place = lax.rem(y + 1, ny) * 2 + core
    far = {"exp": far_place}
    has1, has2, low1 = z + 1 < nz, z + 2 < nz, z >= 1
    border = border_ref[0]
    scale = math.log2(math.e) / math.sqrt(HD)
    greet([up, down, partner, sibling, far])

    def remote(src, dst, send, recv, peer):
        return pltpu.make_async_remote_copy(
            src_ref=src, dst_ref=dst, send_sem=send, recv_sem=recv, device_id=peer, device_id_type=MESH
        )

    def half(ref, h, side):
        return ref.at[h, cut(side * tokens, tokens), :]

    def columns(ref, h, side):
        return ref.at[:, cut((side * group + h) * HD, HD)]

    def loads(h):
        return (
            pltpu.make_async_copy(columns(q_ref, h, x), q0.at[2 * h], load.at[3 * h]),
            pltpu.make_async_copy(columns(k_ref, h, x), half(kb, h, x), load.at[3 * h + 1]),
            pltpu.make_async_copy(columns(v_ref, h, x), half(vb, h, x), load.at[3 * h + 2]),
        )

    def swaps(h):
        side = 1 - x
        return tuple(
            remote(columns(src, h, side), dst, x_send.at[3 * h + t], x_recv.at[3 * h + t], partner)
            for t, (src, dst) in enumerate(
                ((q_ref, q0.at[2 * h + 1]), (k_ref, half(kb, h, x)), (v_ref, half(vb, h, x)))
            )
        )

    def q_down(t):
        return remote(q0.at[t], q1.at[t], d0_send.at[t], d0_recv.at[t], down)

    def q_further(t):
        return remote(q1.at[t], q2.at[t], d1_send.at[t], d1_recv.at[t], down)

    def part2_up(t):
        return (
            remote(s2.at[t], p2.at[t], u2_send.at[t], u2_recv.at[t], up),
            remote(ls2.at[t], lp2.at[t], g2_send.at[t], g2_recv.at[t], up),
        )

    def part1_up(t):
        return (
            remote(s1.at[t], p1.at[t], u1_send.at[t], u1_recv.at[t], up),
            remote(ls1.at[t], lp1.at[t], g1_send.at[t], g1_recv.at[t], up),
        )

    def give_back(t):
        return remote(back.at[t // 2], fin.at[t], b_send.at[t // 2], b_recv.at[t // 2], partner)

    def spot(at, t):
        j = lax.rem(t, 2)
        side = x + j * (1 - 2 * x)
        return o_ref.at[:, cut(((at * 2 + side) * group + t // 2) * HD, HD)]

    def keep(t):
        return pltpu.make_async_copy(fin.at[t], spot(place, t), own.at[t])

    def to_far(t):
        return remote(fin.at[t], spot(place, t), y_send.at[t], y_recv.at[t], far)

    def to_sibling(t):
        return remote(fin.at[t], spot(place, t), m_send.at[t], m_recv.at[t], sibling)

    def relay(t):
        return remote(spot(far_place, t), spot(far_place, t), r_send.at[t], r_recv.at[t], sibling)

    tile = HD
    tiles = tokens // tile
    span = kb.shape[1]
    key_base = z * span
    diagonal = lax.broadcasted_iota(jnp.int32, (tile, tile), 0) == lax.broadcasted_iota(
        jnp.int32, (tile, tile), 1
    )

    def attend(q_of, h, level, t, put):
        j = lax.rem(t, 2)
        side = x + j * (1 - 2 * x)
        base = ((z + level) * 2 + side) * tokens - key_base
        edge = border - key_base
        keys, vals = kb[h], vb[h]
        at = lax.broadcasted_iota(jnp.int32, (tile, span), 1)
        for r in range(tiles):
            rows = base + r * tile + lax.broadcasted_iota(jnp.int32, (tile, 1), 0)
            low = jnp.where(rows >= edge, edge, -key_base)
            s = lax.dot_general(
                q_of[r * tile : (r + 1) * tile, :], keys, (((1,), (1,)), ((), ())),
                preferred_element_type=jnp.float32,
            )
            seen = at >= low
            if level == 0:
                seen = seen & (at <= rows)
            s = jnp.where(seen, s, -1e30)
            top = jnp.max(s, axis=1, keepdims=True) * scale
            p = jnp.exp2(s * scale - top)
            total = jnp.sum(p, axis=1, keepdims=True)
            out = jnp.dot(p.astype(jnp.bfloat16), vals, preferred_element_type=jnp.float32)
            put(r, out / total, top + jnp.log2(total))

    def flat(level):
        return jnp.sum(jnp.where(diagonal, level, 0.0), axis=0, keepdims=True)

    def upright(ref, r):
        return jnp.sum(jnp.where(diagonal, ref[r : r + 1, :], 0.0), axis=1, keepdims=True)

    def joined(out, level, p_of, l_of, r):
        other = upright(l_of, r)
        top = jnp.maximum(level, other)
        mine, theirs = jnp.exp2(level - top), jnp.exp2(other - top)
        both = mine + theirs
        out = (out * mine + p_of[r * tile : (r + 1) * tile, :].astype(jnp.float32) * theirs) / both
        return out, top + jnp.log2(both)

    for h in range(group):
        for copy in swaps(h):
            copy.start()
        for copy in loads(h):
            copy.start()

    def send_own(t):
        @pl.when(lax.rem(t, 2) == 0)
        def _():
            loads(t // 2)[0].wait()

        @pl.when(lax.rem(t, 2) == 1)
        def _():
            swaps(t // 2)[0].wait_recv()

        @pl.when(low1)
        def _():
            q_down(t).start()

    def forward(t):
        @pl.when(has1)
        def _():
            q_down(t).wait_recv()

            @pl.when(low1)
            def _():
                q_further(t).start()

    def spread(t):
        keep(t).start()
        to_far(t).start()
        to_sibling(t).start()

    send_own(jnp.int32(0))
    send_own(jnp.int32(1))
    forward(jnp.int32(0))

    def step(i, carry):
        live = i < steps

        @pl.when(i + 2 < steps)
        def _():
            send_own(i + 2)

        @pl.when(i + 1 < steps)
        def _():
            forward(i + 1)

        @pl.when(live & (lax.rem(i, 2) == 0))
        def _():
            for copy in loads(i // 2)[1:]:
                copy.wait()
            for copy in swaps(i // 2)[1:]:
                copy.wait_recv()

        @pl.when(live & has2)
        def _():
            q_further(i).wait_recv()

            def put(r, out, level):
                s2[i, r * tile : (r + 1) * tile, :] = out.astype(jnp.bfloat16)
                ls2[i, r : r + 1, :] = flat(level)

            attend(q2.at[i], i // 2, 2, i, put)
            for copy in part2_up(i):
                copy.start()

        t1 = i - 1

        @pl.when((t1 >= 0) & (t1 < steps) & has1)
        def _():
            def put(r, out, level):
                s1[t1, r * tile : (r + 1) * tile, :] = out.astype(jnp.bfloat16)
                ls1[t1, r : r + 1, :] = flat(level)

            @pl.when(low1)
            def _():
                for copy in part2_up(t1):
                    copy.wait_recv()
                for r in range(tiles):
                    put(r, *joined(o1[t1, r * tile : (r + 1) * tile, :], c1[t1, r * tile : (r + 1) * tile, :], p2.at[t1], lp2.at[t1], r))

            @pl.when(jnp.logical_not(low1))
            def _():
                for r in range(tiles):
                    put(r, o1[t1, r * tile : (r + 1) * tile, :], c1[t1, r * tile : (r + 1) * tile, :])

            for copy in part1_up(t1):
                copy.start()

        @pl.when(live & has1)
        def _():
            def put(r, out, level):
                o1[i, r * tile : (r + 1) * tile, :] = out
                c1[i, r * tile : (r + 1) * tile, :] = level

            attend(q1.at[i], i // 2, 1, i, put)

        t0 = i - 2

        @pl.when((t0 >= 0) & (t0 < steps))
        def _():
            def finish(put):
                @pl.when(low1)
                def _():
                    for copy in part1_up(t0):
                        copy.wait_recv()
                    for r in range(tiles):
                        out, level = joined(o0[t0, r * tile : (r + 1) * tile, :], c0[t0, r * tile : (r + 1) * tile, :], p1.at[t0], lp1.at[t0], r)
                        put(r, out)

                @pl.when(jnp.logical_not(low1))
                def _():
                    for r in range(tiles):
                        put(r, o0[t0, r * tile : (r + 1) * tile, :])

            @pl.when(lax.rem(t0, 2) == 0)
            def _():
                def put(r, out):
                    fin[t0, r * tile : (r + 1) * tile, :] = out.astype(jnp.bfloat16)

                finish(put)
                spread(t0)

            @pl.when(lax.rem(t0, 2) == 1)
            def _():
                def put(r, out):
                    back[t0 // 2, r * tile : (r + 1) * tile, :] = out.astype(jnp.bfloat16)

                finish(put)
                give_back(t0).start()

        @pl.when(live)
        def _():
            def put(r, out, level):
                o0[i, r * tile : (r + 1) * tile, :] = out
                c0[i, r * tile : (r + 1) * tile, :] = level

            attend(q0.at[i], i // 2, 0, i, put)

        t4 = i - 3

        @pl.when((t4 >= 0) & (t4 < steps) & (lax.rem(t4, 2) == 1))
        def _():
            give_back(t4).wait_recv()
            spread(t4)

        t5 = i - 5

        @pl.when((t5 >= 0) & (t5 < steps))
        def _():
            to_far(t5).wait_recv()
            relay(t5).start()

        return carry

    lax.fori_loop(0, steps + 5, step, 0)

    def settle(t, carry):
        to_sibling(t).wait_recv()
        relay(t).wait_recv()
        keep(t).wait()
        to_far(t).wait_send()
        to_sibling(t).wait_send()
        relay(t).wait_send()

        @pl.when(low1)
        def _():
            q_down(t).wait_send()

            @pl.when(has1)
            def _():
                q_further(t).wait_send()

        @pl.when(has1)
        def _():
            for copy in part1_up(t):
                copy.wait_send()

        @pl.when(has2)
        def _():
            for copy in part2_up(t):
                copy.wait_send()

        @pl.when(lax.rem(t, 2) == 1)
        def _():
            give_back(t).wait_send()
            for copy in swaps(t // 2):
                copy.wait_send()

        return carry

    lax.fori_loop(0, steps, settle, 0)


def attend_by_chain(queries, keys, values, documents, n, n_exp):
    tokens, width = queries.shape
    group = width // HD // 2
    steps = 2 * group
    nz = n // 2
    border = jnp.sum((documents == 0).astype(jnp.int32)).reshape(1)
    anywhere = pl.BlockSpec(memory_space=pl.ANY)
    bf, f32 = jnp.bfloat16, jnp.float32
    chunks = pltpu.VMEM((steps, tokens, HD), bf)
    side = pltpu.VMEM((group, 2 * tokens, HD), bf)
    wide = pltpu.VMEM((steps, tokens, HD), f32)
    thin = pltpu.VMEM((steps, tokens, 1), f32)
    flats = pltpu.VMEM((steps, max(8, tokens // HD), HD), f32)
    sems = lambda count: pltpu.SemaphoreType.DMA((count,))
    return pl.pallas_call(
        functools.partial(chain_kernel, nz, n_exp, group, None),
        out_shape=jax.ShapeDtypeStruct((tokens, n_exp * width), queries.dtype),
        in_specs=[pl.BlockSpec(memory_space=pltpu.SMEM)] + [anywhere] * 3,
        out_specs=anywhere,
        scratch_shapes=[chunks] * 3 + [side] * 2 + [wide] * 2 + [thin] * 2 + [chunks] * 4 + [flats] * 4
        + [chunks, pltpu.VMEM((group, tokens, HD), bf)]
        + [sems(3 * group)] * 3 + [sems(steps)] * 12 + [sems(group)] * 2 + [sems(steps)] * 6 + [sems(steps)],
        compiler_params=pltpu.CompilerParams(
            collective_id=0, has_side_effects=True, vmem_limit_bytes=48 * 1024 * 1024
        ),
    )(border, queries, keys, values)


def attend_by_token(queries, keys, values, documents):
    tokens = queries.shape[0]
    heads_here = queries.shape[1] // HD
    seq_pos = lax.axis_index("seq")
    start_row = seq_pos * tokens
    query_pos = start_row + jnp.arange(tokens, dtype=jnp.int32)
    query_doc = lax.dynamic_slice_in_dim(documents, start_row, tokens, 0)
    query_heads = queries.reshape(tokens, heads_here, HD)
    score_scale = 1.0 / math.sqrt(HD)

    def attend(state, key_rows, value_rows, key_start):
        row_count = key_rows.shape[0]
        key_pos = key_start + jnp.arange(row_count, dtype=jnp.int32)
        key_doc = lax.dynamic_slice_in_dim(documents, key_start, row_count, 0)
        scores = (
            jnp.einsum(
                "qhd,khd->qhk",
                query_heads,
                key_rows.reshape(row_count, heads_here, HD),
                preferred_element_type=jnp.float32,
            )
            * score_scale
        )
        allowed = (key_pos[None, :] <= query_pos[:, None]) & (
            key_doc[None, :] == query_doc[:, None]
        )
        scores = jnp.where(allowed[:, None, :], scores, -jnp.inf)
        running_max, running_sum, running_out = state
        new_max = jnp.maximum(running_max, jnp.max(scores, axis=2))
        factor = jnp.exp(running_max - new_max)
        weights = jnp.exp(scores - new_max[:, :, None])
        running_sum = running_sum * factor + jnp.sum(weights, axis=2)
        running_out = running_out * factor[:, :, None] + jnp.einsum(
            "qhk,khd->qhd",
            weights.astype(jnp.bfloat16),
            value_rows.reshape(row_count, heads_here, HD),
            preferred_element_type=jnp.float32,
        )
        return (new_max, running_sum, running_out)

    def visit_block(state, key_rows, value_rows, key_start):
        row_count = key_rows.shape[0]
        last_doc = lax.dynamic_index_in_dim(documents, key_start + row_count - 1, 0, keepdims=False)
        beyond = (key_start > query_pos[tokens - 1]) | (last_doc < query_doc[0])
        return lax.cond(
            beyond,
            lambda inner_state: inner_state,
            lambda inner_state: attend(inner_state, key_rows, value_rows, key_start),
            state,
        )

    initial = (
        jnp.full((tokens, heads_here), -1e30, jnp.float32),
        jnp.zeros((tokens, heads_here), jnp.float32),
        jnp.zeros((tokens, heads_here, HD), jnp.float32),
    )
    state = initial
    key_piece = lax.all_gather(keys, "seq", axis=0, tiled=True)
    value_piece = lax.all_gather(values, "seq", axis=0, tiled=True)
    row_count = key_piece.shape[0]
    blocks = row_count // block_rows
    key_stack = key_piece.reshape(blocks, block_rows, key_piece.shape[1])
    value_stack = value_piece.reshape(blocks, block_rows, value_piece.shape[1])

    def scan_step(inner_state, block_item):
        block_index, key_rows, value_rows = block_item
        return (visit_block(inner_state, key_rows, value_rows, block_index * block_rows), None)

    state, unused = lax.scan(
        scan_step, state, (jnp.arange(blocks, dtype=jnp.int32), key_stack, value_stack)
    )
    running_max, running_sum, running_out = state
    attended = (
        (running_out / running_sum[:, :, None])
        .reshape(tokens, heads_here * HD)
        .astype(jnp.bfloat16)
    )
    return lax.all_gather(attended, "exp", axis=1, tiled=True)


def shards(
    residual,
    queries,
    keys,
    values,
    documents,
    out_proj,
    modality,
    norm_gain,
    picks,
    router,
    w_gate,
    w_up,
    w_down,
):
    tokens = queries.shape[0]
    seq_pos = lax.axis_index("seq")
    start_row = seq_pos * tokens
    n_seq, n_exp = lax.axis_size("seq"), lax.axis_size("exp")
    if (queries.shape[1] // HD) % n_seq == 0 and n_exp % 2 == 0:
        attended = attend_by_chain(queries, keys, values, documents, n_seq, n_exp)
    else:
        attended = attend_by_token(queries, keys, values, documents)
    mixed = jnp.dot(
        attended,
        out_proj,
        preferred_element_type=jnp.float32,
    )
    hidden_state = (residual.astype(jnp.float32) + mixed).astype(jnp.bfloat16)
    hidden_wide = hidden_state.astype(jnp.float32)
    capacity = tokens // 32
    inside = (picks >= start_row) & (picks < start_row + tokens)
    slot_index = jnp.cumsum(inside.astype(jnp.int32), axis=1) - 1
    matched = inside[:, None, :] & (
        slot_index[:, None, :] == jnp.arange(capacity, dtype=jnp.int32)[None, :, None]
    )
    local_index = jnp.sum(jnp.where(matched, picks[:, None, :] - start_row, 0), axis=2)
    filled = jnp.any(matched, axis=2)
    placing = (
        (jnp.arange(tokens, dtype=jnp.int32)[:, None] == local_index.reshape(1, -1))
        & filled.reshape(1, -1)
    ).astype(jnp.bfloat16)
    picked = lax.dynamic_index_in_dim(picks, lax.axis_index("exp"), 0, keepdims=False)
    home = picked // tokens
    rank = jnp.arange(picked.shape[0], dtype=jnp.int32) - jnp.sum(
        (home[None, :] < home[:, None]).astype(jnp.int32), axis=1
    )
    slot = home * capacity + rank
    pack = (slot[:, None] == jnp.arange(n_seq * capacity, dtype=jnp.int32)[None, :]).astype(jnp.bfloat16)
    returned = run_experts(
        hidden_state, placing.T, pack, pack.T, norm_gain, router.astype(jnp.float32).reshape(1, -1),
        w_gate[0], w_up[0], w_down[0], n_seq, n_exp,
    )
    expert_add = jnp.dot(placing, returned, preferred_element_type=jnp.float32)
    return (hidden_wide + expert_add).astype(jnp.bfloat16)


def solution(mesh):
    return jax.shard_map(
        shards,
        mesh=mesh,
        in_specs=(
            P("seq", "exp"),
            P("seq", "exp"),
            P("seq", "exp"),
            P("seq", "exp"),
            P(),
            P(None, "exp"),
            P("seq"),
            P(None, "exp"),
            P(),
            P(None, "exp"),
            P("exp", None, "seq"),
            P("exp", None, "seq"),
            P("exp", "seq", None),
        ),
        out_specs=P("seq", "exp"),
        check_vma=False,
    )
```

```python
import functools
import math

import jax
import jax.numpy as jnp
from jax import lax
from jax.experimental import pallas as pl
from jax.experimental.pallas import tpu as pltpu
from jax.sharding import PartitionSpec as P

D = 8192
HD = 128


block_rows = 512


MESH = pl.DeviceIdType.MESH


def greet(peers):
    barrier = pltpu.get_barrier_semaphore()
    for peer in peers:
        pl.semaphore_signal(barrier, inc=1, device_id=peer, device_id_type=MESH)
    pl.semaphore_wait(barrier, len(peers))


def cut(start, size):
    return pl.ds(pl.multiple_of(start, size), size)


def heads_out_kernel(n, width, q_ref, k_ref, v_ref, qo, ko, vo, send, recv, own):
    me = lax.axis_index("seq")
    tokens = q_ref.shape[0]
    greet([{"seq": lax.rem(me + i, n)} for i in range(1, n)])
    pairs = ((k_ref, ko), (v_ref, vo), (q_ref, qo))
    copies = []
    for i in range(1, n):
        to = lax.rem(me + i, n)
        for t, (src, dst) in enumerate(pairs):
            copies.append(
                pltpu.make_async_remote_copy(
                    src_ref=src.at[:, cut(to * width, width)],
                    dst_ref=dst.at[cut(me * tokens, tokens), :],
                    send_sem=send.at[t * n + i],
                    recv_sem=recv.at[t * n + i],
                    device_id={"seq": to},
                    device_id_type=MESH,
                )
            )
            copies[-1].start()
    for t, (src, dst) in enumerate(pairs):
        copies.append(
            pltpu.make_async_copy(
                src.at[:, cut(me * width, width)], dst.at[cut(me * tokens, tokens), :], own.at[t]
            )
        )
        copies[-1].start()
    for copy in copies:
        copy.wait()


def heads_out(queries, keys, values, n):
    tokens, columns = queries.shape
    width = columns // n
    whole = jax.ShapeDtypeStruct((n * tokens, width), queries.dtype)
    anywhere = pl.BlockSpec(memory_space=pl.ANY)
    return pl.pallas_call(
        functools.partial(heads_out_kernel, n, width),
        out_shape=(whole, whole, whole),
        in_specs=[anywhere] * 3,
        out_specs=(anywhere,) * 3,
        scratch_shapes=[
            pltpu.SemaphoreType.DMA((3 * n,)),
            pltpu.SemaphoreType.DMA((3 * n,)),
            pltpu.SemaphoreType.DMA((3,)),
        ],
        compiler_params=pltpu.CompilerParams(collective_id=0, has_side_effects=True),
    )(queries, keys, values)


def heads_back_kernel(n, ny, width, a_ref, o_ref, s_send, s_recv, y_send, y_recv, c_send, c_recv, own):
    me = lax.axis_index("seq")
    place = lax.axis_index("exp")
    y, core = place // 2, lax.rem(place, 2)
    sibling = {"exp": y * 2 + 1 - core}
    across = [{"exp": lax.rem(y + k, ny) * 2 + core} for k in range(1, ny)]
    tokens = o_ref.shape[0]
    span = n * width
    greet([{"seq": lax.rem(me + i, n)} for i in range(1, n)] + across + [sibling])

    def piece(exp_at, seq_at):
        return o_ref.at[:, cut(exp_at * span + seq_at * width, width)]

    local = pltpu.make_async_copy(a_ref.at[cut(me * tokens, tokens), :], piece(place, me), own)
    local.start()
    first = []
    for i in range(1, n):
        to = lax.rem(me + i, n)
        first.append(
            push(
                a_ref.at[cut(to * tokens, tokens), :],
                piece(place, me),
                s_send.at[i],
                s_recv.at[i],
                {"seq": to},
            )
        )
    second = []
    third = []
    for i in range(n):
        if i == 0:
            local.wait()
        else:
            first[i - 1].wait_recv()
        part = piece(place, lax.rem(me + n - i, n))
        for k in range(1, ny):
            at = i * ny + k
            second.append(push(part, part, y_send.at[at], y_recv.at[at], across[k - 1]))
        third.append(push(part, part, c_send.at[i * ny], c_recv.at[i * ny], sibling))
    for i in range(n):
        for k in range(1, ny):
            second[i * (ny - 1) + k - 1].wait_recv()
            at = i * ny + k
            part = piece(lax.rem(y + ny - k, ny) * 2 + core, lax.rem(me + n - i, n))
            third.append(push(part, part, c_send.at[at], c_recv.at[at], sibling))
    for copy in third:
        copy.wait_recv()
    for copy in first + second + third:
        copy.wait_send()


def heads_back(attended, n, n_exp):
    rows, width = attended.shape
    ny = n_exp // 2
    anywhere = pl.BlockSpec(memory_space=pl.ANY)
    return pl.pallas_call(
        functools.partial(heads_back_kernel, n, ny, width),
        out_shape=jax.ShapeDtypeStruct((rows // n, n_exp * n * width), attended.dtype),
        in_specs=[anywhere],
        out_specs=anywhere,
        scratch_shapes=[
            pltpu.SemaphoreType.DMA((n,)),
            pltpu.SemaphoreType.DMA((n,)),
            pltpu.SemaphoreType.DMA((n * ny,)),
            pltpu.SemaphoreType.DMA((n * ny,)),
            pltpu.SemaphoreType.DMA((n * ny,)),
            pltpu.SemaphoreType.DMA((n * ny,)),
            pltpu.SemaphoreType.DMA(()),
        ],
        compiler_params=pltpu.CompilerParams(collective_id=1, has_side_effects=True),
    )(attended)


def push(src, dst, send, recv, peer):
    copy = pltpu.make_async_remote_copy(
        src_ref=src, dst_ref=dst, send_sem=send, recv_sem=recv, device_id=peer, device_id_type=MESH
    )
    copy.start()
    return copy


def lines(me, nz):
    z, x = me // 2, lax.rem(me, 2)
    along = [{"seq": lax.rem(z + k, nz) * 2 + x} for k in range(1, nz)]
    return z, x, along, {"seq": z * 2 + 1 - x}


def ring_device(pos, n):
    half = pos // (n // 2)
    return (1 - half) * pos * 2 + half * ((n - 1 - pos) * 2 + 1)


def rows_kernel(n, ne, cap, width, r_ref, o_ref, e_send, e_recv, s_send, s_recv, own):
    me = lax.axis_index("seq")
    place = lax.axis_index("exp")
    z, x = me // 2, lax.rem(me, 2)
    pos = (1 - x) * z + x * (n - 1 - z)
    ways = (1, n - 1)
    nexts = [{"seq": ring_device(lax.rem(pos + way, n), n)} for way in ways]
    others = [{"exp": lax.rem(place + i, ne)} for i in range(1, ne)]
    greet(others + nexts)

    def piece(seq_at, exp_at):
        return o_ref.at[cut(seq_at * cap, cap), cut(exp_at * width, width)]

    local = pltpu.make_async_copy(r_ref.at[cut(place * cap, cap), :], piece(me, place), own)
    local.start()
    first = []
    for i in range(1, ne):
        src = r_ref.at[cut(lax.rem(place + i, ne) * cap, cap), :]
        first.append(push(src, piece(me, place), e_send.at[i], e_recv.at[i], others[i - 1]))
    hops = {}
    for t in range(n // 2):
        for i in range(ne):
            if t == 0:
                local.wait() if i == 0 else first[i - 1].wait_recv()
            for d in range(2):
                if t:
                    hops[i, d, t - 1].wait_recv()
                if t == n // 2 - 1 and i % 2 != d:
                    continue
                seq_at = ring_device(lax.rem(pos + n + t * (ways[1 - d]), n), n)
                part = piece(seq_at, lax.rem(place + ne - i, ne))
                at = (i * 2 + d) * (n // 2) + t
                hops[i, d, t] = push(part, part, s_send.at[at], s_recv.at[at], nexts[d])
    for i in range(ne):
        hops[i, i % 2, n // 2 - 1].wait_recv()
    for copy in first + list(hops.values()):
        copy.wait_send()


def share_rows(rows, n, ne):
    cap, width = rows.shape[0] // ne, rows.shape[1]
    anywhere = pl.BlockSpec(memory_space=pl.ANY)
    return pl.pallas_call(
        functools.partial(rows_kernel, n, ne, cap, width),
        out_shape=jax.ShapeDtypeStruct((n * cap, ne * width), rows.dtype),
        in_specs=[anywhere],
        out_specs=anywhere,
        scratch_shapes=[pltpu.SemaphoreType.DMA((ne,))] * 2
        + [pltpu.SemaphoreType.DMA((ne * n,))] * 2
        + [pltpu.SemaphoreType.DMA(())],
        compiler_params=pltpu.CompilerParams(collective_id=2, has_side_effects=True),
    )(rows)


def sums_kernel(
    nz, ne, cap, p_ref, g_ref, o_ref, x_buf, s_buf, z_buf, total, w_buf,
    x_send, x_recv, z_send, z_recv, e_send, e_recv, own,
):
    me = lax.axis_index("seq")
    z, x, along, partner = lines(me, nz)
    place = lax.axis_index("exp")
    others = [{"exp": lax.rem(place + i, ne)} for i in range(1, ne)]
    greet(along + [partner] + others)

    def rows_of(k, side):
        return cut((lax.rem(z + k, nz) * 2 + side) * cap, cap)

    order = list(range(1, nz)) + [0]
    pairs = {}
    for k in order:
        pairs[k] = push(p_ref.at[rows_of(k, 1 - x), :], x_buf.at[k], x_send.at[k], x_recv.at[k], partner)
    sent = []
    for k in order:
        pairs[k].wait_recv()
        both = p_ref[rows_of(k, x), :].astype(jnp.float32) + x_buf[k].astype(jnp.float32)
        if k:
            s_buf[k] = both.astype(jnp.bfloat16)
            sent.append(push(s_buf.at[k], z_buf.at[k], z_send.at[k], z_recv.at[k], along[k - 1]))
        else:
            total[...] = both
    for k in range(1, nz):
        sent[k - 1].wait_recv()
        total[...] += z_buf[k].astype(jnp.float32)
    w_buf[...] = (g_ref[...] * total[...]).astype(jnp.bfloat16)
    width = w_buf.shape[1] // ne
    mine = o_ref.at[cut(place * cap, cap), :]
    local = pltpu.make_async_copy(w_buf.at[:, cut(place * width, width)], mine, own)
    local.start()
    spread = []
    for i in range(1, ne):
        src = w_buf.at[:, cut(lax.rem(place + i, ne) * width, width)]
        spread.append(push(src, mine, e_send.at[i], e_recv.at[i], others[i - 1]))
    local.wait()
    for copy in spread:
        copy.wait_recv()
    for copy in list(pairs.values()) + sent + spread:
        copy.wait_send()


def sum_rows(partial, gate, n, ne):
    cap, width = partial.shape[0] // n, partial.shape[1]
    nz = n // 2
    slots = pltpu.VMEM((nz, cap, width), jnp.bfloat16)
    return pl.pallas_call(
        functools.partial(sums_kernel, nz, ne, cap),
        out_shape=jax.ShapeDtypeStruct((ne * cap, width // ne), jnp.bfloat16),
        in_specs=[pl.BlockSpec(memory_space=pltpu.VMEM)] * 2,
        out_specs=pl.BlockSpec(memory_space=pl.ANY),
        scratch_shapes=[slots, slots, slots]
        + [pltpu.VMEM((cap, width), jnp.float32), pltpu.VMEM((cap, width), jnp.bfloat16)]
        + [pltpu.SemaphoreType.DMA((nz,))] * 4
        + [pltpu.SemaphoreType.DMA((ne,))] * 2
        + [pltpu.SemaphoreType.DMA(())],
        compiler_params=pltpu.CompilerParams(collective_id=3, has_side_effects=True),
    )(partial, gate)


def experts_kernel(
    n, ne, cap, hid_ref, pick_ref, pack_ref, unpack_ref, gain_ref, router_ref, wg_ref, wu_ref, wd_ref, o_ref,
    wg, wu, wd, r_buf, rows, gains, normed, mine, p_buf, x_buf, s_buf, z_buf, w_buf,
    w_sem, e_send, e_recv, n_send, n_recv, s_send, s_recv, x_send, x_recv, z_send, z_recv,
    t_send, t_recv, own,
):
    me = lax.axis_index("seq")
    place = lax.axis_index("exp")
    nz, z, x = n // 2, me // 2, lax.rem(me, 2)
    loads = [
        pltpu.make_async_copy(src, dst, w_sem.at[t])
        for t, (src, dst) in enumerate(((wg_ref, wg), (wu_ref, wu), (wd_ref, wd)))
    ]
    for copy in loads:
        copy.start()
    pos = (1 - x) * z + x * (n - 1 - z)
    ways = (1, n - 1)
    nexts = [{"seq": ring_device(lax.rem(pos + way, n), n)} for way in ways]
    partner = {"seq": z * 2 + 1 - x}
    along = [{"seq": lax.rem(z + k, nz) * 2 + x} for k in range(1, nz)]
    others = [{"exp": lax.rem(place + i, ne)} for i in range(1, ne)]
    flat_at = me * ne + place
    everyone = n * ne

    barrier = pltpu.get_barrier_semaphore()

    def hello(i, carry):
        at = lax.rem(flat_at + i, everyone)
        pl.semaphore_signal(
            barrier, inc=1, device_id={"seq": at // ne, "exp": lax.rem(at, ne)}, device_id_type=MESH
        )
        return carry

    lax.fori_loop(1, everyone, hello, 0)
    r_buf[...] = jnp.dot(pick_ref[...], hid_ref[...], preferred_element_type=jnp.float32).astype(jnp.bfloat16)
    width = r_buf.shape[1]
    pl.semaphore_wait(barrier, everyone - 1)

    def piece(seq_at, exp_at):
        return rows.at[cut(seq_at * cap, cap), cut(exp_at * width, width)]

    def kind(e):
        return (2 * e) // ne

    local = pltpu.make_async_copy(r_buf.at[cut(place * cap, cap), :], piece(me, place), own.at[0])
    local.start()
    own_gain = pltpu.make_async_copy(
        gain_ref.at[pl.ds(kind(place), 1), :], gains.at[:, cut(place * width, width)], own.at[1]
    )
    own_gain.start()
    first = []
    scales = []
    for i in range(1, ne):
        to = lax.rem(place + i, ne)
        first.append(
            push(r_buf.at[cut(to * cap, cap), :], piece(me, place), e_send.at[i], e_recv.at[i], others[i - 1])
        )
    hops = {}
    for t in range(n // 2):
        for i in range(ne):
            if t == 0:
                local.wait() if i == 0 else first[i - 1].wait_recv()
            for d in range(2):
                if t:
                    hops[i, d, t - 1].wait_recv()
                if t == n // 2 - 1 and i % 2 != d:
                    continue
                seq_at = ring_device(lax.rem(pos + n + t * (ways[1 - d]), n), n)
                part = piece(seq_at, lax.rem(place + ne - i, ne))
                at = (i * 2 + d) * (n // 2) + t
                hops[i, d, t] = push(part, part, s_send.at[at], s_recv.at[at], nexts[d])
        if t == 0:
            for i in range(1, ne):
                to = lax.rem(place + i, ne)
                scales.append(
                    push(
                        gain_ref.at[pl.ds(kind(to), 1), :], gains.at[:, cut(place * width, width)],
                        n_send.at[i], n_recv.at[i], others[i - 1],
                    )
                )
    own_gain.wait()
    for copy in scales:
        copy.wait_recv()
    for i in range(ne):
        hops[i, i % 2, n // 2 - 1].wait_recv()

    count = pack_ref.shape[0]
    depth = ne * width
    square = jnp.zeros((count, 1), jnp.float32)
    for e in range(ne):
        span = slice(e * width, (e + 1) * width)
        packed = jnp.dot(pack_ref[...], rows[:, span], preferred_element_type=jnp.float32)
        square += jnp.sum(packed * packed, axis=1, keepdims=True)
        normed[:, span] = packed.astype(jnp.bfloat16)
    inverse = lax.rsqrt(square / depth + 1e-05)
    logits = jnp.zeros((count, 1), jnp.float32)
    for e in range(ne):
        span = slice(e * width, (e + 1) * width)
        scaled = (normed[:, span].astype(jnp.float32) * inverse * gains[:, span]).astype(jnp.bfloat16)
        normed[:, span] = scaled
        logits += jnp.sum(scaled.astype(jnp.float32) * router_ref[:, span], axis=1, keepdims=True)
    gate = jax.nn.sigmoid(logits)

    loads[0].wait()
    loads[1].wait()
    hidden = wg.shape[1]
    block = depth // n

    def expand(j, sums):
        at = cut(j * block, block)
        part = normed[:, at]
        return (
            sums[0] + jnp.dot(part, wg[at, :], preferred_element_type=jnp.float32),
            sums[1] + jnp.dot(part, wu[at, :], preferred_element_type=jnp.float32),
        )

    zero = jnp.zeros((count, hidden), jnp.float32)
    gate_part, up_part = lax.fori_loop(0, n, expand, (zero, zero))
    inner = (jax.nn.silu(gate_part) * up_part).astype(jnp.bfloat16)
    loads[2].wait()

    def partial(k, side):
        at = lax.rem(z + k, nz) * 2 + side
        return jnp.dot(inner, wd[:, cut(at * block, block)], preferred_element_type=jnp.float32)

    order = list(range(1, nz)) + [0]
    pairs = {}
    for k in order:
        p_buf[k] = partial(k, 1 - x).astype(jnp.bfloat16)
        pairs[k] = push(p_buf.at[k], x_buf.at[k], x_send.at[k], x_recv.at[k], partner)
    for k in order:
        mine[k] = partial(k, x)
    sent = []
    for k in order:
        pairs[k].wait_recv()
        if k:
            s_buf[k] = (mine[k] + x_buf[k].astype(jnp.float32)).astype(jnp.bfloat16)
            sent.append(push(s_buf.at[k], z_buf.at[k], z_send.at[k], z_recv.at[k], along[k - 1]))
    total = mine[0] + x_buf[0].astype(jnp.float32)
    for k in range(1, nz):
        sent[k - 1].wait_recv()
        total += z_buf[k].astype(jnp.float32)
    weighted = (gate * total).astype(jnp.bfloat16)
    w_buf[...] = jnp.dot(unpack_ref[...], weighted, preferred_element_type=jnp.float32).astype(jnp.bfloat16)

    per = n // ne
    target = me // per
    turn = lax.rem(me, per)

    def deliver(i):
        to = lax.rem(me + i, n)
        at = turn * ne + place
        return pltpu.make_async_remote_copy(
            src_ref=w_buf.at[cut(to * cap, cap), :],
            dst_ref=o_ref.at[cut(place * cap, cap), cut(turn * block, block)],
            send_sem=t_send.at[i], recv_sem=t_recv.at[at],
            device_id={"seq": to, "exp": target}, device_id_type=MESH,
        )

    home = pltpu.make_async_copy(
        w_buf.at[cut(me * cap, cap), :], o_ref.at[cut(place * cap, cap), cut(turn * block, block)], own.at[2]
    )
    stays = target == place
    for i in range(1, n):
        deliver(i).start()

    @pl.when(stays)
    def _():
        home.start()

    @pl.when(jnp.logical_not(stays))
    def _():
        deliver(0).start()

    for k in range(per):
        for e in range(ne):
            arrival = pltpu.make_async_remote_copy(
                src_ref=w_buf.at[cut(me * cap, cap), :],
                dst_ref=o_ref.at[e * cap : (e + 1) * cap, k * block : (k + 1) * block],
                send_sem=t_send.at[0], recv_sem=t_recv.at[k * ne + e],
                device_id=partner, device_id_type=MESH,
            )

            @pl.when(jnp.logical_not(stays & (turn == k) & (place == e)))
            def _():
                arrival.wait_recv()

    @pl.when(stays)
    def _():
        home.wait()

    @pl.when(jnp.logical_not(stays))
    def _():
        deliver(0).wait_send()

    for i in range(1, n):
        deliver(i).wait_send()
    for copy in first + scales + list(hops.values()) + list(pairs.values()) + sent:
        copy.wait_send()


def run_experts(hidden_state, pick_rows, pack, unpack, norm_gain, router_row, w_gate, w_up, w_down, n, ne):
    count, slots = pack.shape
    cap = slots // n
    width = hidden_state.shape[1]
    depth, hidden = w_gate.shape
    nz, block = n // 2, depth // n
    bf, f32 = jnp.bfloat16, jnp.float32
    inside = pl.BlockSpec(memory_space=pltpu.VMEM)
    anywhere = pl.BlockSpec(memory_space=pl.ANY)
    slab = pltpu.VMEM((nz, count, block), bf)
    sems = lambda size: pltpu.SemaphoreType.DMA((size,))
    return pl.pallas_call(
        functools.partial(experts_kernel, n, ne, cap),
        out_shape=jax.ShapeDtypeStruct((ne * cap, width), bf),
        in_specs=[inside] * 6 + [anywhere] * 3,
        out_specs=anywhere,
        scratch_shapes=[
            pltpu.VMEM((depth, hidden), bf), pltpu.VMEM((depth, hidden), bf), pltpu.VMEM((hidden, depth), bf),
            pltpu.VMEM((ne * cap, width), bf), pltpu.VMEM((slots, depth), bf), pltpu.VMEM((1, depth), f32),
            pltpu.VMEM((count, depth), bf), pltpu.VMEM((nz, count, block), f32),
            slab, slab, slab, slab, pltpu.VMEM((slots, block), bf),
            sems(3), sems(ne), sems(ne), sems(ne), sems(ne), sems(ne * n), sems(ne * n),
            sems(nz), sems(nz), sems(nz), sems(nz), sems(n), sems(n), sems(3),
        ],
        compiler_params=pltpu.CompilerParams(
            collective_id=2, has_side_effects=True, vmem_limit_bytes=56 * 1024 * 1024
        ),
    )(hidden_state, pick_rows, pack, unpack, norm_gain, router_row, w_gate, w_up, w_down)


def flash_kernel(block, border_ref, q_ref, k_ref, v_ref, o_ref):
    at = pl.program_id(1)
    border = border_ref[0]
    q_start = at * block
    rows = q_start + lax.broadcasted_iota(jnp.int32, (block, 1), 0)
    low = jnp.where(rows >= border, border, 0)
    steps = lax.broadcasted_iota(jnp.int32, (block, block), 1)
    q = q_ref[...]
    scale = math.log2(math.e) / math.sqrt(HD)

    def scored(j):
        start = pl.multiple_of(j * block, block)
        s = lax.dot_general(
            q, k_ref[pl.ds(start, block), :], (((1,), (1,)), ((), ())), preferred_element_type=jnp.float32
        )
        return s * scale, start

    def mix(p, start):
        return jnp.dot(
            p.astype(jnp.bfloat16), v_ref[pl.ds(start, block), :], preferred_element_type=jnp.float32
        )

    s, start = scored(at)
    s = jnp.where((steps >= low - start) & (steps <= rows - start), s, -jnp.inf)
    top = jnp.max(s, axis=1, keepdims=True)
    p = jnp.exp2(s - top)
    state = (top, jnp.sum(p, axis=1, keepdims=True), mix(p, start))

    def step(j, state):
        top, total, out = state
        s, start = scored(j)
        s = jnp.where(steps >= low - start, s, -jnp.inf)
        new_top = jnp.maximum(top, jnp.max(s, axis=1, keepdims=True))
        factor = jnp.exp2(top - new_top)
        p = jnp.exp2(s - new_top)
        return (
            new_top,
            total * factor + jnp.sum(p, axis=1, keepdims=True),
            out * factor + mix(p, start),
        )

    begin = jnp.where(q_start >= border, border // block, 0)
    top, total, out = lax.fori_loop(begin, at, step, state)
    o_ref[...] = (out / total).astype(o_ref.dtype)


def flash(queries, keys, values, border):
    rows, width = queries.shape
    block = block_rows
    return pl.pallas_call(
        functools.partial(flash_kernel, block),
        out_shape=jax.ShapeDtypeStruct((rows, width), queries.dtype),
        grid_spec=pltpu.PrefetchScalarGridSpec(
            num_scalar_prefetch=1,
            grid=(width // HD, rows // block),
            in_specs=[
                pl.BlockSpec((block, HD), lambda h, i, b: (i, h)),
                pl.BlockSpec((rows, HD), lambda h, i, b: (0, h)),
                pl.BlockSpec((rows, HD), lambda h, i, b: (0, h)),
            ],
            out_specs=pl.BlockSpec((block, HD), lambda h, i, b: (i, h)),
        ),
    )(border, queries, keys, values)


def attend_by_head(queries, keys, values, documents, n, n_exp):
    border = jnp.sum((documents == 0).astype(jnp.int32)).reshape(1)
    q_all, k_all, v_all = heads_out(queries, keys, values, n)
    return heads_back(flash(q_all, k_all, v_all, border), n, n_exp)


def chain_kernel(
    nz, ne, group, docs_ref, q_ref, k_ref, v_ref, res_ref, w_ref, o_ref,
    q0, q1, q2, kb, vb, o0, o1, c0, c1, s2, s1, p2, p1, ls2, ls1, lp2, lp1, back, att, proj, acc, res,
    load, x_send, x_recv, d0_send, d0_recv, d1_send, d1_recv, u2_send, u2_recv, g2_send, g2_recv,
    u1_send, u1_recv, g1_send, g1_recv, b_send, b_recv, y_send, y_recv, m_send, m_recv,
    r_send, r_recv, w_sem, res_sem,
):
    me = lax.axis_index("seq")
    place = lax.axis_index("exp")
    z, x = me // 2, lax.rem(me, 2)
    y, core = place // 2, lax.rem(place, 2)
    ny = ne // 2
    tokens = q_ref.shape[0]
    steps = 2 * group
    up = {"seq": lax.rem(z + 1, nz) * 2 + x}
    down = {"seq": lax.rem(z + nz - 1, nz) * 2 + x}
    partner = {"seq": z * 2 + 1 - x}
    sibling = {"exp": y * 2 + 1 - core}
    far_place = lax.rem(y + 1, ny) * 2 + core
    far = {"exp": far_place}
    has1, has2, low1 = z + 1 < nz, z + 2 < nz, z >= 1
    border = jnp.sum(
        jnp.sum((docs_ref[...] == 0).astype(jnp.int32), axis=1, keepdims=True), axis=0, keepdims=True
    )
    scale = math.log2(math.e) / math.sqrt(HD)
    greet([up, down, partner, sibling, far])

    def remote(src, dst, send, recv, peer):
        return pltpu.make_async_remote_copy(
            src_ref=src, dst_ref=dst, send_sem=send, recv_sem=recv, device_id=peer, device_id_type=MESH
        )

    def half(ref, h, side):
        return ref.at[h, cut(side * tokens, tokens), :]

    def columns(ref, h, side):
        return ref.at[:, cut((side * group + h) * HD, HD)]

    def loads(h):
        return (
            pltpu.make_async_copy(columns(q_ref, h, x), q0.at[2 * h], load.at[3 * h]),
            pltpu.make_async_copy(columns(k_ref, h, x), half(kb, h, x), load.at[3 * h + 1]),
            pltpu.make_async_copy(columns(v_ref, h, x), half(vb, h, x), load.at[3 * h + 2]),
        )

    def swaps(h):
        side = 1 - x
        return tuple(
            remote(columns(src, h, side), dst, x_send.at[3 * h + t], x_recv.at[3 * h + t], partner)
            for t, (src, dst) in enumerate(
                ((q_ref, q0.at[2 * h + 1]), (k_ref, half(kb, h, x)), (v_ref, half(vb, h, x)))
            )
        )

    def q_down(t):
        return remote(q0.at[t], q1.at[t], d0_send.at[t], d0_recv.at[t], down)

    def q_further(t):
        return remote(q1.at[t], q2.at[t], d1_send.at[t], d1_recv.at[t], down)

    def part2_up(t):
        return (
            remote(s2.at[t], p2.at[t], u2_send.at[t], u2_recv.at[t], up),
            remote(ls2.at[t], lp2.at[t], g2_send.at[t], g2_recv.at[t], up),
        )

    def part1_up(t):
        return (
            remote(s1.at[t], p1.at[t], u1_send.at[t], u1_recv.at[t], up),
            remote(ls1.at[t], lp1.at[t], g1_send.at[t], g1_recv.at[t], up),
        )

    def spot(at, t):
        return att.at[t, :, cut(at * HD, HD)]

    def give_back(t):
        return remote(back.at[t // 2], spot(place, t), b_send.at[t // 2], b_recv.at[t // 2], partner)

    def to_far(t):
        return remote(spot(place, t), spot(place, t), y_send.at[t], y_recv.at[t], far)

    def to_sibling(t):
        return remote(spot(place, t), spot(place, t), m_send.at[t], m_recv.at[t], sibling)

    def relay(t):
        return remote(spot(far_place, t), spot(far_place, t), r_send.at[t], r_recv.at[t], sibling)

    def proj_loads(t):
        side = x + (t % 2) * (1 - 2 * x)
        return [
            pltpu.make_async_copy(
                w_ref.at[cut(((e * 2 + side) * group + t // 2) * HD, HD), :],
                proj.at[t, e * HD : (e + 1) * HD, :],
                w_sem.at[t, e],
            )
            for e in range(ne)
        ]

    res_load = pltpu.make_async_copy(res_ref, res, res_sem)

    tile = HD
    tiles = tokens // tile
    span = kb.shape[1]
    key_base = z * span
    diagonal = lax.broadcasted_iota(jnp.int32, (tile, tile), 0) == lax.broadcasted_iota(
        jnp.int32, (tile, tile), 1
    )

    big = 2 * tile
    at = lax.broadcasted_iota(jnp.int32, (big, tokens), 1)

    def attend(q_of, level, t, put, blocks):
        h = t // 2
        side = x + lax.rem(t, 2) * (1 - 2 * x)
        base = ((z + level) * 2 + side) * tokens - key_base
        edge = border - key_base

        def score(r):
            rows = base + r * big + lax.broadcasted_iota(jnp.int32, (big, 1), 0)
            low = jnp.where(rows >= edge, edge, -key_base)
            out = []
            for b in range(blocks):
                s = lax.dot_general(
                    q_of[r * big : (r + 1) * big, :], kb[h, b * tokens : (b + 1) * tokens, :],
                    (((1,), (1,)), ((), ())), preferred_element_type=jnp.float32,
                )
                seen = at >= low - b * tokens
                if level == 0 and b == blocks - 1:
                    seen = seen & (at <= rows - b * tokens)
                out.append(jnp.where(seen, s, -1e30))
            return out

        later = score(0)
        for r in range(tokens // big):
            now = later
            if (r + 1) * big < tokens:
                later = score(r + 1)
            top = jnp.max(functools.reduce(jnp.maximum, now), axis=1, keepdims=True) * scale
            total = jnp.zeros((big, 1), jnp.float32)
            out = jnp.zeros((big, HD), jnp.float32)
            for b, s in enumerate(now):
                p = jnp.exp2(s * scale - top)
                total += jnp.sum(p, axis=1, keepdims=True)
                out += jnp.dot(
                    p.astype(jnp.bfloat16), vb[h, b * tokens : (b + 1) * tokens, :],
                    preferred_element_type=jnp.float32,
                )
            put(r * big, out / total, top + jnp.log2(total))

    def flat(level):
        return jnp.sum(jnp.where(diagonal, level, 0.0), axis=0, keepdims=True)

    def upright(ref, r):
        return jnp.sum(jnp.where(diagonal, ref[r : r + 1, :], 0.0), axis=1, keepdims=True)

    def joined(out, level, p_of, l_of, r):
        other = upright(l_of, r)
        top = jnp.maximum(level, other)
        mine, theirs = jnp.exp2(level - top), jnp.exp2(other - top)
        both = mine + theirs
        out = (out * mine + p_of[r * tile : (r + 1) * tile, :].astype(jnp.float32) * theirs) / both
        return out, top + jnp.log2(both)

    for h in range(group):
        for copy in swaps(h):
            copy.start()
        for copy in loads(h):
            copy.start()

    for t in range(steps):
        for copy in proj_loads(t):
            copy.start()
    res_load.start()

    def send_own(t):
        @pl.when(lax.rem(t, 2) == 0)
        def _():
            loads(t // 2)[0].wait()

        @pl.when(lax.rem(t, 2) == 1)
        def _():
            swaps(t // 2)[0].wait_recv()

        @pl.when(low1)
        def _():
            q_down(t).start()

    def forward(t):
        @pl.when(has1)
        def _():
            q_down(t).wait_recv()

            @pl.when(low1)
            def _():
                q_further(t).start()

    def spread(t):
        to_far(t).start()
        to_sibling(t).start()

    send_own(jnp.int32(0))
    send_own(jnp.int32(1))
    forward(jnp.int32(0))

    def step(i, carry):
        live = i < steps

        @pl.when(i + 2 < steps)
        def _():
            send_own(i + 2)

        @pl.when(i + 1 < steps)
        def _():
            forward(i + 1)

        @pl.when(live & (lax.rem(i, 2) == 0))
        def _():
            for copy in loads(i // 2)[1:]:
                copy.wait()
            for copy in swaps(i // 2)[1:]:
                copy.wait_recv()

        @pl.when(live & has2)
        def _():
            q_further(i).wait_recv()

            def put(at, out, level):
                s2[i, at : at + big, :] = out.astype(jnp.bfloat16)
                for r in range(big // tile):
                    row = at // tile + r
                    ls2[i, row : row + 1, :] = flat(level[r * tile : (r + 1) * tile])

            attend(q2.at[i], 2, i, put, 2)
            for copy in part2_up(i):
                copy.start()

        @pl.when(i == 1)
        def _():
            res_load.wait()
            acc[...] = res[...].astype(jnp.float32)

        t1 = i - 1

        @pl.when((t1 >= 0) & (t1 < steps) & has1)
        def _():
            def put(r, out, level):
                s1[t1, r * tile : (r + 1) * tile, :] = out.astype(jnp.bfloat16)
                ls1[t1, r : r + 1, :] = flat(level)

            @pl.when(low1)
            def _():
                for copy in part2_up(t1):
                    copy.wait_recv()
                for r in range(tiles):
                    put(r, *joined(o1[t1, r * tile : (r + 1) * tile, :], c1[t1, r * tile : (r + 1) * tile, :], p2.at[t1], lp2.at[t1], r))

            @pl.when(jnp.logical_not(low1))
            def _():
                for r in range(tiles):
                    put(r, o1[t1, r * tile : (r + 1) * tile, :], c1[t1, r * tile : (r + 1) * tile, :])

            for copy in part1_up(t1):
                copy.start()

        @pl.when(live & has1)
        def _():
            def put(at, out, level):
                o1[i, at : at + big, :] = out
                c1[i, at : at + big, :] = level

            attend(q1.at[i], 1, i, put, 2)

        t0 = i - 2

        @pl.when((t0 >= 0) & (t0 < steps))
        def _():
            def finish(put):
                @pl.when(low1)
                def _():
                    for copy in part1_up(t0):
                        copy.wait_recv()
                    for r in range(tiles):
                        out, level = joined(o0[t0, r * tile : (r + 1) * tile, :], c0[t0, r * tile : (r + 1) * tile, :], p1.at[t0], lp1.at[t0], r)
                        put(r, out)

                @pl.when(jnp.logical_not(low1))
                def _():
                    for r in range(tiles):
                        put(r, o0[t0, r * tile : (r + 1) * tile, :])

            @pl.when(lax.rem(t0, 2) == 0)
            def _():
                def put(r, out):
                    att[t0, r * tile : (r + 1) * tile, cut(place * HD, HD)] = out.astype(jnp.bfloat16)

                finish(put)
                spread(t0)

            @pl.when(lax.rem(t0, 2) == 1)
            def _():
                def put(r, out):
                    back[t0 // 2, r * tile : (r + 1) * tile, :] = out.astype(jnp.bfloat16)

                finish(put)
                give_back(t0).start()

        @pl.when(live)
        def _():
            def put(at, out, level):
                o0[i, at : at + big, :] = out
                c0[i, at : at + big, :] = level

            first_half = lax.rem(i, 2) == x

            @pl.when(first_half)
            def _():
                attend(q0.at[i], 0, i, put, 1)

            @pl.when(jnp.logical_not(first_half))
            def _():
                attend(q0.at[i], 0, i, put, 2)

        t4 = i - 3

        @pl.when((t4 >= 0) & (t4 < steps) & (lax.rem(t4, 2) == 1))
        def _():
            give_back(t4).wait_recv()
            spread(t4)

        t5 = i - 5

        @pl.when((t5 >= 0) & (t5 < steps))
        def _():
            to_far(t5).wait_recv()
            relay(t5).start()

        t6 = i - 6

        @pl.when((t6 >= 0) & (t6 < steps))
        def _():
            to_sibling(t6).wait_recv()
            relay(t6).wait_recv()
            for copy in proj_loads(t6):
                copy.wait()

            acc[...] += jnp.dot(att[t6], proj[t6], preferred_element_type=jnp.float32)

        return carry

    lax.fori_loop(0, steps + 6, step, 0)
    o_ref[...] = acc[...].astype(o_ref.dtype)


    def settle(t, carry):
        to_far(t).wait_send()
        to_sibling(t).wait_send()
        relay(t).wait_send()

        @pl.when(low1)
        def _():
            q_down(t).wait_send()

            @pl.when(has1)
            def _():
                q_further(t).wait_send()

        @pl.when(has1)
        def _():
            for copy in part1_up(t):
                copy.wait_send()

        @pl.when(has2)
        def _():
            for copy in part2_up(t):
                copy.wait_send()

        @pl.when(lax.rem(t, 2) == 1)
        def _():
            give_back(t).wait_send()
            for copy in swaps(t // 2):
                copy.wait_send()

        return carry

    lax.fori_loop(0, steps, settle, 0)


def attend_by_chain(queries, keys, values, documents, residual, out_proj, n, n_exp):
    tokens, width = queries.shape
    group = width // HD // 2
    steps = 2 * group
    nz = n // 2
    features = out_proj.shape[1]
    outside = pl.BlockSpec(memory_space=pltpu.HBM)
    inside = pl.BlockSpec(memory_space=pltpu.VMEM)
    bf, f32 = jnp.bfloat16, jnp.float32
    chunks = pltpu.VMEM((steps, tokens, HD), bf)
    side = pltpu.VMEM((group, 2 * tokens, HD), bf)
    wide = pltpu.VMEM((steps, tokens, HD), f32)
    thin = pltpu.VMEM((steps, tokens, 1), f32)
    flats = pltpu.VMEM((steps, max(8, tokens // HD), HD), f32)
    sems = lambda count: pltpu.SemaphoreType.DMA((count,))
    return pl.pallas_call(
        functools.partial(chain_kernel, nz, n_exp, group),
        out_shape=jax.ShapeDtypeStruct((tokens, features), queries.dtype),
        in_specs=[inside] + [outside] * 5,
        out_specs=inside,
        scratch_shapes=[chunks] * 3 + [side] * 2 + [wide] * 2 + [thin] * 2 + [chunks] * 4 + [flats] * 4
        + [pltpu.VMEM((group, tokens, HD), bf), pltpu.VMEM((steps, tokens, n_exp * HD), bf)]
        + [pltpu.VMEM((steps, n_exp * HD, features), bf), pltpu.VMEM((tokens, features), f32)]
        + [pltpu.VMEM((tokens, features), bf)]
        + [sems(3 * group)] * 3 + [sems(steps)] * 12 + [sems(group)] * 2 + [sems(steps)] * 6
        + [pltpu.SemaphoreType.DMA((steps, n_exp)), pltpu.SemaphoreType.DMA(())],
        compiler_params=pltpu.CompilerParams(
            collective_id=0, has_side_effects=True, vmem_limit_bytes=60 * 1024 * 1024
        ),
    )(documents.reshape(-1, HD), queries, keys, values, residual, out_proj)


def attend_by_token(queries, keys, values, documents):
    tokens = queries.shape[0]
    heads_here = queries.shape[1] // HD
    seq_pos = lax.axis_index("seq")
    start_row = seq_pos * tokens
    query_pos = start_row + jnp.arange(tokens, dtype=jnp.int32)
    query_doc = lax.dynamic_slice_in_dim(documents, start_row, tokens, 0)
    query_heads = queries.reshape(tokens, heads_here, HD)
    score_scale = 1.0 / math.sqrt(HD)

    def attend(state, key_rows, value_rows, key_start):
        row_count = key_rows.shape[0]
        key_pos = key_start + jnp.arange(row_count, dtype=jnp.int32)
        key_doc = lax.dynamic_slice_in_dim(documents, key_start, row_count, 0)
        scores = (
            jnp.einsum(
                "qhd,khd->qhk",
                query_heads,
                key_rows.reshape(row_count, heads_here, HD),
                preferred_element_type=jnp.float32,
            )
            * score_scale
        )
        allowed = (key_pos[None, :] <= query_pos[:, None]) & (
            key_doc[None, :] == query_doc[:, None]
        )
        scores = jnp.where(allowed[:, None, :], scores, -jnp.inf)
        running_max, running_sum, running_out = state
        new_max = jnp.maximum(running_max, jnp.max(scores, axis=2))
        factor = jnp.exp(running_max - new_max)
        weights = jnp.exp(scores - new_max[:, :, None])
        running_sum = running_sum * factor + jnp.sum(weights, axis=2)
        running_out = running_out * factor[:, :, None] + jnp.einsum(
            "qhk,khd->qhd",
            weights.astype(jnp.bfloat16),
            value_rows.reshape(row_count, heads_here, HD),
            preferred_element_type=jnp.float32,
        )
        return (new_max, running_sum, running_out)

    def visit_block(state, key_rows, value_rows, key_start):
        row_count = key_rows.shape[0]
        last_doc = lax.dynamic_index_in_dim(documents, key_start + row_count - 1, 0, keepdims=False)
        beyond = (key_start > query_pos[tokens - 1]) | (last_doc < query_doc[0])
        return lax.cond(
            beyond,
            lambda inner_state: inner_state,
            lambda inner_state: attend(inner_state, key_rows, value_rows, key_start),
            state,
        )

    initial = (
        jnp.full((tokens, heads_here), -1e30, jnp.float32),
        jnp.zeros((tokens, heads_here), jnp.float32),
        jnp.zeros((tokens, heads_here, HD), jnp.float32),
    )
    state = initial
    key_piece = lax.all_gather(keys, "seq", axis=0, tiled=True)
    value_piece = lax.all_gather(values, "seq", axis=0, tiled=True)
    row_count = key_piece.shape[0]
    blocks = row_count // block_rows
    key_stack = key_piece.reshape(blocks, block_rows, key_piece.shape[1])
    value_stack = value_piece.reshape(blocks, block_rows, value_piece.shape[1])

    def scan_step(inner_state, block_item):
        block_index, key_rows, value_rows = block_item
        return (visit_block(inner_state, key_rows, value_rows, block_index * block_rows), None)

    state, unused = lax.scan(
        scan_step, state, (jnp.arange(blocks, dtype=jnp.int32), key_stack, value_stack)
    )
    running_max, running_sum, running_out = state
    attended = (
        (running_out / running_sum[:, :, None])
        .reshape(tokens, heads_here * HD)
        .astype(jnp.bfloat16)
    )
    return lax.all_gather(attended, "exp", axis=1, tiled=True)


def shards(
    residual,
    queries,
    keys,
    values,
    documents,
    out_proj,
    modality,
    norm_gain,
    picks,
    router,
    w_gate,
    w_up,
    w_down,
):
    tokens = queries.shape[0]
    seq_pos = lax.axis_index("seq")
    start_row = seq_pos * tokens
    n_seq, n_exp = lax.axis_size("seq"), lax.axis_size("exp")
    if (queries.shape[1] // HD) % n_seq == 0 and n_exp == 4:
        hidden_state = attend_by_chain(
            queries, keys, values, documents, residual, out_proj, n_seq, n_exp
        )
    else:
        attended = attend_by_token(queries, keys, values, documents)
        mixed = jnp.dot(attended, out_proj, preferred_element_type=jnp.float32)
        hidden_state = (residual.astype(jnp.float32) + mixed).astype(jnp.bfloat16)
    hidden_wide = hidden_state.astype(jnp.float32)
    capacity = tokens // 32
    inside = (picks >= start_row) & (picks < start_row + tokens)
    slot_index = jnp.cumsum(inside.astype(jnp.int32), axis=1) - 1
    matched = inside[:, None, :] & (
        slot_index[:, None, :] == jnp.arange(capacity, dtype=jnp.int32)[None, :, None]
    )
    local_index = jnp.sum(jnp.where(matched, picks[:, None, :] - start_row, 0), axis=2)
    filled = jnp.any(matched, axis=2)
    placing = (
        (jnp.arange(tokens, dtype=jnp.int32)[:, None] == local_index.reshape(1, -1))
        & filled.reshape(1, -1)
    ).astype(jnp.bfloat16)
    picked = lax.dynamic_index_in_dim(picks, lax.axis_index("exp"), 0, keepdims=False)
    home = picked // tokens
    rank = jnp.arange(picked.shape[0], dtype=jnp.int32) - jnp.sum(
        (home[None, :] < home[:, None]).astype(jnp.int32), axis=1
    )
    slot = home * capacity + rank
    pack = (slot[:, None] == jnp.arange(n_seq * capacity, dtype=jnp.int32)[None, :]).astype(jnp.bfloat16)
    returned = run_experts(
        hidden_state, placing.T, pack, pack.T, norm_gain, router.astype(jnp.float32).reshape(1, -1),
        w_gate[0], w_up[0], w_down[0], n_seq, n_exp,
    )
    expert_add = jnp.dot(placing, returned, preferred_element_type=jnp.float32)
    return (hidden_wide + expert_add).astype(jnp.bfloat16)


def solution(mesh):
    return jax.shard_map(
        shards,
        mesh=mesh,
        in_specs=(
            P("seq", "exp"),
            P("seq", "exp"),
            P("seq", "exp"),
            P("seq", "exp"),
            P(),
            P(None, "exp"),
            P("seq"),
            P(None, "exp"),
            P(),
            P(None, "exp"),
            P("exp", None, "seq"),
            P("exp", None, "seq"),
            P("exp", "seq", None),
        ),
        out_specs=P("seq", "exp"),
        check_vma=False,
    )
```

```python
import functools
import math

import jax
import jax.numpy as jnp
from jax import lax
from jax.experimental import pallas as pl
from jax.experimental.pallas import tpu as pltpu
from jax.sharding import PartitionSpec as P

D = 8192
HD = 128


block_rows = 512


MESH = pl.DeviceIdType.MESH


def greet(peers):
    barrier = pltpu.get_barrier_semaphore()
    for peer in peers:
        pl.semaphore_signal(barrier, inc=1, device_id=peer, device_id_type=MESH)
    pl.semaphore_wait(barrier, len(peers))


def cut(start, size):
    return pl.ds(pl.multiple_of(start, size), size)


def heads_out_kernel(n, width, q_ref, k_ref, v_ref, qo, ko, vo, send, recv, own):
    me = lax.axis_index("seq")
    tokens = q_ref.shape[0]
    greet([{"seq": lax.rem(me + i, n)} for i in range(1, n)])
    pairs = ((k_ref, ko), (v_ref, vo), (q_ref, qo))
    copies = []
    for i in range(1, n):
        to = lax.rem(me + i, n)
        for t, (src, dst) in enumerate(pairs):
            copies.append(
                pltpu.make_async_remote_copy(
                    src_ref=src.at[:, cut(to * width, width)],
                    dst_ref=dst.at[cut(me * tokens, tokens), :],
                    send_sem=send.at[t * n + i],
                    recv_sem=recv.at[t * n + i],
                    device_id={"seq": to},
                    device_id_type=MESH,
                )
            )
            copies[-1].start()
    for t, (src, dst) in enumerate(pairs):
        copies.append(
            pltpu.make_async_copy(
                src.at[:, cut(me * width, width)], dst.at[cut(me * tokens, tokens), :], own.at[t]
            )
        )
        copies[-1].start()
    for copy in copies:
        copy.wait()


def heads_out(queries, keys, values, n):
    tokens, columns = queries.shape
    width = columns // n
    whole = jax.ShapeDtypeStruct((n * tokens, width), queries.dtype)
    anywhere = pl.BlockSpec(memory_space=pl.ANY)
    return pl.pallas_call(
        functools.partial(heads_out_kernel, n, width),
        out_shape=(whole, whole, whole),
        in_specs=[anywhere] * 3,
        out_specs=(anywhere,) * 3,
        scratch_shapes=[
            pltpu.SemaphoreType.DMA((3 * n,)),
            pltpu.SemaphoreType.DMA((3 * n,)),
            pltpu.SemaphoreType.DMA((3,)),
        ],
        compiler_params=pltpu.CompilerParams(collective_id=0, has_side_effects=True),
    )(queries, keys, values)


def heads_back_kernel(n, ny, width, a_ref, o_ref, s_send, s_recv, y_send, y_recv, c_send, c_recv, own):
    me = lax.axis_index("seq")
    place = lax.axis_index("exp")
    y, core = place // 2, lax.rem(place, 2)
    sibling = {"exp": y * 2 + 1 - core}
    across = [{"exp": lax.rem(y + k, ny) * 2 + core} for k in range(1, ny)]
    tokens = o_ref.shape[0]
    span = n * width
    greet([{"seq": lax.rem(me + i, n)} for i in range(1, n)] + across + [sibling])

    def piece(exp_at, seq_at):
        return o_ref.at[:, cut(exp_at * span + seq_at * width, width)]

    local = pltpu.make_async_copy(a_ref.at[cut(me * tokens, tokens), :], piece(place, me), own)
    local.start()
    first = []
    for i in range(1, n):
        to = lax.rem(me + i, n)
        first.append(
            push(
                a_ref.at[cut(to * tokens, tokens), :],
                piece(place, me),
                s_send.at[i],
                s_recv.at[i],
                {"seq": to},
            )
        )
    second = []
    third = []
    for i in range(n):
        if i == 0:
            local.wait()
        else:
            first[i - 1].wait_recv()
        part = piece(place, lax.rem(me + n - i, n))
        for k in range(1, ny):
            at = i * ny + k
            second.append(push(part, part, y_send.at[at], y_recv.at[at], across[k - 1]))
        third.append(push(part, part, c_send.at[i * ny], c_recv.at[i * ny], sibling))
    for i in range(n):
        for k in range(1, ny):
            second[i * (ny - 1) + k - 1].wait_recv()
            at = i * ny + k
            part = piece(lax.rem(y + ny - k, ny) * 2 + core, lax.rem(me + n - i, n))
            third.append(push(part, part, c_send.at[at], c_recv.at[at], sibling))
    for copy in third:
        copy.wait_recv()
    for copy in first + second + third:
        copy.wait_send()


def heads_back(attended, n, n_exp):
    rows, width = attended.shape
    ny = n_exp // 2
    anywhere = pl.BlockSpec(memory_space=pl.ANY)
    return pl.pallas_call(
        functools.partial(heads_back_kernel, n, ny, width),
        out_shape=jax.ShapeDtypeStruct((rows // n, n_exp * n * width), attended.dtype),
        in_specs=[anywhere],
        out_specs=anywhere,
        scratch_shapes=[
            pltpu.SemaphoreType.DMA((n,)),
            pltpu.SemaphoreType.DMA((n,)),
            pltpu.SemaphoreType.DMA((n * ny,)),
            pltpu.SemaphoreType.DMA((n * ny,)),
            pltpu.SemaphoreType.DMA((n * ny,)),
            pltpu.SemaphoreType.DMA((n * ny,)),
            pltpu.SemaphoreType.DMA(()),
        ],
        compiler_params=pltpu.CompilerParams(collective_id=1, has_side_effects=True),
    )(attended)


def push(src, dst, send, recv, peer):
    copy = pltpu.make_async_remote_copy(
        src_ref=src, dst_ref=dst, send_sem=send, recv_sem=recv, device_id=peer, device_id_type=MESH
    )
    copy.start()
    return copy


def lines(me, nz):
    z, x = me // 2, lax.rem(me, 2)
    along = [{"seq": lax.rem(z + k, nz) * 2 + x} for k in range(1, nz)]
    return z, x, along, {"seq": z * 2 + 1 - x}


def ring_device(pos, n):
    half = pos // (n // 2)
    return (1 - half) * pos * 2 + half * ((n - 1 - pos) * 2 + 1)


def rows_kernel(n, ne, cap, width, r_ref, o_ref, e_send, e_recv, s_send, s_recv, own):
    me = lax.axis_index("seq")
    place = lax.axis_index("exp")
    z, x = me // 2, lax.rem(me, 2)
    pos = (1 - x) * z + x * (n - 1 - z)
    ways = (1, n - 1)
    nexts = [{"seq": ring_device(lax.rem(pos + way, n), n)} for way in ways]
    others = [{"exp": lax.rem(place + i, ne)} for i in range(1, ne)]
    greet(others + nexts)

    def piece(seq_at, exp_at):
        return o_ref.at[cut(seq_at * cap, cap), cut(exp_at * width, width)]

    local = pltpu.make_async_copy(r_ref.at[cut(place * cap, cap), :], piece(me, place), own)
    local.start()
    first = []
    for i in range(1, ne):
        src = r_ref.at[cut(lax.rem(place + i, ne) * cap, cap), :]
        first.append(push(src, piece(me, place), e_send.at[i], e_recv.at[i], others[i - 1]))
    hops = {}
    for t in range(n // 2):
        for i in range(ne):
            if t == 0:
                local.wait() if i == 0 else first[i - 1].wait_recv()
            for d in range(2):
                if t:
                    hops[i, d, t - 1].wait_recv()
                if t == n // 2 - 1 and i % 2 != d:
                    continue
                seq_at = ring_device(lax.rem(pos + n + t * (ways[1 - d]), n), n)
                part = piece(seq_at, lax.rem(place + ne - i, ne))
                at = (i * 2 + d) * (n // 2) + t
                hops[i, d, t] = push(part, part, s_send.at[at], s_recv.at[at], nexts[d])
    for i in range(ne):
        hops[i, i % 2, n // 2 - 1].wait_recv()
    for copy in first + list(hops.values()):
        copy.wait_send()


def share_rows(rows, n, ne):
    cap, width = rows.shape[0] // ne, rows.shape[1]
    anywhere = pl.BlockSpec(memory_space=pl.ANY)
    return pl.pallas_call(
        functools.partial(rows_kernel, n, ne, cap, width),
        out_shape=jax.ShapeDtypeStruct((n * cap, ne * width), rows.dtype),
        in_specs=[anywhere],
        out_specs=anywhere,
        scratch_shapes=[pltpu.SemaphoreType.DMA((ne,))] * 2
        + [pltpu.SemaphoreType.DMA((ne * n,))] * 2
        + [pltpu.SemaphoreType.DMA(())],
        compiler_params=pltpu.CompilerParams(collective_id=2, has_side_effects=True),
    )(rows)


def sums_kernel(
    nz, ne, cap, p_ref, g_ref, o_ref, x_buf, s_buf, z_buf, total, w_buf,
    x_send, x_recv, z_send, z_recv, e_send, e_recv, own,
):
    me = lax.axis_index("seq")
    z, x, along, partner = lines(me, nz)
    place = lax.axis_index("exp")
    others = [{"exp": lax.rem(place + i, ne)} for i in range(1, ne)]
    greet(along + [partner] + others)

    def rows_of(k, side):
        return cut((lax.rem(z + k, nz) * 2 + side) * cap, cap)

    order = list(range(1, nz)) + [0]
    pairs = {}
    for k in order:
        pairs[k] = push(p_ref.at[rows_of(k, 1 - x), :], x_buf.at[k], x_send.at[k], x_recv.at[k], partner)
    sent = []
    for k in order:
        pairs[k].wait_recv()
        both = p_ref[rows_of(k, x), :].astype(jnp.float32) + x_buf[k].astype(jnp.float32)
        if k:
            s_buf[k] = both.astype(jnp.bfloat16)
            sent.append(push(s_buf.at[k], z_buf.at[k], z_send.at[k], z_recv.at[k], along[k - 1]))
        else:
            total[...] = both
    for k in range(1, nz):
        sent[k - 1].wait_recv()
        total[...] += z_buf[k].astype(jnp.float32)
    w_buf[...] = (g_ref[...] * total[...]).astype(jnp.bfloat16)
    width = w_buf.shape[1] // ne
    mine = o_ref.at[cut(place * cap, cap), :]
    local = pltpu.make_async_copy(w_buf.at[:, cut(place * width, width)], mine, own)
    local.start()
    spread = []
    for i in range(1, ne):
        src = w_buf.at[:, cut(lax.rem(place + i, ne) * width, width)]
        spread.append(push(src, mine, e_send.at[i], e_recv.at[i], others[i - 1]))
    local.wait()
    for copy in spread:
        copy.wait_recv()
    for copy in list(pairs.values()) + sent + spread:
        copy.wait_send()


def sum_rows(partial, gate, n, ne):
    cap, width = partial.shape[0] // n, partial.shape[1]
    nz = n // 2
    slots = pltpu.VMEM((nz, cap, width), jnp.bfloat16)
    return pl.pallas_call(
        functools.partial(sums_kernel, nz, ne, cap),
        out_shape=jax.ShapeDtypeStruct((ne * cap, width // ne), jnp.bfloat16),
        in_specs=[pl.BlockSpec(memory_space=pltpu.VMEM)] * 2,
        out_specs=pl.BlockSpec(memory_space=pl.ANY),
        scratch_shapes=[slots, slots, slots]
        + [pltpu.VMEM((cap, width), jnp.float32), pltpu.VMEM((cap, width), jnp.bfloat16)]
        + [pltpu.SemaphoreType.DMA((nz,))] * 4
        + [pltpu.SemaphoreType.DMA((ne,))] * 2
        + [pltpu.SemaphoreType.DMA(())],
        compiler_params=pltpu.CompilerParams(collective_id=3, has_side_effects=True),
    )(partial, gate)


def experts_kernel(
    n, ne, cap, hid_ref, pick_ref, gain_ref, router_ref, wg_ref, wu_ref, wd_ref, o_ref, place_ref,
    wg, wu, wd, r_buf, rows, gains, gate_sum, up_sum, mine, p_buf, x_buf, s_buf, z_buf, w_buf,
    w_sem, e_send, e_recv, n_send, n_recv, s_send, s_recv, x_send, x_recv, z_send, z_recv,
    t_send, t_recv, own,
):
    me = lax.axis_index("seq")
    place = lax.axis_index("exp")
    nz, z, x = n // 2, me // 2, lax.rem(me, 2)
    loads = [
        pltpu.make_async_copy(src, dst, w_sem.at[t])
        for t, (src, dst) in enumerate(((wg_ref, wg), (wu_ref, wu), (wd_ref, wd)))
    ]
    for copy in loads:
        copy.start()
    pos = (1 - x) * z + x * (n - 1 - z)
    ways = (1, n - 1)
    nexts = [{"seq": ring_device(lax.rem(pos + way, n), n)} for way in ways]
    partner = {"seq": z * 2 + 1 - x}
    along = [{"seq": lax.rem(z + k, nz) * 2 + x} for k in range(1, nz)]
    others = [{"exp": lax.rem(place + i, ne)} for i in range(1, ne)]
    flat_at = me * ne + place
    everyone = n * ne

    barrier = pltpu.get_barrier_semaphore()

    def hello(i, carry):
        at = lax.rem(flat_at + i, everyone)
        pl.semaphore_signal(
            barrier, inc=1, device_id={"seq": at // ne, "exp": lax.rem(at, ne)}, device_id_type=MESH
        )
        return carry

    lax.fori_loop(1, everyone, hello, 0)
    tokens, count = hid_ref.shape[0], pick_ref.shape[1]

    def counted(shape, axis):
        return lax.broadcasted_iota(jnp.int32, shape, axis)

    def upright(row):
        same = counted((count, count), 0) == counted((count, count), 1)
        return jnp.sum(jnp.where(same, row, 0), axis=1, keepdims=True)

    def chosen(seen):
        return jnp.where(seen, 1.0, 0.0).astype(jnp.bfloat16)

    def crossed(a, b):
        return lax.dot_general(a, b, (((0,), (0,)), ((), ())), preferred_element_type=jnp.float32)

    for e in range(ne):
        local_at = upright(pick_ref[e : e + 1, :]) - me * tokens
        before = jnp.sum((local_at < 0).astype(jnp.int32), axis=0, keepdims=True)
        turns = chosen(counted((count, cap), 0) - before == counted((count, cap), 1))
        hits = chosen(local_at == counted((count, tokens), 1))
        place_ref[e * cap : (e + 1) * cap, :] = crossed(turns, hits).astype(jnp.bfloat16)
    whole_at = upright(pick_ref[pl.ds(place, 1), :])
    slot = counted((1, n * cap), 1)
    begin = (slot // cap) * tokens
    before = jnp.sum((whole_at < begin).astype(jnp.int32), axis=0, keepdims=True)
    pack = chosen(
        (whole_at >= begin)
        & (whole_at < begin + tokens)
        & (counted((count, n * cap), 0) - before == lax.rem(slot, cap))
    )
    r_buf[...] = jnp.dot(place_ref[...], hid_ref[...], preferred_element_type=jnp.float32).astype(jnp.bfloat16)
    width = r_buf.shape[1]
    pl.semaphore_wait(barrier, everyone - 1)

    def piece(seq_at, exp_at):
        return rows.at[cut(seq_at * cap, cap), cut(exp_at * width, width)]

    def kind(e):
        return (2 * e) // ne

    local = pltpu.make_async_copy(r_buf.at[cut(place * cap, cap), :], piece(me, place), own.at[0])
    local.start()
    own_gain = pltpu.make_async_copy(
        gain_ref.at[pl.ds(kind(place), 1), :], gains.at[:, cut(place * width, width)], own.at[1]
    )
    own_gain.start()
    first = []
    scales = []
    for i in range(1, ne):
        to = lax.rem(place + i, ne)
        first.append(
            push(r_buf.at[cut(to * cap, cap), :], piece(me, place), e_send.at[i], e_recv.at[i], others[i - 1])
        )
    for i in range(1, ne):
        to = lax.rem(place + i, ne)
        scales.append(
            push(
                gain_ref.at[pl.ds(kind(to), 1), :], gains.at[:, cut(place * width, width)],
                n_send.at[i], n_recv.at[i], others[i - 1],
            )
        )
    hops = {}
    last = n // 2 - 1

    def turn_ring(slices, t):
        for i in slices:
            if t == 0:
                local.wait() if i == 0 else first[i - 1].wait_recv()
            for d in range(2):
                if t:
                    hops[i, d, t - 1].wait_recv()
                if t == last and i % 2 != d:
                    continue
                seq_at = ring_device(lax.rem(pos + n + t * (ways[1 - d]), n), n)
                part = piece(seq_at, lax.rem(place + ne - i, ne))
                at = (i * 2 + d) * (n // 2) + t
                hops[i, d, t] = push(part, part, s_send.at[at], s_recv.at[at], nexts[d])

    def finish_ring(slices):
        for i in slices:
            hops[i, i % 2, last].wait_recv()

    depth = ne * width
    block = depth // n
    per = n // ne
    gate_sum[...] = jnp.zeros_like(gate_sum)
    up_sum[...] = jnp.zeros_like(up_sum)
    state = [jnp.zeros((count, 1), jnp.float32), jnp.zeros((count, HD), jnp.float32)]

    def expand(i, sub):
        origin = lax.rem(place + ne - i, ne) * width + sub * block
        at = cut(origin, block)
        packed = jnp.dot(pack, rows[:, at], preferred_element_type=jnp.float32)
        state[0] += jnp.sum(packed * packed, axis=1, keepdims=True)
        scaled = packed * gains[:, at]
        scored = scaled * router_ref[:, at].astype(jnp.float32)
        for r in range(block // HD):
            state[1] += scored[:, r * HD : (r + 1) * HD]
        part = scaled.astype(jnp.bfloat16)
        gate_sum[...] += jnp.dot(part, wg[at, :], preferred_element_type=jnp.float32)
        up_sum[...] += jnp.dot(part, wu[at, :], preferred_element_type=jnp.float32)

    early, late = range(ne // 2), range(ne // 2, ne)
    for t in range(n // 2):
        turn_ring(early, t)
    turn_ring(late, 0)
    own_gain.wait()
    for copy in scales:
        copy.wait_recv()
    finish_ring(early)
    loads[0].wait()
    loads[1].wait()
    for t in range(n // 2):
        if t:
            turn_ring(late, t)
        expand(t // per, t % per)
    finish_ring(late)
    for t in range(n // 2):
        expand(ne // 2 + t // per, t % per)
    inverse = lax.rsqrt(state[0] / depth + 1e-05)
    gate = jax.nn.sigmoid(inverse * jnp.sum(state[1], axis=1, keepdims=True))
    inner = (jax.nn.silu(inverse * gate_sum[...]) * (inverse * up_sum[...])).astype(jnp.bfloat16)
    loads[2].wait()

    def partial(k, side):
        at = lax.rem(z + k, nz) * 2 + side
        return jnp.dot(inner, wd[:, cut(at * block, block)], preferred_element_type=jnp.float32)

    order = list(range(1, nz)) + [0]
    pairs = {}
    for k in order:
        p_buf[k] = partial(k, 1 - x).astype(jnp.bfloat16)
        pairs[k] = push(p_buf.at[k], x_buf.at[k], x_send.at[k], x_recv.at[k], partner)
    for k in order:
        mine[k] = partial(k, x)
    sent = []
    for k in order:
        pairs[k].wait_recv()
        if k:
            s_buf[k] = (mine[k] + x_buf[k].astype(jnp.float32)).astype(jnp.bfloat16)
            sent.append(push(s_buf.at[k], z_buf.at[k], z_send.at[k], z_recv.at[k], along[k - 1]))
    total = mine[0] + x_buf[0].astype(jnp.float32)
    for k in range(1, nz):
        sent[k - 1].wait_recv()
        total += z_buf[k].astype(jnp.float32)
    weighted = (gate * total).astype(jnp.bfloat16)
    w_buf[...] = crossed(pack, weighted).astype(jnp.bfloat16)

    target = me // per
    turn = lax.rem(me, per)

    def deliver(i):
        to = lax.rem(me + i, n)
        at = turn * ne + place
        return pltpu.make_async_remote_copy(
            src_ref=w_buf.at[cut(to * cap, cap), :],
            dst_ref=o_ref.at[cut(place * cap, cap), cut(turn * block, block)],
            send_sem=t_send.at[i], recv_sem=t_recv.at[at],
            device_id={"seq": to, "exp": target}, device_id_type=MESH,
        )

    home = pltpu.make_async_copy(
        w_buf.at[cut(me * cap, cap), :], o_ref.at[cut(place * cap, cap), cut(turn * block, block)], own.at[2]
    )
    stays = target == place
    for i in range(1, n):
        deliver(i).start()

    @pl.when(stays)
    def _():
        home.start()

    @pl.when(jnp.logical_not(stays))
    def _():
        deliver(0).start()

    for k in range(per):
        for e in range(ne):
            arrival = pltpu.make_async_remote_copy(
                src_ref=w_buf.at[cut(me * cap, cap), :],
                dst_ref=o_ref.at[e * cap : (e + 1) * cap, k * block : (k + 1) * block],
                send_sem=t_send.at[0], recv_sem=t_recv.at[k * ne + e],
                device_id=partner, device_id_type=MESH,
            )

            @pl.when(jnp.logical_not(stays & (turn == k) & (place == e)))
            def _():
                arrival.wait_recv()

    @pl.when(stays)
    def _():
        home.wait()

    @pl.when(jnp.logical_not(stays))
    def _():
        deliver(0).wait_send()

    for i in range(1, n):
        deliver(i).wait_send()
    for copy in first + scales + list(hops.values()) + list(pairs.values()) + sent:
        copy.wait_send()


def run_experts(hidden_state, picks, norm_gain, router, w_gate, w_up, w_down, n, ne, cap):
    tokens, width = hidden_state.shape
    count, slots = picks.shape[1], n * cap
    depth, hidden = w_gate.shape
    nz, block = n // 2, depth // n
    bf, f32 = jnp.bfloat16, jnp.float32
    inside = pl.BlockSpec(memory_space=pltpu.VMEM)
    outside = pl.BlockSpec(memory_space=pltpu.HBM)
    slab = pltpu.VMEM((nz, count, block), bf)
    sems = lambda size: pltpu.SemaphoreType.DMA((size,))
    return pl.pallas_call(
        functools.partial(experts_kernel, n, ne, cap),
        out_shape=(
            jax.ShapeDtypeStruct((ne * cap, width), bf),
            jax.ShapeDtypeStruct((ne * cap, tokens), bf),
        ),
        in_specs=[inside] * 4 + [outside] * 3,
        out_specs=(outside, inside),
        scratch_shapes=[
            pltpu.VMEM((depth, hidden), bf), pltpu.VMEM((depth, hidden), bf), pltpu.VMEM((hidden, depth), bf),
            pltpu.VMEM((ne * cap, width), bf), pltpu.VMEM((slots, depth), bf), pltpu.VMEM((1, depth), f32),
            pltpu.VMEM((count, hidden), f32), pltpu.VMEM((count, hidden), f32), pltpu.VMEM((nz, count, block), f32),
            slab, slab, slab, slab, pltpu.VMEM((slots, block), bf),
            sems(3), sems(ne), sems(ne), sems(ne), sems(ne), sems(ne * n), sems(ne * n),
            sems(nz), sems(nz), sems(nz), sems(nz), sems(n), sems(n), sems(3),
        ],
        compiler_params=pltpu.CompilerParams(
            collective_id=2, has_side_effects=True, vmem_limit_bytes=44 * 1024 * 1024
        ),
    )(hidden_state, picks, norm_gain, router.reshape(1, -1), w_gate, w_up, w_down)


def flash_kernel(block, border_ref, q_ref, k_ref, v_ref, o_ref):
    at = pl.program_id(1)
    border = border_ref[0]
    q_start = at * block
    rows = q_start + lax.broadcasted_iota(jnp.int32, (block, 1), 0)
    low = jnp.where(rows >= border, border, 0)
    steps = lax.broadcasted_iota(jnp.int32, (block, block), 1)
    q = q_ref[...]
    scale = math.log2(math.e) / math.sqrt(HD)

    def scored(j):
        start = pl.multiple_of(j * block, block)
        s = lax.dot_general(
            q, k_ref[pl.ds(start, block), :], (((1,), (1,)), ((), ())), preferred_element_type=jnp.float32
        )
        return s * scale, start

    def mix(p, start):
        return jnp.dot(
            p.astype(jnp.bfloat16), v_ref[pl.ds(start, block), :], preferred_element_type=jnp.float32
        )

    s, start = scored(at)
    s = jnp.where((steps >= low - start) & (steps <= rows - start), s, -jnp.inf)
    top = jnp.max(s, axis=1, keepdims=True)
    p = jnp.exp2(s - top)
    state = (top, jnp.sum(p, axis=1, keepdims=True), mix(p, start))

    def step(j, state):
        top, total, out = state
        s, start = scored(j)
        s = jnp.where(steps >= low - start, s, -jnp.inf)
        new_top = jnp.maximum(top, jnp.max(s, axis=1, keepdims=True))
        factor = jnp.exp2(top - new_top)
        p = jnp.exp2(s - new_top)
        return (
            new_top,
            total * factor + jnp.sum(p, axis=1, keepdims=True),
            out * factor + mix(p, start),
        )

    begin = jnp.where(q_start >= border, border // block, 0)
    top, total, out = lax.fori_loop(begin, at, step, state)
    o_ref[...] = (out / total).astype(o_ref.dtype)


def flash(queries, keys, values, border):
    rows, width = queries.shape
    block = block_rows
    return pl.pallas_call(
        functools.partial(flash_kernel, block),
        out_shape=jax.ShapeDtypeStruct((rows, width), queries.dtype),
        grid_spec=pltpu.PrefetchScalarGridSpec(
            num_scalar_prefetch=1,
            grid=(width // HD, rows // block),
            in_specs=[
                pl.BlockSpec((block, HD), lambda h, i, b: (i, h)),
                pl.BlockSpec((rows, HD), lambda h, i, b: (0, h)),
                pl.BlockSpec((rows, HD), lambda h, i, b: (0, h)),
            ],
            out_specs=pl.BlockSpec((block, HD), lambda h, i, b: (i, h)),
        ),
    )(border, queries, keys, values)


def attend_by_head(queries, keys, values, documents, n, n_exp):
    border = jnp.sum((documents == 0).astype(jnp.int32)).reshape(1)
    q_all, k_all, v_all = heads_out(queries, keys, values, n)
    return heads_back(flash(q_all, k_all, v_all, border), n, n_exp)


def chain_kernel(
    nz, ne, group, docs_ref, q_ref, k_ref, v_ref, res_ref, w_ref, o_ref,
    q0, q1, q2, kb, vb, o0, o1, c0, c1, s2, s1, p2, p1, ls2, ls1, lp2, lp1, back, att, proj, acc, res,
    load, x_send, x_recv, d0_send, d0_recv, d1_send, d1_recv, u2_send, u2_recv, g2_send, g2_recv,
    u1_send, u1_recv, g1_send, g1_recv, b_send, b_recv, y_send, y_recv, m_send, m_recv,
    r_send, r_recv, w_sem, res_sem,
):
    me = lax.axis_index("seq")
    place = lax.axis_index("exp")
    z, x = me // 2, lax.rem(me, 2)
    y, core = place // 2, lax.rem(place, 2)
    ny = ne // 2
    tokens = q_ref.shape[0]
    steps = 2 * group
    up = {"seq": lax.rem(z + 1, nz) * 2 + x}
    down = {"seq": lax.rem(z + nz - 1, nz) * 2 + x}
    partner = {"seq": z * 2 + 1 - x}
    sibling = {"exp": y * 2 + 1 - core}
    far_place = lax.rem(y + 1, ny) * 2 + core
    far = {"exp": far_place}
    has1, has2, low1 = z + 1 < nz, z + 2 < nz, z >= 1
    border = jnp.sum(
        jnp.sum((docs_ref[...] == 0).astype(jnp.int32), axis=1, keepdims=True), axis=0, keepdims=True
    )
    scale = math.log2(math.e) / math.sqrt(HD)
    greet([up, down, partner, sibling, far])

    def remote(src, dst, send, recv, peer):
        return pltpu.make_async_remote_copy(
            src_ref=src, dst_ref=dst, send_sem=send, recv_sem=recv, device_id=peer, device_id_type=MESH
        )

    def half(ref, h, side):
        return ref.at[h, cut(side * tokens, tokens), :]

    def columns(ref, h, side):
        return ref.at[:, cut((side * group + h) * HD, HD)]

    def loads(h):
        return (
            pltpu.make_async_copy(columns(q_ref, h, x), q0.at[2 * h], load.at[3 * h]),
            pltpu.make_async_copy(columns(k_ref, h, x), half(kb, h, x), load.at[3 * h + 1]),
            pltpu.make_async_copy(columns(v_ref, h, x), half(vb, h, x), load.at[3 * h + 2]),
        )

    def swaps(h):
        side = 1 - x
        return tuple(
            remote(columns(src, h, side), dst, x_send.at[3 * h + t], x_recv.at[3 * h + t], partner)
            for t, (src, dst) in enumerate(
                ((q_ref, q0.at[2 * h + 1]), (k_ref, half(kb, h, x)), (v_ref, half(vb, h, x)))
            )
        )

    def q_down(t):
        return remote(q0.at[t], q1.at[t], d0_send.at[t], d0_recv.at[t], down)

    def q_further(t):
        return remote(q1.at[t], q2.at[t], d1_send.at[t], d1_recv.at[t], down)

    def part2_up(t):
        return (
            remote(s2.at[t], p2.at[t], u2_send.at[t], u2_recv.at[t], up),
            remote(ls2.at[t], lp2.at[t], g2_send.at[t], g2_recv.at[t], up),
        )

    def part1_up(t):
        return (
            remote(s1.at[t], p1.at[t], u1_send.at[t], u1_recv.at[t], up),
            remote(ls1.at[t], lp1.at[t], g1_send.at[t], g1_recv.at[t], up),
        )

    def spot(at, t):
        return att.at[t, :, cut(at * HD, HD)]

    def give_back(t):
        return remote(back.at[t // 2], spot(place, t), b_send.at[t // 2], b_recv.at[t // 2], partner)

    def to_far(t):
        return remote(spot(place, t), spot(place, t), y_send.at[t], y_recv.at[t], far)

    def to_sibling(t):
        return remote(spot(place, t), spot(place, t), m_send.at[t], m_recv.at[t], sibling)

    def relay(t):
        return remote(spot(far_place, t), spot(far_place, t), r_send.at[t], r_recv.at[t], sibling)

    def proj_loads(t):
        side = x + (t % 2) * (1 - 2 * x)
        return [
            pltpu.make_async_copy(
                w_ref.at[cut(((e * 2 + side) * group + t // 2) * HD, HD), :],
                proj.at[t, e * HD : (e + 1) * HD, :],
                w_sem.at[t, e],
            )
            for e in range(ne)
        ]

    res_load = pltpu.make_async_copy(res_ref, res, res_sem)

    tile = HD
    tiles = tokens // tile
    span = kb.shape[1]
    key_base = z * span
    diagonal = lax.broadcasted_iota(jnp.int32, (tile, tile), 0) == lax.broadcasted_iota(
        jnp.int32, (tile, tile), 1
    )

    big = 2 * tile
    at = lax.broadcasted_iota(jnp.int32, (big, tokens), 1)

    def attend(q_of, level, t, put, blocks):
        h = t // 2
        side = x + lax.rem(t, 2) * (1 - 2 * x)
        base = ((z + level) * 2 + side) * tokens - key_base
        edge = border - key_base

        def score(r):
            rows = base + r * big + lax.broadcasted_iota(jnp.int32, (big, 1), 0)
            low = jnp.where(rows >= edge, edge, -key_base)
            out = []
            for b in range(blocks):
                s = lax.dot_general(
                    q_of[r * big : (r + 1) * big, :], kb[h, b * tokens : (b + 1) * tokens, :],
                    (((1,), (1,)), ((), ())), preferred_element_type=jnp.float32,
                )
                seen = at >= low - b * tokens
                if level == 0 and b == blocks - 1:
                    seen = seen & (at <= rows - b * tokens)
                out.append(jnp.where(seen, s, -1e30))
            return out

        later = score(0)
        for r in range(tokens // big):
            now = later
            if (r + 1) * big < tokens:
                later = score(r + 1)
            top = jnp.max(functools.reduce(jnp.maximum, now), axis=1, keepdims=True) * scale
            total = jnp.zeros((big, 1), jnp.float32)
            out = jnp.zeros((big, HD), jnp.float32)
            for b, s in enumerate(now):
                p = jnp.exp2(s * scale - top)
                total += jnp.sum(p, axis=1, keepdims=True)
                out += jnp.dot(
                    p.astype(jnp.bfloat16), vb[h, b * tokens : (b + 1) * tokens, :],
                    preferred_element_type=jnp.float32,
                )
            put(r * big, out / total, top + jnp.log2(total))

    def flat(level):
        return jnp.sum(jnp.where(diagonal, level, 0.0), axis=0, keepdims=True)

    def upright(ref, r):
        return jnp.sum(jnp.where(diagonal, ref[r : r + 1, :], 0.0), axis=1, keepdims=True)

    def joined(out, level, p_of, l_of, r):
        other = upright(l_of, r)
        top = jnp.maximum(level, other)
        mine, theirs = jnp.exp2(level - top), jnp.exp2(other - top)
        both = mine + theirs
        out = (out * mine + p_of[r * tile : (r + 1) * tile, :].astype(jnp.float32) * theirs) / both
        return out, top + jnp.log2(both)

    for h in range(group):
        for copy in swaps(h):
            copy.start()
        for copy in loads(h):
            copy.start()

    for t in range(steps):
        for copy in proj_loads(t):
            copy.start()
    res_load.start()

    def send_own(t):
        @pl.when(lax.rem(t, 2) == 0)
        def _():
            loads(t // 2)[0].wait()

        @pl.when(lax.rem(t, 2) == 1)
        def _():
            swaps(t // 2)[0].wait_recv()

        @pl.when(low1)
        def _():
            q_down(t).start()

    def forward(t):
        @pl.when(has1)
        def _():
            q_down(t).wait_recv()

            @pl.when(low1)
            def _():
                q_further(t).start()

    def spread(t):
        to_far(t).start()
        to_sibling(t).start()

    send_own(jnp.int32(0))
    send_own(jnp.int32(1))
    forward(jnp.int32(0))

    def step(i, carry):
        live = i < steps

        @pl.when(i + 2 < steps)
        def _():
            send_own(i + 2)

        @pl.when(i + 1 < steps)
        def _():
            forward(i + 1)

        @pl.when(live & (lax.rem(i, 2) == 0))
        def _():
            for copy in loads(i // 2)[1:]:
                copy.wait()
            for copy in swaps(i // 2)[1:]:
                copy.wait_recv()

        @pl.when(live & has2)
        def _():
            q_further(i).wait_recv()

            def put(at, out, level):
                s2[i, at : at + big, :] = out.astype(jnp.bfloat16)
                for r in range(big // tile):
                    row = at // tile + r
                    ls2[i, row : row + 1, :] = flat(level[r * tile : (r + 1) * tile])

            attend(q2.at[i], 2, i, put, 2)
            for copy in part2_up(i):
                copy.start()

        @pl.when(i == 1)
        def _():
            res_load.wait()
            acc[...] = res[...].astype(jnp.float32)

        t1 = i - 1

        @pl.when((t1 >= 0) & (t1 < steps) & has1)
        def _():
            def put(r, out, level):
                s1[t1, r * tile : (r + 1) * tile, :] = out.astype(jnp.bfloat16)
                ls1[t1, r : r + 1, :] = flat(level)

            @pl.when(low1)
            def _():
                for copy in part2_up(t1):
                    copy.wait_recv()
                for r in range(tiles):
                    put(r, *joined(o1[t1, r * tile : (r + 1) * tile, :], c1[t1, r * tile : (r + 1) * tile, :], p2.at[t1], lp2.at[t1], r))

            @pl.when(jnp.logical_not(low1))
            def _():
                for r in range(tiles):
                    put(r, o1[t1, r * tile : (r + 1) * tile, :], c1[t1, r * tile : (r + 1) * tile, :])

            for copy in part1_up(t1):
                copy.start()

        @pl.when(live & has1)
        def _():
            def put(at, out, level):
                o1[i, at : at + big, :] = out
                c1[i, at : at + big, :] = level

            attend(q1.at[i], 1, i, put, 2)

        t0 = i - 2

        @pl.when((t0 >= 0) & (t0 < steps))
        def _():
            def finish(put):
                @pl.when(low1)
                def _():
                    for copy in part1_up(t0):
                        copy.wait_recv()
                    for r in range(tiles):
                        out, level = joined(o0[t0, r * tile : (r + 1) * tile, :], c0[t0, r * tile : (r + 1) * tile, :], p1.at[t0], lp1.at[t0], r)
                        put(r, out)

                @pl.when(jnp.logical_not(low1))
                def _():
                    for r in range(tiles):
                        put(r, o0[t0, r * tile : (r + 1) * tile, :])

            @pl.when(lax.rem(t0, 2) == 0)
            def _():
                def put(r, out):
                    att[t0, r * tile : (r + 1) * tile, cut(place * HD, HD)] = out.astype(jnp.bfloat16)

                finish(put)
                spread(t0)

            @pl.when(lax.rem(t0, 2) == 1)
            def _():
                def put(r, out):
                    back[t0 // 2, r * tile : (r + 1) * tile, :] = out.astype(jnp.bfloat16)

                finish(put)
                give_back(t0).start()

        @pl.when(live)
        def _():
            def put(at, out, level):
                o0[i, at : at + big, :] = out
                c0[i, at : at + big, :] = level

            first_half = lax.rem(i, 2) == x

            @pl.when(first_half)
            def _():
                attend(q0.at[i], 0, i, put, 1)

            @pl.when(jnp.logical_not(first_half))
            def _():
                attend(q0.at[i], 0, i, put, 2)

        t4 = i - 3

        @pl.when((t4 >= 0) & (t4 < steps) & (lax.rem(t4, 2) == 1))
        def _():
            give_back(t4).wait_recv()
            spread(t4)

        t5 = i - 5

        @pl.when((t5 >= 0) & (t5 < steps))
        def _():
            to_far(t5).wait_recv()
            relay(t5).start()

        t6 = i - 6

        @pl.when((t6 >= 0) & (t6 < steps))
        def _():
            to_sibling(t6).wait_recv()
            relay(t6).wait_recv()
            for copy in proj_loads(t6):
                copy.wait()

            acc[...] += jnp.dot(att[t6], proj[t6], preferred_element_type=jnp.float32)

        return carry

    lax.fori_loop(0, steps + 6, step, 0)
    o_ref[...] = acc[...].astype(o_ref.dtype)


    def settle(t, carry):
        to_far(t).wait_send()
        to_sibling(t).wait_send()
        relay(t).wait_send()

        @pl.when(low1)
        def _():
            q_down(t).wait_send()

            @pl.when(has1)
            def _():
                q_further(t).wait_send()

        @pl.when(has1)
        def _():
            for copy in part1_up(t):
                copy.wait_send()

        @pl.when(has2)
        def _():
            for copy in part2_up(t):
                copy.wait_send()

        @pl.when(lax.rem(t, 2) == 1)
        def _():
            give_back(t).wait_send()
            for copy in swaps(t // 2):
                copy.wait_send()

        return carry

    lax.fori_loop(0, steps, settle, 0)


def attend_by_chain(queries, keys, values, documents, residual, out_proj, n, n_exp):
    tokens, width = queries.shape
    group = width // HD // 2
    steps = 2 * group
    nz = n // 2
    features = out_proj.shape[1]
    outside = pl.BlockSpec(memory_space=pltpu.HBM)
    inside = pl.BlockSpec(memory_space=pltpu.VMEM)
    bf, f32 = jnp.bfloat16, jnp.float32
    chunks = pltpu.VMEM((steps, tokens, HD), bf)
    side = pltpu.VMEM((group, 2 * tokens, HD), bf)
    wide = pltpu.VMEM((steps, tokens, HD), f32)
    thin = pltpu.VMEM((steps, tokens, 1), f32)
    flats = pltpu.VMEM((steps, max(8, tokens // HD), HD), f32)
    sems = lambda count: pltpu.SemaphoreType.DMA((count,))
    return pl.pallas_call(
        functools.partial(chain_kernel, nz, n_exp, group),
        out_shape=jax.ShapeDtypeStruct((tokens, features), queries.dtype),
        in_specs=[inside] + [outside] * 5,
        out_specs=inside,
        scratch_shapes=[chunks] * 3 + [side] * 2 + [wide] * 2 + [thin] * 2 + [chunks] * 4 + [flats] * 4
        + [pltpu.VMEM((group, tokens, HD), bf), pltpu.VMEM((steps, tokens, n_exp * HD), bf)]
        + [pltpu.VMEM((steps, n_exp * HD, features), bf), pltpu.VMEM((tokens, features), f32)]
        + [pltpu.VMEM((tokens, features), bf)]
        + [sems(3 * group)] * 3 + [sems(steps)] * 12 + [sems(group)] * 2 + [sems(steps)] * 6
        + [pltpu.SemaphoreType.DMA((steps, n_exp)), pltpu.SemaphoreType.DMA(())],
        compiler_params=pltpu.CompilerParams(
            collective_id=0, has_side_effects=True, vmem_limit_bytes=54 * 1024 * 1024
        ),
    )(documents.reshape(-1, HD), queries, keys, values, residual, out_proj)


def attend_by_token(queries, keys, values, documents):
    tokens = queries.shape[0]
    heads_here = queries.shape[1] // HD
    seq_pos = lax.axis_index("seq")
    start_row = seq_pos * tokens
    query_pos = start_row + jnp.arange(tokens, dtype=jnp.int32)
    query_doc = lax.dynamic_slice_in_dim(documents, start_row, tokens, 0)
    query_heads = queries.reshape(tokens, heads_here, HD)
    score_scale = 1.0 / math.sqrt(HD)

    def attend(state, key_rows, value_rows, key_start):
        row_count = key_rows.shape[0]
        key_pos = key_start + jnp.arange(row_count, dtype=jnp.int32)
        key_doc = lax.dynamic_slice_in_dim(documents, key_start, row_count, 0)
        scores = (
            jnp.einsum(
                "qhd,khd->qhk",
                query_heads,
                key_rows.reshape(row_count, heads_here, HD),
                preferred_element_type=jnp.float32,
            )
            * score_scale
        )
        allowed = (key_pos[None, :] <= query_pos[:, None]) & (
            key_doc[None, :] == query_doc[:, None]
        )
        scores = jnp.where(allowed[:, None, :], scores, -jnp.inf)
        running_max, running_sum, running_out = state
        new_max = jnp.maximum(running_max, jnp.max(scores, axis=2))
        factor = jnp.exp(running_max - new_max)
        weights = jnp.exp(scores - new_max[:, :, None])
        running_sum = running_sum * factor + jnp.sum(weights, axis=2)
        running_out = running_out * factor[:, :, None] + jnp.einsum(
            "qhk,khd->qhd",
            weights.astype(jnp.bfloat16),
            value_rows.reshape(row_count, heads_here, HD),
            preferred_element_type=jnp.float32,
        )
        return (new_max, running_sum, running_out)

    def visit_block(state, key_rows, value_rows, key_start):
        row_count = key_rows.shape[0]
        last_doc = lax.dynamic_index_in_dim(documents, key_start + row_count - 1, 0, keepdims=False)
        beyond = (key_start > query_pos[tokens - 1]) | (last_doc < query_doc[0])
        return lax.cond(
            beyond,
            lambda inner_state: inner_state,
            lambda inner_state: attend(inner_state, key_rows, value_rows, key_start),
            state,
        )

    initial = (
        jnp.full((tokens, heads_here), -1e30, jnp.float32),
        jnp.zeros((tokens, heads_here), jnp.float32),
        jnp.zeros((tokens, heads_here, HD), jnp.float32),
    )
    state = initial
    key_piece = lax.all_gather(keys, "seq", axis=0, tiled=True)
    value_piece = lax.all_gather(values, "seq", axis=0, tiled=True)
    row_count = key_piece.shape[0]
    blocks = row_count // block_rows
    key_stack = key_piece.reshape(blocks, block_rows, key_piece.shape[1])
    value_stack = value_piece.reshape(blocks, block_rows, value_piece.shape[1])

    def scan_step(inner_state, block_item):
        block_index, key_rows, value_rows = block_item
        return (visit_block(inner_state, key_rows, value_rows, block_index * block_rows), None)

    state, unused = lax.scan(
        scan_step, state, (jnp.arange(blocks, dtype=jnp.int32), key_stack, value_stack)
    )
    running_max, running_sum, running_out = state
    attended = (
        (running_out / running_sum[:, :, None])
        .reshape(tokens, heads_here * HD)
        .astype(jnp.bfloat16)
    )
    return lax.all_gather(attended, "exp", axis=1, tiled=True)


def shards(
    residual,
    queries,
    keys,
    values,
    documents,
    out_proj,
    modality,
    norm_gain,
    picks,
    router,
    w_gate,
    w_up,
    w_down,
):
    tokens = queries.shape[0]
    seq_pos = lax.axis_index("seq")
    start_row = seq_pos * tokens
    n_seq, n_exp = lax.axis_size("seq"), lax.axis_size("exp")
    if (queries.shape[1] // HD) % n_seq == 0 and n_exp == 4:
        hidden_state = attend_by_chain(
            queries, keys, values, documents, residual, out_proj, n_seq, n_exp
        )
    else:
        attended = attend_by_token(queries, keys, values, documents)
        mixed = jnp.dot(attended, out_proj, preferred_element_type=jnp.float32)
        hidden_state = (residual.astype(jnp.float32) + mixed).astype(jnp.bfloat16)
    returned, placing = run_experts(
        hidden_state, picks, norm_gain, router, w_gate[0], w_up[0], w_down[0], n_seq, n_exp, tokens // 32
    )
    expert_add = lax.dot_general(
        placing, returned, (((0,), (0,)), ((), ())), preferred_element_type=jnp.float32
    )
    return (hidden_state.astype(jnp.float32) + expert_add).astype(jnp.bfloat16)


def solution(mesh):
    return jax.shard_map(
        shards,
        mesh=mesh,
        in_specs=(
            P("seq", "exp"),
            P("seq", "exp"),
            P("seq", "exp"),
            P("seq", "exp"),
            P(),
            P(None, "exp"),
            P("seq"),
            P(None, "exp"),
            P(),
            P(None, "exp"),
            P("exp", None, "seq"),
            P("exp", None, "seq"),
            P("exp", "seq", None),
        ),
        out_specs=P("seq", "exp"),
        check_vma=False,
    )
```

```python
import functools
import math

import jax
import jax.numpy as jnp
from jax import lax
from jax.experimental import pallas as pl
from jax.experimental.pallas import tpu as pltpu
from jax.sharding import PartitionSpec as P

D = 8192
HD = 128


block_rows = 512


MESH = pl.DeviceIdType.MESH


def greet(peers):
    barrier = pltpu.get_barrier_semaphore()
    for peer in peers:
        pl.semaphore_signal(barrier, inc=1, device_id=peer, device_id_type=MESH)
    pl.semaphore_wait(barrier, len(peers))


def cut(start, size):
    return pl.ds(pl.multiple_of(start, size), size)


def heads_out_kernel(n, width, q_ref, k_ref, v_ref, qo, ko, vo, send, recv, own):
    me = lax.axis_index("seq")
    tokens = q_ref.shape[0]
    greet([{"seq": lax.rem(me + i, n)} for i in range(1, n)])
    pairs = ((k_ref, ko), (v_ref, vo), (q_ref, qo))
    copies = []
    for i in range(1, n):
        to = lax.rem(me + i, n)
        for t, (src, dst) in enumerate(pairs):
            copies.append(
                pltpu.make_async_remote_copy(
                    src_ref=src.at[:, cut(to * width, width)],
                    dst_ref=dst.at[cut(me * tokens, tokens), :],
                    send_sem=send.at[t * n + i],
                    recv_sem=recv.at[t * n + i],
                    device_id={"seq": to},
                    device_id_type=MESH,
                )
            )
            copies[-1].start()
    for t, (src, dst) in enumerate(pairs):
        copies.append(
            pltpu.make_async_copy(
                src.at[:, cut(me * width, width)], dst.at[cut(me * tokens, tokens), :], own.at[t]
            )
        )
        copies[-1].start()
    for copy in copies:
        copy.wait()


def heads_out(queries, keys, values, n):
    tokens, columns = queries.shape
    width = columns // n
    whole = jax.ShapeDtypeStruct((n * tokens, width), queries.dtype)
    anywhere = pl.BlockSpec(memory_space=pl.ANY)
    return pl.pallas_call(
        functools.partial(heads_out_kernel, n, width),
        out_shape=(whole, whole, whole),
        in_specs=[anywhere] * 3,
        out_specs=(anywhere,) * 3,
        scratch_shapes=[
            pltpu.SemaphoreType.DMA((3 * n,)),
            pltpu.SemaphoreType.DMA((3 * n,)),
            pltpu.SemaphoreType.DMA((3,)),
        ],
        compiler_params=pltpu.CompilerParams(collective_id=0, has_side_effects=True),
    )(queries, keys, values)


def heads_back_kernel(n, ny, width, a_ref, o_ref, s_send, s_recv, y_send, y_recv, c_send, c_recv, own):
    me = lax.axis_index("seq")
    place = lax.axis_index("exp")
    y, core = place // 2, lax.rem(place, 2)
    sibling = {"exp": y * 2 + 1 - core}
    across = [{"exp": lax.rem(y + k, ny) * 2 + core} for k in range(1, ny)]
    tokens = o_ref.shape[0]
    span = n * width
    greet([{"seq": lax.rem(me + i, n)} for i in range(1, n)] + across + [sibling])

    def piece(exp_at, seq_at):
        return o_ref.at[:, cut(exp_at * span + seq_at * width, width)]

    local = pltpu.make_async_copy(a_ref.at[cut(me * tokens, tokens), :], piece(place, me), own)
    local.start()
    first = []
    for i in range(1, n):
        to = lax.rem(me + i, n)
        first.append(
            push(
                a_ref.at[cut(to * tokens, tokens), :],
                piece(place, me),
                s_send.at[i],
                s_recv.at[i],
                {"seq": to},
            )
        )
    second = []
    third = []
    for i in range(n):
        if i == 0:
            local.wait()
        else:
            first[i - 1].wait_recv()
        part = piece(place, lax.rem(me + n - i, n))
        for k in range(1, ny):
            at = i * ny + k
            second.append(push(part, part, y_send.at[at], y_recv.at[at], across[k - 1]))
        third.append(push(part, part, c_send.at[i * ny], c_recv.at[i * ny], sibling))
    for i in range(n):
        for k in range(1, ny):
            second[i * (ny - 1) + k - 1].wait_recv()
            at = i * ny + k
            part = piece(lax.rem(y + ny - k, ny) * 2 + core, lax.rem(me + n - i, n))
            third.append(push(part, part, c_send.at[at], c_recv.at[at], sibling))
    for copy in third:
        copy.wait_recv()
    for copy in first + second + third:
        copy.wait_send()


def heads_back(attended, n, n_exp):
    rows, width = attended.shape
    ny = n_exp // 2
    anywhere = pl.BlockSpec(memory_space=pl.ANY)
    return pl.pallas_call(
        functools.partial(heads_back_kernel, n, ny, width),
        out_shape=jax.ShapeDtypeStruct((rows // n, n_exp * n * width), attended.dtype),
        in_specs=[anywhere],
        out_specs=anywhere,
        scratch_shapes=[
            pltpu.SemaphoreType.DMA((n,)),
            pltpu.SemaphoreType.DMA((n,)),
            pltpu.SemaphoreType.DMA((n * ny,)),
            pltpu.SemaphoreType.DMA((n * ny,)),
            pltpu.SemaphoreType.DMA((n * ny,)),
            pltpu.SemaphoreType.DMA((n * ny,)),
            pltpu.SemaphoreType.DMA(()),
        ],
        compiler_params=pltpu.CompilerParams(collective_id=1, has_side_effects=True),
    )(attended)


def push(src, dst, send, recv, peer):
    copy = pltpu.make_async_remote_copy(
        src_ref=src, dst_ref=dst, send_sem=send, recv_sem=recv, device_id=peer, device_id_type=MESH
    )
    copy.start()
    return copy


def lines(me, nz):
    z, x = me // 2, lax.rem(me, 2)
    along = [{"seq": lax.rem(z + k, nz) * 2 + x} for k in range(1, nz)]
    return z, x, along, {"seq": z * 2 + 1 - x}


def ring_device(pos, n):
    half = pos // (n // 2)
    return (1 - half) * pos * 2 + half * ((n - 1 - pos) * 2 + 1)


def rows_kernel(n, ne, cap, width, r_ref, o_ref, e_send, e_recv, s_send, s_recv, own):
    me = lax.axis_index("seq")
    place = lax.axis_index("exp")
    z, x = me // 2, lax.rem(me, 2)
    pos = (1 - x) * z + x * (n - 1 - z)
    ways = (1, n - 1)
    nexts = [{"seq": ring_device(lax.rem(pos + way, n), n)} for way in ways]
    others = [{"exp": lax.rem(place + i, ne)} for i in range(1, ne)]
    greet(others + nexts)

    def piece(seq_at, exp_at):
        return o_ref.at[cut(seq_at * cap, cap), cut(exp_at * width, width)]

    local = pltpu.make_async_copy(r_ref.at[cut(place * cap, cap), :], piece(me, place), own)
    local.start()
    first = []
    for i in range(1, ne):
        src = r_ref.at[cut(lax.rem(place + i, ne) * cap, cap), :]
        first.append(push(src, piece(me, place), e_send.at[i], e_recv.at[i], others[i - 1]))
    hops = {}
    for t in range(n // 2):
        for i in range(ne):
            if t == 0:
                local.wait() if i == 0 else first[i - 1].wait_recv()
            for d in range(2):
                if t:
                    hops[i, d, t - 1].wait_recv()
                if t == n // 2 - 1 and i % 2 != d:
                    continue
                seq_at = ring_device(lax.rem(pos + n + t * (ways[1 - d]), n), n)
                part = piece(seq_at, lax.rem(place + ne - i, ne))
                at = (i * 2 + d) * (n // 2) + t
                hops[i, d, t] = push(part, part, s_send.at[at], s_recv.at[at], nexts[d])
    for i in range(ne):
        hops[i, i % 2, n // 2 - 1].wait_recv()
    for copy in first + list(hops.values()):
        copy.wait_send()


def share_rows(rows, n, ne):
    cap, width = rows.shape[0] // ne, rows.shape[1]
    anywhere = pl.BlockSpec(memory_space=pl.ANY)
    return pl.pallas_call(
        functools.partial(rows_kernel, n, ne, cap, width),
        out_shape=jax.ShapeDtypeStruct((n * cap, ne * width), rows.dtype),
        in_specs=[anywhere],
        out_specs=anywhere,
        scratch_shapes=[pltpu.SemaphoreType.DMA((ne,))] * 2
        + [pltpu.SemaphoreType.DMA((ne * n,))] * 2
        + [pltpu.SemaphoreType.DMA(())],
        compiler_params=pltpu.CompilerParams(collective_id=2, has_side_effects=True),
    )(rows)


def sums_kernel(
    nz, ne, cap, p_ref, g_ref, o_ref, x_buf, s_buf, z_buf, total, w_buf,
    x_send, x_recv, z_send, z_recv, e_send, e_recv, own,
):
    me = lax.axis_index("seq")
    z, x, along, partner = lines(me, nz)
    place = lax.axis_index("exp")
    others = [{"exp": lax.rem(place + i, ne)} for i in range(1, ne)]
    greet(along + [partner] + others)

    def rows_of(k, side):
        return cut((lax.rem(z + k, nz) * 2 + side) * cap, cap)

    order = list(range(1, nz)) + [0]
    pairs = {}
    for k in order:
        pairs[k] = push(p_ref.at[rows_of(k, 1 - x), :], x_buf.at[k], x_send.at[k], x_recv.at[k], partner)
    sent = []
    for k in order:
        pairs[k].wait_recv()
        both = p_ref[rows_of(k, x), :].astype(jnp.float32) + x_buf[k].astype(jnp.float32)
        if k:
            s_buf[k] = both.astype(jnp.bfloat16)
            sent.append(push(s_buf.at[k], z_buf.at[k], z_send.at[k], z_recv.at[k], along[k - 1]))
        else:
            total[...] = both
    for k in range(1, nz):
        sent[k - 1].wait_recv()
        total[...] += z_buf[k].astype(jnp.float32)
    w_buf[...] = (g_ref[...] * total[...]).astype(jnp.bfloat16)
    width = w_buf.shape[1] // ne
    mine = o_ref.at[cut(place * cap, cap), :]
    local = pltpu.make_async_copy(w_buf.at[:, cut(place * width, width)], mine, own)
    local.start()
    spread = []
    for i in range(1, ne):
        src = w_buf.at[:, cut(lax.rem(place + i, ne) * width, width)]
        spread.append(push(src, mine, e_send.at[i], e_recv.at[i], others[i - 1]))
    local.wait()
    for copy in spread:
        copy.wait_recv()
    for copy in list(pairs.values()) + sent + spread:
        copy.wait_send()


def sum_rows(partial, gate, n, ne):
    cap, width = partial.shape[0] // n, partial.shape[1]
    nz = n // 2
    slots = pltpu.VMEM((nz, cap, width), jnp.bfloat16)
    return pl.pallas_call(
        functools.partial(sums_kernel, nz, ne, cap),
        out_shape=jax.ShapeDtypeStruct((ne * cap, width // ne), jnp.bfloat16),
        in_specs=[pl.BlockSpec(memory_space=pltpu.VMEM)] * 2,
        out_specs=pl.BlockSpec(memory_space=pl.ANY),
        scratch_shapes=[slots, slots, slots]
        + [pltpu.VMEM((cap, width), jnp.float32), pltpu.VMEM((cap, width), jnp.bfloat16)]
        + [pltpu.SemaphoreType.DMA((nz,))] * 4
        + [pltpu.SemaphoreType.DMA((ne,))] * 2
        + [pltpu.SemaphoreType.DMA(())],
        compiler_params=pltpu.CompilerParams(collective_id=3, has_side_effects=True),
    )(partial, gate)


def experts_kernel(
    n, ne, cap, hid_ref, pick_ref, gain_ref, router_ref, wg_ref, wu_ref, wd_ref, o_ref, place_ref,
    wg, wu, wd, r_buf, slots, packed, gains, gate_sum, up_sum, mine, p_buf, x_buf, s_buf, z_buf, w_buf,
    w_sem, a_send, a_recv, n_send, n_recv, s_send, s_recv, x_send, x_recv, z_send, z_recv,
    t_send, t_recv, own,
):
    me = lax.axis_index("seq")
    place = lax.axis_index("exp")
    nz, z, x = n // 2, me // 2, lax.rem(me, 2)
    loads = [
        pltpu.make_async_copy(src, dst, w_sem.at[t])
        for t, (src, dst) in enumerate(((wg_ref, wg), (wu_ref, wu), (wd_ref, wd)))
    ]
    for copy in loads:
        copy.start()
    pos = (1 - x) * z + x * (n - 1 - z)
    ways = (1, n - 1)
    nexts = [{"seq": ring_device(lax.rem(pos + way, n), n)} for way in ways]
    partner = {"seq": z * 2 + 1 - x}
    along = [{"seq": lax.rem(z + k, nz) * 2 + x} for k in range(1, nz)]
    others = [{"exp": lax.rem(place + i, ne)} for i in range(1, ne)]
    flat_at = me * ne + place
    everyone = n * ne

    barrier = pltpu.get_barrier_semaphore()

    def hello(i, carry):
        at = lax.rem(flat_at + i, everyone)
        pl.semaphore_signal(
            barrier, inc=1, device_id={"seq": at // ne, "exp": lax.rem(at, ne)}, device_id_type=MESH
        )
        return carry

    lax.fori_loop(1, everyone, hello, 0)
    tokens, count = hid_ref.shape[0], pick_ref.shape[1]

    def counted(shape, axis):
        return lax.broadcasted_iota(jnp.int32, shape, axis)

    def upright(row):
        same = counted((count, count), 0) == counted((count, count), 1)
        return jnp.sum(jnp.where(same, row, 0), axis=1, keepdims=True)

    def chosen(seen):
        return jnp.where(seen, 1.0, 0.0).astype(jnp.bfloat16)

    def crossed(a, b):
        return lax.dot_general(a, b, (((0,), (0,)), ((), ())), preferred_element_type=jnp.float32)

    for e in range(ne):
        local_at = upright(pick_ref[e : e + 1, :]) - me * tokens
        before = jnp.sum((local_at < 0).astype(jnp.int32), axis=0, keepdims=True)
        turns = chosen(counted((count, cap), 0) - before == counted((count, cap), 1))
        hits = chosen(local_at == counted((count, tokens), 1))
        place_ref[e * cap : (e + 1) * cap, :] = crossed(turns, hits).astype(jnp.bfloat16)
    whole_at = upright(pick_ref[pl.ds(place, 1), :])
    slot = counted((1, n * cap), 1)
    begin = (slot // cap) * tokens
    before = jnp.sum((whole_at < begin).astype(jnp.int32), axis=0, keepdims=True)
    pack = chosen(
        (whole_at >= begin)
        & (whole_at < begin + tokens)
        & (counted((count, n * cap), 0) - before == lax.rem(slot, cap))
    )
    r_buf[...] = jnp.dot(place_ref[...], hid_ref[...], preferred_element_type=jnp.float32).astype(jnp.bfloat16)
    width = r_buf.shape[1]
    pl.semaphore_wait(barrier, everyone - 1)

    def kind(e):
        return (2 * e) // ne

    depth = ne * width
    block = depth // n
    per = n // ne
    target = me // per
    turn = lax.rem(me, per)
    stays = target == place

    sub = max(HD, width // n)
    share = width // sub
    groups = depth // (sub * n)

    def hand(k, e):
        number = place * share + k
        group = number // n
        return pltpu.make_async_remote_copy(
            src_ref=r_buf.at[e * cap : (e + 1) * cap, k * sub : (k + 1) * sub],
            dst_ref=slots.at[cut(me * cap, cap), cut(group * sub, sub)],
            send_sem=a_send.at[k * ne + e], recv_sem=a_recv.at[me * groups + group],
            device_id={"seq": lax.rem(number, n), "exp": e}, device_id_type=MESH,
        )

    def given(at, group):
        spot = slots.at[at * cap : (at + 1) * cap, group * sub : (group + 1) * sub]
        return pltpu.make_async_remote_copy(
            src_ref=spot, dst_ref=spot, send_sem=a_send.at[0], recv_sem=a_recv.at[at * groups + group],
            device_id=partner, device_id_type=MESH,
        )

    def to_self(k, e):
        return stays & (turn == k) & (place == e)

    def hand_self(k, e):
        return (lax.rem(place * share + k, n) == me) & (place == e)

    def kept(k, e):
        group = (place * share + k) // n
        return pltpu.make_async_copy(
            r_buf.at[e * cap : (e + 1) * cap, k * sub : (k + 1) * sub],
            slots.at[cut(me * cap, cap), cut(group * sub, sub)],
            own.at[0],
        )

    for k in range(share):
        for e in range(ne):
            handed, held = hand(k, e), kept(k, e)

            @pl.when(jnp.logical_not(hand_self(k, e)))
            def _():
                handed.start()

            @pl.when(hand_self(k, e))
            def _():
                held.start()

    own_gain = pltpu.make_async_copy(
        gain_ref.at[pl.ds(kind(place), 1), :], gains.at[:, cut(place * width, width)], own.at[1]
    )
    own_gain.start()
    scales = []
    for i in range(1, ne):
        to = lax.rem(place + i, ne)
        scales.append(
            push(
                gain_ref.at[pl.ds(kind(to), 1), :], gains.at[:, cut(place * width, width)],
                n_send.at[i], n_recv.at[i], others[i - 1],
            )
        )
    first_own = place * share
    for at in range(n):
        for group in range(groups):
            arrived = given(at, group)
            from_self = (me == at) & (first_own <= group * n + me) & (group * n + me < first_own + share)

            @pl.when(jnp.logical_not(from_self))
            def _():
                arrived.wait_recv()

    for k in range(share):
        for e in range(ne):
            held = kept(k, e)

            @pl.when(hand_self(k, e))
            def _():
                held.wait()

    packed[me] = jnp.dot(pack, slots[...], preferred_element_type=jnp.float32).astype(jnp.bfloat16)
    pieces = 4
    lines_at = count // pieces
    gate_sum[...] = jnp.zeros_like(gate_sum)
    up_sum[...] = jnp.zeros_like(up_sum)
    state = [jnp.zeros((count, 1), jnp.float32), jnp.zeros((count, HD), jnp.float32)]

    def expand(seq_at):
        for group in range(groups):
            at = cut((group * n + seq_at) * sub, sub)
            raw = packed[seq_at, :, group * sub : (group + 1) * sub].astype(jnp.float32)
            state[0] += jnp.sum(raw * raw, axis=1, keepdims=True)
            scaled = raw * gains[:, at]
            scored = scaled * router_ref[:, at].astype(jnp.float32)
            for r in range(sub // HD):
                state[1] += scored[:, r * HD : (r + 1) * HD]
            part = scaled.astype(jnp.bfloat16)
            gate_sum[...] += jnp.dot(part, wg[at, :], preferred_element_type=jnp.float32)
            up_sum[...] += jnp.dot(part, wu[at, :], preferred_element_type=jnp.float32)

    hops = {}
    last = n // 2 - 1
    for t in range(n // 2):
        arrived_at = [ring_device(lax.rem(pos + n + t * ways[1 - d], n), n) for d in range(2)]
        for i in range(pieces):
            for d in range(2):
                if t:
                    hops[i, d, t - 1].wait_recv()
                if t == last and i % 2 != d:
                    continue
                part = packed.at[arrived_at[d], i * lines_at : (i + 1) * lines_at, :]
                at = (i * 2 + d) * (n // 2) + t
                hops[i, d, t] = push(part, part, s_send.at[at], s_recv.at[at], nexts[d])
        if t == 0:
            own_gain.wait()
            for copy in scales:
                copy.wait_recv()
            loads[0].wait()
            loads[1].wait()
        for d in range(2 if t else 1):
            expand(arrived_at[d])
    for i in range(pieces):
        hops[i, i % 2, last].wait_recv()
    expand(ring_device(lax.rem(pos + n // 2, n), n))
    inverse = lax.rsqrt(state[0] / depth + 1e-05)
    gate = jax.nn.sigmoid(inverse * jnp.sum(state[1], axis=1, keepdims=True))
    inner = (jax.nn.silu(inverse * gate_sum[...]) * (inverse * up_sum[...])).astype(jnp.bfloat16)
    loads[2].wait()

    def partial(k, side):
        at = lax.rem(z + k, nz) * 2 + side
        return jnp.dot(inner, wd[:, cut(at * block, block)], preferred_element_type=jnp.float32)

    order = list(range(1, nz)) + [0]
    pairs = {}
    for k in order:
        p_buf[k] = partial(k, 1 - x).astype(jnp.bfloat16)
        pairs[k] = push(p_buf.at[k], x_buf.at[k], x_send.at[k], x_recv.at[k], partner)
    for k in order:
        mine[k] = partial(k, x)
    sent = []
    for k in order:
        pairs[k].wait_recv()
        if k:
            s_buf[k] = (mine[k] + x_buf[k].astype(jnp.float32)).astype(jnp.bfloat16)
            sent.append(push(s_buf.at[k], z_buf.at[k], z_send.at[k], z_recv.at[k], along[k - 1]))
    total = mine[0] + x_buf[0].astype(jnp.float32)
    for k in range(1, nz):
        sent[k - 1].wait_recv()
        total += z_buf[k].astype(jnp.float32)
    weighted = (gate * total).astype(jnp.bfloat16)
    w_buf[...] = crossed(pack, weighted).astype(jnp.bfloat16)

    def deliver(i):
        to = lax.rem(me + i, n)
        at = turn * ne + place
        return pltpu.make_async_remote_copy(
            src_ref=w_buf.at[cut(to * cap, cap), :],
            dst_ref=o_ref.at[cut(place * cap, cap), cut(turn * block, block)],
            send_sem=t_send.at[i], recv_sem=t_recv.at[at],
            device_id={"seq": to, "exp": target}, device_id_type=MESH,
        )

    home = pltpu.make_async_copy(
        w_buf.at[cut(me * cap, cap), :], o_ref.at[cut(place * cap, cap), cut(turn * block, block)], own.at[2]
    )
    for i in range(1, n):
        deliver(i).start()

    @pl.when(stays)
    def _():
        home.start()

    @pl.when(jnp.logical_not(stays))
    def _():
        deliver(0).start()

    for k in range(per):
        for e in range(ne):
            arrival = pltpu.make_async_remote_copy(
                src_ref=w_buf.at[cut(me * cap, cap), :],
                dst_ref=o_ref.at[e * cap : (e + 1) * cap, k * block : (k + 1) * block],
                send_sem=t_send.at[0], recv_sem=t_recv.at[k * ne + e],
                device_id=partner, device_id_type=MESH,
            )

            @pl.when(jnp.logical_not(to_self(k, e)))
            def _():
                arrival.wait_recv()

    @pl.when(stays)
    def _():
        home.wait()

    @pl.when(jnp.logical_not(stays))
    def _():
        deliver(0).wait_send()

    for i in range(1, n):
        deliver(i).wait_send()
    for k in range(share):
        for e in range(ne):
            handed = hand(k, e)

            @pl.when(jnp.logical_not(hand_self(k, e)))
            def _():
                handed.wait_send()

    for copy in scales + list(hops.values()) + list(pairs.values()) + sent:
        copy.wait_send()


def run_experts(hidden_state, picks, norm_gain, router, w_gate, w_up, w_down, n, ne, cap):
    tokens, width = hidden_state.shape
    count, slots = picks.shape[1], n * cap
    depth, hidden = w_gate.shape
    nz, block = n // 2, depth // n
    bf, f32 = jnp.bfloat16, jnp.float32
    inside = pl.BlockSpec(memory_space=pltpu.VMEM)
    outside = pl.BlockSpec(memory_space=pltpu.HBM)
    slab = pltpu.VMEM((nz, count, block), bf)
    sems = lambda size: pltpu.SemaphoreType.DMA((size,))
    return pl.pallas_call(
        functools.partial(experts_kernel, n, ne, cap),
        out_shape=(
            jax.ShapeDtypeStruct((ne * cap, width), bf),
            jax.ShapeDtypeStruct((ne * cap, tokens), bf),
        ),
        in_specs=[inside] * 4 + [outside] * 3,
        out_specs=(outside, inside),
        scratch_shapes=[
            pltpu.VMEM((depth, hidden), bf), pltpu.VMEM((depth, hidden), bf), pltpu.VMEM((hidden, depth), bf),
            pltpu.VMEM((ne * cap, width), bf), pltpu.VMEM((slots, block), bf),
            pltpu.VMEM((n, count, block), bf), pltpu.VMEM((1, depth), f32),
            pltpu.VMEM((count, hidden), f32), pltpu.VMEM((count, hidden), f32), pltpu.VMEM((nz, count, block), f32),
            slab, slab, slab, slab, pltpu.VMEM((slots, block), bf),
            sems(3), sems(ne * n), sems(ne * n), sems(ne), sems(ne), sems(4 * n), sems(4 * n),
            sems(nz), sems(nz), sems(nz), sems(nz), sems(n), sems(n), sems(3),
        ],
        compiler_params=pltpu.CompilerParams(
            collective_id=2, has_side_effects=True, vmem_limit_bytes=44 * 1024 * 1024
        ),
    )(hidden_state, picks, norm_gain, router.reshape(1, -1), w_gate, w_up, w_down)


def flash_kernel(block, border_ref, q_ref, k_ref, v_ref, o_ref):
    at = pl.program_id(1)
    border = border_ref[0]
    q_start = at * block
    rows = q_start + lax.broadcasted_iota(jnp.int32, (block, 1), 0)
    low = jnp.where(rows >= border, border, 0)
    steps = lax.broadcasted_iota(jnp.int32, (block, block), 1)
    q = q_ref[...]
    scale = math.log2(math.e) / math.sqrt(HD)

    def scored(j):
        start = pl.multiple_of(j * block, block)
        s = lax.dot_general(
            q, k_ref[pl.ds(start, block), :], (((1,), (1,)), ((), ())), preferred_element_type=jnp.float32
        )
        return s * scale, start

    def mix(p, start):
        return jnp.dot(
            p.astype(jnp.bfloat16), v_ref[pl.ds(start, block), :], preferred_element_type=jnp.float32
        )

    s, start = scored(at)
    s = jnp.where((steps >= low - start) & (steps <= rows - start), s, -jnp.inf)
    top = jnp.max(s, axis=1, keepdims=True)
    p = jnp.exp2(s - top)
    state = (top, jnp.sum(p, axis=1, keepdims=True), mix(p, start))

    def step(j, state):
        top, total, out = state
        s, start = scored(j)
        s = jnp.where(steps >= low - start, s, -jnp.inf)
        new_top = jnp.maximum(top, jnp.max(s, axis=1, keepdims=True))
        factor = jnp.exp2(top - new_top)
        p = jnp.exp2(s - new_top)
        return (
            new_top,
            total * factor + jnp.sum(p, axis=1, keepdims=True),
            out * factor + mix(p, start),
        )

    begin = jnp.where(q_start >= border, border // block, 0)
    top, total, out = lax.fori_loop(begin, at, step, state)
    o_ref[...] = (out / total).astype(o_ref.dtype)


def flash(queries, keys, values, border):
    rows, width = queries.shape
    block = block_rows
    return pl.pallas_call(
        functools.partial(flash_kernel, block),
        out_shape=jax.ShapeDtypeStruct((rows, width), queries.dtype),
        grid_spec=pltpu.PrefetchScalarGridSpec(
            num_scalar_prefetch=1,
            grid=(width // HD, rows // block),
            in_specs=[
                pl.BlockSpec((block, HD), lambda h, i, b: (i, h)),
                pl.BlockSpec((rows, HD), lambda h, i, b: (0, h)),
                pl.BlockSpec((rows, HD), lambda h, i, b: (0, h)),
            ],
            out_specs=pl.BlockSpec((block, HD), lambda h, i, b: (i, h)),
        ),
    )(border, queries, keys, values)


def attend_by_head(queries, keys, values, documents, n, n_exp):
    border = jnp.sum((documents == 0).astype(jnp.int32)).reshape(1)
    q_all, k_all, v_all = heads_out(queries, keys, values, n)
    return heads_back(flash(q_all, k_all, v_all, border), n, n_exp)


def chain_kernel(
    nz, ne, group, docs_ref, q_ref, k_ref, v_ref, res_ref, w_ref, o_ref,
    q0, q1, q2, kb, vb, o0, o1, c0, c1, s2, s1, p2, p1, ls2, ls1, lp2, lp1, back, att, proj, acc, res,
    load, x_send, x_recv, d0_send, d0_recv, d1_send, d1_recv, u2_send, u2_recv, g2_send, g2_recv,
    u1_send, u1_recv, g1_send, g1_recv, b_send, b_recv, y_send, y_recv, m_send, m_recv,
    r_send, r_recv, w_sem, res_sem,
):
    me = lax.axis_index("seq")
    place = lax.axis_index("exp")
    z, x = me // 2, lax.rem(me, 2)
    y, core = place // 2, lax.rem(place, 2)
    ny = ne // 2
    tokens = q_ref.shape[0]
    steps = 2 * group
    up = {"seq": lax.rem(z + 1, nz) * 2 + x}
    down = {"seq": lax.rem(z + nz - 1, nz) * 2 + x}
    partner = {"seq": z * 2 + 1 - x}
    sibling = {"exp": y * 2 + 1 - core}
    far_place = lax.rem(y + 1, ny) * 2 + core
    far = {"exp": far_place}
    has1, has2, low1 = z + 1 < nz, z + 2 < nz, z >= 1
    border = jnp.sum(
        jnp.sum((docs_ref[...] == 0).astype(jnp.int32), axis=1, keepdims=True), axis=0, keepdims=True
    )
    scale = math.log2(math.e) / math.sqrt(HD)
    greet([up, down, partner, sibling, far])

    def remote(src, dst, send, recv, peer):
        return pltpu.make_async_remote_copy(
            src_ref=src, dst_ref=dst, send_sem=send, recv_sem=recv, device_id=peer, device_id_type=MESH
        )

    def half(ref, h, side):
        return ref.at[h, cut(side * tokens, tokens), :]

    def columns(ref, h, side):
        return ref.at[:, cut((side * group + h) * HD, HD)]

    def loads(h):
        return (
            pltpu.make_async_copy(columns(q_ref, h, x), q0.at[2 * h], load.at[3 * h]),
            pltpu.make_async_copy(columns(k_ref, h, x), half(kb, h, x), load.at[3 * h + 1]),
            pltpu.make_async_copy(columns(v_ref, h, x), half(vb, h, x), load.at[3 * h + 2]),
        )

    def swaps(h):
        side = 1 - x
        return tuple(
            remote(columns(src, h, side), dst, x_send.at[3 * h + t], x_recv.at[3 * h + t], partner)
            for t, (src, dst) in enumerate(
                ((q_ref, q0.at[2 * h + 1]), (k_ref, half(kb, h, x)), (v_ref, half(vb, h, x)))
            )
        )

    def q_down(t):
        return remote(q0.at[t], q1.at[t], d0_send.at[t], d0_recv.at[t], down)

    def q_further(t):
        return remote(q1.at[t], q2.at[t], d1_send.at[t], d1_recv.at[t], down)

    def part2_up(t):
        return (
            remote(s2.at[t], p2.at[t], u2_send.at[t], u2_recv.at[t], up),
            remote(ls2.at[t], lp2.at[t], g2_send.at[t], g2_recv.at[t], up),
        )

    def part1_up(t):
        return (
            remote(s1.at[t], p1.at[t], u1_send.at[t], u1_recv.at[t], up),
            remote(ls1.at[t], lp1.at[t], g1_send.at[t], g1_recv.at[t], up),
        )

    def spot(at, t):
        return att.at[t, :, cut(at * HD, HD)]

    def give_back(t):
        return remote(back.at[t // 2], spot(place, t), b_send.at[t // 2], b_recv.at[t // 2], partner)

    def to_far(t):
        return remote(spot(place, t), spot(place, t), y_send.at[t], y_recv.at[t], far)

    def to_sibling(t):
        return remote(spot(place, t), spot(place, t), m_send.at[t], m_recv.at[t], sibling)

    def relay(t):
        return remote(spot(far_place, t), spot(far_place, t), r_send.at[t], r_recv.at[t], sibling)

    def proj_loads(t):
        side = x + (t % 2) * (1 - 2 * x)
        return [
            pltpu.make_async_copy(
                w_ref.at[cut(((e * 2 + side) * group + t // 2) * HD, HD), :],
                proj.at[t, e * HD : (e + 1) * HD, :],
                w_sem.at[t, e],
            )
            for e in range(ne)
        ]

    res_load = pltpu.make_async_copy(res_ref, res, res_sem)

    tile = HD
    tiles = tokens // tile
    span = kb.shape[1]
    key_base = z * span
    diagonal = lax.broadcasted_iota(jnp.int32, (tile, tile), 0) == lax.broadcasted_iota(
        jnp.int32, (tile, tile), 1
    )

    big = 2 * tile
    at = lax.broadcasted_iota(jnp.int32, (big, tokens), 1)

    def attend(q_of, level, t, put, blocks):
        h = t // 2
        side = x + lax.rem(t, 2) * (1 - 2 * x)
        base = ((z + level) * 2 + side) * tokens - key_base
        edge = border - key_base

        def score(r):
            rows = base + r * big + lax.broadcasted_iota(jnp.int32, (big, 1), 0)
            low = jnp.where(rows >= edge, edge, -key_base)
            out = []
            for b in range(blocks):
                s = lax.dot_general(
                    q_of[r * big : (r + 1) * big, :], kb[h, b * tokens : (b + 1) * tokens, :],
                    (((1,), (1,)), ((), ())), preferred_element_type=jnp.float32,
                )
                seen = at >= low - b * tokens
                if level == 0 and b == blocks - 1:
                    seen = seen & (at <= rows - b * tokens)
                out.append(jnp.where(seen, s, -1e30))
            return out

        later = score(0)
        for r in range(tokens // big):
            now = later
            if (r + 1) * big < tokens:
                later = score(r + 1)
            top = jnp.max(functools.reduce(jnp.maximum, now), axis=1, keepdims=True) * scale
            total = jnp.zeros((big, 1), jnp.float32)
            out = jnp.zeros((big, HD), jnp.float32)
            for b, s in enumerate(now):
                p = jnp.exp2(s * scale - top)
                total += jnp.sum(p, axis=1, keepdims=True)
                out += jnp.dot(
                    p.astype(jnp.bfloat16), vb[h, b * tokens : (b + 1) * tokens, :],
                    preferred_element_type=jnp.float32,
                )
            put(r * big, out / total, top + jnp.log2(total))

    def flat(level):
        return jnp.sum(jnp.where(diagonal, level, 0.0), axis=0, keepdims=True)

    def upright(ref, r):
        return jnp.sum(jnp.where(diagonal, ref[r : r + 1, :], 0.0), axis=1, keepdims=True)

    def joined(out, level, p_of, l_of, r):
        other = upright(l_of, r)
        top = jnp.maximum(level, other)
        mine, theirs = jnp.exp2(level - top), jnp.exp2(other - top)
        both = mine + theirs
        out = (out * mine + p_of[r * tile : (r + 1) * tile, :].astype(jnp.float32) * theirs) / both
        return out, top + jnp.log2(both)

    for h in range(group):
        for copy in swaps(h):
            copy.start()
        for copy in loads(h):
            copy.start()

    for t in range(steps):
        for copy in proj_loads(t):
            copy.start()
    res_load.start()

    def send_own(t):
        @pl.when(lax.rem(t, 2) == 0)
        def _():
            loads(t // 2)[0].wait()

        @pl.when(lax.rem(t, 2) == 1)
        def _():
            swaps(t // 2)[0].wait_recv()

        @pl.when(low1)
        def _():
            q_down(t).start()

    def forward(t):
        @pl.when(has1)
        def _():
            q_down(t).wait_recv()

            @pl.when(low1)
            def _():
                q_further(t).start()

    def spread(t):
        to_far(t).start()
        to_sibling(t).start()

    send_own(jnp.int32(0))
    send_own(jnp.int32(1))
    forward(jnp.int32(0))

    def step(i, carry):
        live = i < steps

        @pl.when(i + 2 < steps)
        def _():
            send_own(i + 2)

        @pl.when(i + 1 < steps)
        def _():
            forward(i + 1)

        @pl.when(live & (lax.rem(i, 2) == 0))
        def _():
            for copy in loads(i // 2)[1:]:
                copy.wait()
            for copy in swaps(i // 2)[1:]:
                copy.wait_recv()

        @pl.when(live & has2)
        def _():
            q_further(i).wait_recv()

            def put(at, out, level):
                s2[i, at : at + big, :] = out.astype(jnp.bfloat16)
                for r in range(big // tile):
                    row = at // tile + r
                    ls2[i, row : row + 1, :] = flat(level[r * tile : (r + 1) * tile])

            attend(q2.at[i], 2, i, put, 2)
            for copy in part2_up(i):
                copy.start()

        @pl.when(i == 1)
        def _():
            res_load.wait()
            acc[...] = res[...].astype(jnp.float32)

        t1 = i - 1

        @pl.when((t1 >= 0) & (t1 < steps) & has1)
        def _():
            def put(r, out, level):
                s1[t1, r * tile : (r + 1) * tile, :] = out.astype(jnp.bfloat16)
                ls1[t1, r : r + 1, :] = flat(level)

            @pl.when(low1)
            def _():
                for copy in part2_up(t1):
                    copy.wait_recv()
                for r in range(tiles):
                    put(r, *joined(o1[t1, r * tile : (r + 1) * tile, :], c1[t1, r * tile : (r + 1) * tile, :], p2.at[t1], lp2.at[t1], r))

            @pl.when(jnp.logical_not(low1))
            def _():
                for r in range(tiles):
                    put(r, o1[t1, r * tile : (r + 1) * tile, :], c1[t1, r * tile : (r + 1) * tile, :])

            for copy in part1_up(t1):
                copy.start()

        @pl.when(live & has1)
        def _():
            def put(at, out, level):
                o1[i, at : at + big, :] = out
                c1[i, at : at + big, :] = level

            attend(q1.at[i], 1, i, put, 2)

        t0 = i - 2

        @pl.when((t0 >= 0) & (t0 < steps))
        def _():
            def finish(put):
                @pl.when(low1)
                def _():
                    for copy in part1_up(t0):
                        copy.wait_recv()
                    for r in range(tiles):
                        out, level = joined(o0[t0, r * tile : (r + 1) * tile, :], c0[t0, r * tile : (r + 1) * tile, :], p1.at[t0], lp1.at[t0], r)
                        put(r, out)

                @pl.when(jnp.logical_not(low1))
                def _():
                    for r in range(tiles):
                        put(r, o0[t0, r * tile : (r + 1) * tile, :])

            @pl.when(lax.rem(t0, 2) == 0)
            def _():
                def put(r, out):
                    att[t0, r * tile : (r + 1) * tile, cut(place * HD, HD)] = out.astype(jnp.bfloat16)

                finish(put)
                spread(t0)

            @pl.when(lax.rem(t0, 2) == 1)
            def _():
                def put(r, out):
                    back[t0 // 2, r * tile : (r + 1) * tile, :] = out.astype(jnp.bfloat16)

                finish(put)
                give_back(t0).start()

        @pl.when(live)
        def _():
            def put(at, out, level):
                o0[i, at : at + big, :] = out
                c0[i, at : at + big, :] = level

            first_half = lax.rem(i, 2) == x

            @pl.when(first_half)
            def _():
                attend(q0.at[i], 0, i, put, 1)

            @pl.when(jnp.logical_not(first_half))
            def _():
                attend(q0.at[i], 0, i, put, 2)

        t4 = i - 3

        @pl.when((t4 >= 0) & (t4 < steps) & (lax.rem(t4, 2) == 1))
        def _():
            give_back(t4).wait_recv()
            spread(t4)

        t5 = i - 5

        @pl.when((t5 >= 0) & (t5 < steps))
        def _():
            to_far(t5).wait_recv()
            relay(t5).start()

        t6 = i - 6

        @pl.when((t6 >= 0) & (t6 < steps))
        def _():
            to_sibling(t6).wait_recv()
            relay(t6).wait_recv()
            for copy in proj_loads(t6):
                copy.wait()

            acc[...] += jnp.dot(att[t6], proj[t6], preferred_element_type=jnp.float32)

        return carry

    lax.fori_loop(0, steps + 6, step, 0)
    o_ref[...] = acc[...].astype(o_ref.dtype)


    def settle(t, carry):
        to_far(t).wait_send()
        to_sibling(t).wait_send()
        relay(t).wait_send()

        @pl.when(low1)
        def _():
            q_down(t).wait_send()

            @pl.when(has1)
            def _():
                q_further(t).wait_send()

        @pl.when(has1)
        def _():
            for copy in part1_up(t):
                copy.wait_send()

        @pl.when(has2)
        def _():
            for copy in part2_up(t):
                copy.wait_send()

        @pl.when(lax.rem(t, 2) == 1)
        def _():
            give_back(t).wait_send()
            for copy in swaps(t // 2):
                copy.wait_send()

        return carry

    lax.fori_loop(0, steps, settle, 0)


def attend_by_chain(queries, keys, values, documents, residual, out_proj, n, n_exp):
    tokens, width = queries.shape
    group = width // HD // 2
    steps = 2 * group
    nz = n // 2
    features = out_proj.shape[1]
    outside = pl.BlockSpec(memory_space=pltpu.HBM)
    inside = pl.BlockSpec(memory_space=pltpu.VMEM)
    bf, f32 = jnp.bfloat16, jnp.float32
    chunks = pltpu.VMEM((steps, tokens, HD), bf)
    side = pltpu.VMEM((group, 2 * tokens, HD), bf)
    wide = pltpu.VMEM((steps, tokens, HD), f32)
    thin = pltpu.VMEM((steps, tokens, 1), f32)
    flats = pltpu.VMEM((steps, max(8, tokens // HD), HD), f32)
    sems = lambda count: pltpu.SemaphoreType.DMA((count,))
    return pl.pallas_call(
        functools.partial(chain_kernel, nz, n_exp, group),
        out_shape=jax.ShapeDtypeStruct((tokens, features), queries.dtype),
        in_specs=[inside] + [outside] * 5,
        out_specs=inside,
        scratch_shapes=[chunks] * 3 + [side] * 2 + [wide] * 2 + [thin] * 2 + [chunks] * 4 + [flats] * 4
        + [pltpu.VMEM((group, tokens, HD), bf), pltpu.VMEM((steps, tokens, n_exp * HD), bf)]
        + [pltpu.VMEM((steps, n_exp * HD, features), bf), pltpu.VMEM((tokens, features), f32)]
        + [pltpu.VMEM((tokens, features), bf)]
        + [sems(3 * group)] * 3 + [sems(steps)] * 12 + [sems(group)] * 2 + [sems(steps)] * 6
        + [pltpu.SemaphoreType.DMA((steps, n_exp)), pltpu.SemaphoreType.DMA(())],
        compiler_params=pltpu.CompilerParams(
            collective_id=0, has_side_effects=True, vmem_limit_bytes=54 * 1024 * 1024
        ),
    )(documents.reshape(-1, HD), queries, keys, values, residual, out_proj)


def attend_by_token(queries, keys, values, documents):
    tokens = queries.shape[0]
    heads_here = queries.shape[1] // HD
    seq_pos = lax.axis_index("seq")
    start_row = seq_pos * tokens
    query_pos = start_row + jnp.arange(tokens, dtype=jnp.int32)
    query_doc = lax.dynamic_slice_in_dim(documents, start_row, tokens, 0)
    query_heads = queries.reshape(tokens, heads_here, HD)
    score_scale = 1.0 / math.sqrt(HD)

    def attend(state, key_rows, value_rows, key_start):
        row_count = key_rows.shape[0]
        key_pos = key_start + jnp.arange(row_count, dtype=jnp.int32)
        key_doc = lax.dynamic_slice_in_dim(documents, key_start, row_count, 0)
        scores = (
            jnp.einsum(
                "qhd,khd->qhk",
                query_heads,
                key_rows.reshape(row_count, heads_here, HD),
                preferred_element_type=jnp.float32,
            )
            * score_scale
        )
        allowed = (key_pos[None, :] <= query_pos[:, None]) & (
            key_doc[None, :] == query_doc[:, None]
        )
        scores = jnp.where(allowed[:, None, :], scores, -jnp.inf)
        running_max, running_sum, running_out = state
        new_max = jnp.maximum(running_max, jnp.max(scores, axis=2))
        factor = jnp.exp(running_max - new_max)
        weights = jnp.exp(scores - new_max[:, :, None])
        running_sum = running_sum * factor + jnp.sum(weights, axis=2)
        running_out = running_out * factor[:, :, None] + jnp.einsum(
            "qhk,khd->qhd",
            weights.astype(jnp.bfloat16),
            value_rows.reshape(row_count, heads_here, HD),
            preferred_element_type=jnp.float32,
        )
        return (new_max, running_sum, running_out)

    def visit_block(state, key_rows, value_rows, key_start):
        row_count = key_rows.shape[0]
        last_doc = lax.dynamic_index_in_dim(documents, key_start + row_count - 1, 0, keepdims=False)
        beyond = (key_start > query_pos[tokens - 1]) | (last_doc < query_doc[0])
        return lax.cond(
            beyond,
            lambda inner_state: inner_state,
            lambda inner_state: attend(inner_state, key_rows, value_rows, key_start),
            state,
        )

    initial = (
        jnp.full((tokens, heads_here), -1e30, jnp.float32),
        jnp.zeros((tokens, heads_here), jnp.float32),
        jnp.zeros((tokens, heads_here, HD), jnp.float32),
    )
    state = initial
    key_piece = lax.all_gather(keys, "seq", axis=0, tiled=True)
    value_piece = lax.all_gather(values, "seq", axis=0, tiled=True)
    row_count = key_piece.shape[0]
    blocks = row_count // block_rows
    key_stack = key_piece.reshape(blocks, block_rows, key_piece.shape[1])
    value_stack = value_piece.reshape(blocks, block_rows, value_piece.shape[1])

    def scan_step(inner_state, block_item):
        block_index, key_rows, value_rows = block_item
        return (visit_block(inner_state, key_rows, value_rows, block_index * block_rows), None)

    state, unused = lax.scan(
        scan_step, state, (jnp.arange(blocks, dtype=jnp.int32), key_stack, value_stack)
    )
    running_max, running_sum, running_out = state
    attended = (
        (running_out / running_sum[:, :, None])
        .reshape(tokens, heads_here * HD)
        .astype(jnp.bfloat16)
    )
    return lax.all_gather(attended, "exp", axis=1, tiled=True)


def shards(
    residual,
    queries,
    keys,
    values,
    documents,
    out_proj,
    modality,
    norm_gain,
    picks,
    router,
    w_gate,
    w_up,
    w_down,
):
    tokens = queries.shape[0]
    seq_pos = lax.axis_index("seq")
    start_row = seq_pos * tokens
    n_seq, n_exp = lax.axis_size("seq"), lax.axis_size("exp")
    if (queries.shape[1] // HD) % n_seq == 0 and n_exp == 4:
        hidden_state = attend_by_chain(
            queries, keys, values, documents, residual, out_proj, n_seq, n_exp
        )
    else:
        attended = attend_by_token(queries, keys, values, documents)
        mixed = jnp.dot(attended, out_proj, preferred_element_type=jnp.float32)
        hidden_state = (residual.astype(jnp.float32) + mixed).astype(jnp.bfloat16)
    returned, placing = run_experts(
        hidden_state, picks, norm_gain, router, w_gate[0], w_up[0], w_down[0], n_seq, n_exp, tokens // 32
    )
    expert_add = lax.dot_general(
        placing, returned, (((0,), (0,)), ((), ())), preferred_element_type=jnp.float32
    )
    return (hidden_state.astype(jnp.float32) + expert_add).astype(jnp.bfloat16)


def solution(mesh):
    return jax.shard_map(
        shards,
        mesh=mesh,
        in_specs=(
            P("seq", "exp"),
            P("seq", "exp"),
            P("seq", "exp"),
            P("seq", "exp"),
            P(),
            P(None, "exp"),
            P("seq"),
            P(None, "exp"),
            P(),
            P(None, "exp"),
            P("exp", None, "seq"),
            P("exp", None, "seq"),
            P("exp", "seq", None),
        ),
        out_specs=P("seq", "exp"),
        check_vma=False,
    )
```

```python
import functools
import math

import jax
import jax.numpy as jnp
from jax import lax
from jax.experimental import pallas as pl
from jax.experimental.pallas import tpu as pltpu
from jax.sharding import PartitionSpec as P

D = 8192
HD = 128


block_rows = 512


MESH = pl.DeviceIdType.MESH


def greet(peers):
    barrier = pltpu.get_barrier_semaphore()
    for peer in peers:
        pl.semaphore_signal(barrier, inc=1, device_id=peer, device_id_type=MESH)
    pl.semaphore_wait(barrier, len(peers))


def cut(start, size):
    return pl.ds(pl.multiple_of(start, size), size)


def heads_out_kernel(n, width, q_ref, k_ref, v_ref, qo, ko, vo, send, recv, own):
    me = lax.axis_index("seq")
    tokens = q_ref.shape[0]
    greet([{"seq": lax.rem(me + i, n)} for i in range(1, n)])
    pairs = ((k_ref, ko), (v_ref, vo), (q_ref, qo))
    copies = []
    for i in range(1, n):
        to = lax.rem(me + i, n)
        for t, (src, dst) in enumerate(pairs):
            copies.append(
                pltpu.make_async_remote_copy(
                    src_ref=src.at[:, cut(to * width, width)],
                    dst_ref=dst.at[cut(me * tokens, tokens), :],
                    send_sem=send.at[t * n + i],
                    recv_sem=recv.at[t * n + i],
                    device_id={"seq": to},
                    device_id_type=MESH,
                )
            )
            copies[-1].start()
    for t, (src, dst) in enumerate(pairs):
        copies.append(
            pltpu.make_async_copy(
                src.at[:, cut(me * width, width)], dst.at[cut(me * tokens, tokens), :], own.at[t]
            )
        )
        copies[-1].start()
    for copy in copies:
        copy.wait()


def heads_out(queries, keys, values, n):
    tokens, columns = queries.shape
    width = columns // n
    whole = jax.ShapeDtypeStruct((n * tokens, width), queries.dtype)
    anywhere = pl.BlockSpec(memory_space=pl.ANY)
    return pl.pallas_call(
        functools.partial(heads_out_kernel, n, width),
        out_shape=(whole, whole, whole),
        in_specs=[anywhere] * 3,
        out_specs=(anywhere,) * 3,
        scratch_shapes=[
            pltpu.SemaphoreType.DMA((3 * n,)),
            pltpu.SemaphoreType.DMA((3 * n,)),
            pltpu.SemaphoreType.DMA((3,)),
        ],
        compiler_params=pltpu.CompilerParams(collective_id=0, has_side_effects=True),
    )(queries, keys, values)


def heads_back_kernel(n, ny, width, a_ref, o_ref, s_send, s_recv, y_send, y_recv, c_send, c_recv, own):
    me = lax.axis_index("seq")
    place = lax.axis_index("exp")
    y, core = place // 2, lax.rem(place, 2)
    sibling = {"exp": y * 2 + 1 - core}
    across = [{"exp": lax.rem(y + k, ny) * 2 + core} for k in range(1, ny)]
    tokens = o_ref.shape[0]
    span = n * width
    greet([{"seq": lax.rem(me + i, n)} for i in range(1, n)] + across + [sibling])

    def piece(exp_at, seq_at):
        return o_ref.at[:, cut(exp_at * span + seq_at * width, width)]

    local = pltpu.make_async_copy(a_ref.at[cut(me * tokens, tokens), :], piece(place, me), own)
    local.start()
    first = []
    for i in range(1, n):
        to = lax.rem(me + i, n)
        first.append(
            push(
                a_ref.at[cut(to * tokens, tokens), :],
                piece(place, me),
                s_send.at[i],
                s_recv.at[i],
                {"seq": to},
            )
        )
    second = []
    third = []
    for i in range(n):
        if i == 0:
            local.wait()
        else:
            first[i - 1].wait_recv()
        part = piece(place, lax.rem(me + n - i, n))
        for k in range(1, ny):
            at = i * ny + k
            second.append(push(part, part, y_send.at[at], y_recv.at[at], across[k - 1]))
        third.append(push(part, part, c_send.at[i * ny], c_recv.at[i * ny], sibling))
    for i in range(n):
        for k in range(1, ny):
            second[i * (ny - 1) + k - 1].wait_recv()
            at = i * ny + k
            part = piece(lax.rem(y + ny - k, ny) * 2 + core, lax.rem(me + n - i, n))
            third.append(push(part, part, c_send.at[at], c_recv.at[at], sibling))
    for copy in third:
        copy.wait_recv()
    for copy in first + second + third:
        copy.wait_send()


def heads_back(attended, n, n_exp):
    rows, width = attended.shape
    ny = n_exp // 2
    anywhere = pl.BlockSpec(memory_space=pl.ANY)
    return pl.pallas_call(
        functools.partial(heads_back_kernel, n, ny, width),
        out_shape=jax.ShapeDtypeStruct((rows // n, n_exp * n * width), attended.dtype),
        in_specs=[anywhere],
        out_specs=anywhere,
        scratch_shapes=[
            pltpu.SemaphoreType.DMA((n,)),
            pltpu.SemaphoreType.DMA((n,)),
            pltpu.SemaphoreType.DMA((n * ny,)),
            pltpu.SemaphoreType.DMA((n * ny,)),
            pltpu.SemaphoreType.DMA((n * ny,)),
            pltpu.SemaphoreType.DMA((n * ny,)),
            pltpu.SemaphoreType.DMA(()),
        ],
        compiler_params=pltpu.CompilerParams(collective_id=1, has_side_effects=True),
    )(attended)


def push(src, dst, send, recv, peer):
    copy = pltpu.make_async_remote_copy(
        src_ref=src, dst_ref=dst, send_sem=send, recv_sem=recv, device_id=peer, device_id_type=MESH
    )
    copy.start()
    return copy


def lines(me, nz):
    z, x = me // 2, lax.rem(me, 2)
    along = [{"seq": lax.rem(z + k, nz) * 2 + x} for k in range(1, nz)]
    return z, x, along, {"seq": z * 2 + 1 - x}


def ring_device(pos, n):
    half = pos // (n // 2)
    return (1 - half) * pos * 2 + half * ((n - 1 - pos) * 2 + 1)


def rows_kernel(n, ne, cap, width, r_ref, o_ref, e_send, e_recv, s_send, s_recv, own):
    me = lax.axis_index("seq")
    place = lax.axis_index("exp")
    z, x = me // 2, lax.rem(me, 2)
    pos = (1 - x) * z + x * (n - 1 - z)
    ways = (1, n - 1)
    nexts = [{"seq": ring_device(lax.rem(pos + way, n), n)} for way in ways]
    others = [{"exp": lax.rem(place + i, ne)} for i in range(1, ne)]
    greet(others + nexts)

    def piece(seq_at, exp_at):
        return o_ref.at[cut(seq_at * cap, cap), cut(exp_at * width, width)]

    local = pltpu.make_async_copy(r_ref.at[cut(place * cap, cap), :], piece(me, place), own)
    local.start()
    first = []
    for i in range(1, ne):
        src = r_ref.at[cut(lax.rem(place + i, ne) * cap, cap), :]
        first.append(push(src, piece(me, place), e_send.at[i], e_recv.at[i], others[i - 1]))
    hops = {}
    for t in range(n // 2):
        for i in range(ne):
            if t == 0:
                local.wait() if i == 0 else first[i - 1].wait_recv()
            for d in range(2):
                if t:
                    hops[i, d, t - 1].wait_recv()
                if t == n // 2 - 1 and i % 2 != d:
                    continue
                seq_at = ring_device(lax.rem(pos + n + t * (ways[1 - d]), n), n)
                part = piece(seq_at, lax.rem(place + ne - i, ne))
                at = (i * 2 + d) * (n // 2) + t
                hops[i, d, t] = push(part, part, s_send.at[at], s_recv.at[at], nexts[d])
    for i in range(ne):
        hops[i, i % 2, n // 2 - 1].wait_recv()
    for copy in first + list(hops.values()):
        copy.wait_send()


def share_rows(rows, n, ne):
    cap, width = rows.shape[0] // ne, rows.shape[1]
    anywhere = pl.BlockSpec(memory_space=pl.ANY)
    return pl.pallas_call(
        functools.partial(rows_kernel, n, ne, cap, width),
        out_shape=jax.ShapeDtypeStruct((n * cap, ne * width), rows.dtype),
        in_specs=[anywhere],
        out_specs=anywhere,
        scratch_shapes=[pltpu.SemaphoreType.DMA((ne,))] * 2
        + [pltpu.SemaphoreType.DMA((ne * n,))] * 2
        + [pltpu.SemaphoreType.DMA(())],
        compiler_params=pltpu.CompilerParams(collective_id=2, has_side_effects=True),
    )(rows)


def sums_kernel(
    nz, ne, cap, p_ref, g_ref, o_ref, x_buf, s_buf, z_buf, total, w_buf,
    x_send, x_recv, z_send, z_recv, e_send, e_recv, own,
):
    me = lax.axis_index("seq")
    z, x, along, partner = lines(me, nz)
    place = lax.axis_index("exp")
    others = [{"exp": lax.rem(place + i, ne)} for i in range(1, ne)]
    greet(along + [partner] + others)

    def rows_of(k, side):
        return cut((lax.rem(z + k, nz) * 2 + side) * cap, cap)

    order = list(range(1, nz)) + [0]
    pairs = {}
    for k in order:
        pairs[k] = push(p_ref.at[rows_of(k, 1 - x), :], x_buf.at[k], x_send.at[k], x_recv.at[k], partner)
    sent = []
    for k in order:
        pairs[k].wait_recv()
        both = p_ref[rows_of(k, x), :].astype(jnp.float32) + x_buf[k].astype(jnp.float32)
        if k:
            s_buf[k] = both.astype(jnp.bfloat16)
            sent.append(push(s_buf.at[k], z_buf.at[k], z_send.at[k], z_recv.at[k], along[k - 1]))
        else:
            total[...] = both
    for k in range(1, nz):
        sent[k - 1].wait_recv()
        total[...] += z_buf[k].astype(jnp.float32)
    w_buf[...] = (g_ref[...] * total[...]).astype(jnp.bfloat16)
    width = w_buf.shape[1] // ne
    mine = o_ref.at[cut(place * cap, cap), :]
    local = pltpu.make_async_copy(w_buf.at[:, cut(place * width, width)], mine, own)
    local.start()
    spread = []
    for i in range(1, ne):
        src = w_buf.at[:, cut(lax.rem(place + i, ne) * width, width)]
        spread.append(push(src, mine, e_send.at[i], e_recv.at[i], others[i - 1]))
    local.wait()
    for copy in spread:
        copy.wait_recv()
    for copy in list(pairs.values()) + sent + spread:
        copy.wait_send()


def sum_rows(partial, gate, n, ne):
    cap, width = partial.shape[0] // n, partial.shape[1]
    nz = n // 2
    slots = pltpu.VMEM((nz, cap, width), jnp.bfloat16)
    return pl.pallas_call(
        functools.partial(sums_kernel, nz, ne, cap),
        out_shape=jax.ShapeDtypeStruct((ne * cap, width // ne), jnp.bfloat16),
        in_specs=[pl.BlockSpec(memory_space=pltpu.VMEM)] * 2,
        out_specs=pl.BlockSpec(memory_space=pl.ANY),
        scratch_shapes=[slots, slots, slots]
        + [pltpu.VMEM((cap, width), jnp.float32), pltpu.VMEM((cap, width), jnp.bfloat16)]
        + [pltpu.SemaphoreType.DMA((nz,))] * 4
        + [pltpu.SemaphoreType.DMA((ne,))] * 2
        + [pltpu.SemaphoreType.DMA(())],
        compiler_params=pltpu.CompilerParams(collective_id=3, has_side_effects=True),
    )(partial, gate)


def experts_kernel(
    n, ne, cap, hid_ref, pick_ref, gain_ref, router_ref, wg_ref, wu_ref, wd_ref, o_ref, place_ref,
    wg, wu, wd, r_buf, slots, packed, gains, gate_sum, up_sum, mine, p_buf, x_buf, s_buf, z_buf, w_buf,
    w_sem, a_send, a_recv, n_send, n_recv, s_send, s_recv, x_send, x_recv, z_send, z_recv,
    t_send, t_recv, own,
):
    me = lax.axis_index("seq")
    place = lax.axis_index("exp")
    nz, z, x = n // 2, me // 2, lax.rem(me, 2)
    loads = [
        pltpu.make_async_copy(src, dst, w_sem.at[t])
        for t, (src, dst) in enumerate(((wg_ref, wg), (wu_ref, wu), (wd_ref, wd)))
    ]
    for copy in loads:
        copy.start()
    pos = (1 - x) * z + x * (n - 1 - z)
    ways = (1, n - 1)
    nexts = [{"seq": ring_device(lax.rem(pos + way, n), n)} for way in ways]
    partner = {"seq": z * 2 + 1 - x}
    along = [{"seq": lax.rem(z + k, nz) * 2 + x} for k in range(1, nz)]
    others = [{"exp": lax.rem(place + i, ne)} for i in range(1, ne)]
    flat_at = me * ne + place
    everyone = n * ne

    barrier = pltpu.get_barrier_semaphore()

    def hello(i, carry):
        at = lax.rem(flat_at + i, everyone)
        pl.semaphore_signal(
            barrier, inc=1, device_id={"seq": at // ne, "exp": lax.rem(at, ne)}, device_id_type=MESH
        )
        return carry

    lax.fori_loop(1, everyone, hello, 0)
    tokens, count = hid_ref.shape[0], pick_ref.shape[1]

    def counted(shape, axis):
        return lax.broadcasted_iota(jnp.int32, shape, axis)

    def upright(row):
        same = counted((count, count), 0) == counted((count, count), 1)
        return jnp.sum(jnp.where(same, row, 0), axis=1, keepdims=True)

    def chosen(seen):
        return jnp.where(seen, 1.0, 0.0).astype(jnp.bfloat16)

    def crossed(a, b):
        return lax.dot_general(a, b, (((0,), (0,)), ((), ())), preferred_element_type=jnp.float32)

    for e in range(ne):
        local_at = upright(pick_ref[e : e + 1, :]) - me * tokens
        before = jnp.sum((local_at < 0).astype(jnp.int32), axis=0, keepdims=True)
        turns = chosen(counted((count, cap), 0) - before == counted((count, cap), 1))
        hits = chosen(local_at == counted((count, tokens), 1))
        place_ref[e * cap : (e + 1) * cap, :] = crossed(turns, hits).astype(jnp.bfloat16)
    whole_at = upright(pick_ref[pl.ds(place, 1), :])
    slot = counted((1, n * cap), 1)
    begin = (slot // cap) * tokens
    before = jnp.sum((whole_at < begin).astype(jnp.int32), axis=0, keepdims=True)
    pack = chosen(
        (whole_at >= begin)
        & (whole_at < begin + tokens)
        & (counted((count, n * cap), 0) - before == lax.rem(slot, cap))
    )
    r_buf[...] = jnp.dot(place_ref[...], hid_ref[...], preferred_element_type=jnp.float32).astype(jnp.bfloat16)
    width = r_buf.shape[1]
    pl.semaphore_wait(barrier, everyone - 1)

    def kind(e):
        return (2 * e) // ne

    depth = ne * width
    block = depth // n
    per = n // ne
    target = me // per
    turn = lax.rem(me, per)
    stays = target == place

    sub = max(HD, width // n)
    share = width // sub
    groups = depth // (sub * n)

    def hand(k, e):
        number = place * share + k
        group = number // n
        return pltpu.make_async_remote_copy(
            src_ref=r_buf.at[e * cap : (e + 1) * cap, k * sub : (k + 1) * sub],
            dst_ref=slots.at[cut(me * cap, cap), cut(group * sub, sub)],
            send_sem=a_send.at[k * ne + e], recv_sem=a_recv.at[me * groups + group],
            device_id={"seq": lax.rem(number, n), "exp": e}, device_id_type=MESH,
        )

    def given(at, group):
        spot = slots.at[at * cap : (at + 1) * cap, group * sub : (group + 1) * sub]
        return pltpu.make_async_remote_copy(
            src_ref=spot, dst_ref=spot, send_sem=a_send.at[0], recv_sem=a_recv.at[at * groups + group],
            device_id=partner, device_id_type=MESH,
        )

    def to_self(k, e):
        return stays & (turn == k) & (place == e)

    def hand_self(k, e):
        return (lax.rem(place * share + k, n) == me) & (place == e)

    def kept(k, e):
        group = (place * share + k) // n
        return pltpu.make_async_copy(
            r_buf.at[e * cap : (e + 1) * cap, k * sub : (k + 1) * sub],
            slots.at[cut(me * cap, cap), cut(group * sub, sub)],
            own.at[0],
        )

    for k in range(share):
        for e in range(ne):
            handed, held = hand(k, e), kept(k, e)

            @pl.when(jnp.logical_not(hand_self(k, e)))
            def _():
                handed.start()

            @pl.when(hand_self(k, e))
            def _():
                held.start()

    own_gain = pltpu.make_async_copy(
        gain_ref.at[pl.ds(kind(place), 1), :], gains.at[:, cut(place * width, width)], own.at[1]
    )
    own_gain.start()
    scales = []
    for i in range(1, ne):
        to = lax.rem(place + i, ne)
        scales.append(
            push(
                gain_ref.at[pl.ds(kind(to), 1), :], gains.at[:, cut(place * width, width)],
                n_send.at[i], n_recv.at[i], others[i - 1],
            )
        )
    first_own = place * share
    for at in range(n):
        for group in range(groups):
            arrived = given(at, group)
            from_self = (me == at) & (first_own <= group * n + me) & (group * n + me < first_own + share)

            @pl.when(jnp.logical_not(from_self))
            def _():
                arrived.wait_recv()

    for k in range(share):
        for e in range(ne):
            held = kept(k, e)

            @pl.when(hand_self(k, e))
            def _():
                held.wait()

    packed[me] = jnp.dot(pack, slots[...], preferred_element_type=jnp.float32).astype(jnp.bfloat16)
    pieces = 4
    lines_at = count // pieces
    gate_sum[...] = jnp.zeros_like(gate_sum)
    up_sum[...] = jnp.zeros_like(up_sum)
    state = [jnp.zeros((count, 1), jnp.float32), jnp.zeros((count, HD), jnp.float32)]

    def expand(seq_at):
        for group in range(groups):
            at = cut((group * n + seq_at) * sub, sub)
            raw = packed[seq_at, :, group * sub : (group + 1) * sub].astype(jnp.float32)
            state[0] += jnp.sum(raw * raw, axis=1, keepdims=True)
            scaled = raw * gains[:, at]
            scored = scaled * router_ref[:, at].astype(jnp.float32)
            for r in range(sub // HD):
                state[1] += scored[:, r * HD : (r + 1) * HD]
            part = scaled.astype(jnp.bfloat16)
            gate_sum[...] += jnp.dot(part, wg[at, :], preferred_element_type=jnp.float32)
            up_sum[...] += jnp.dot(part, wu[at, :], preferred_element_type=jnp.float32)

    hops = {}
    last = n // 2 - 1
    for t in range(n // 2):
        arrived_at = [ring_device(lax.rem(pos + n + t * ways[1 - d], n), n) for d in range(2)]
        for i in range(pieces):
            for d in range(2):
                if t:
                    hops[i, d, t - 1].wait_recv()
                if t == last and i % 2 != d:
                    continue
                part = packed.at[arrived_at[d], i * lines_at : (i + 1) * lines_at, :]
                at = (i * 2 + d) * (n // 2) + t
                hops[i, d, t] = push(part, part, s_send.at[at], s_recv.at[at], nexts[d])
        if t == 0:
            own_gain.wait()
            for copy in scales:
                copy.wait_recv()
            loads[0].wait()
            loads[1].wait()
        for d in range(2 if t else 1):
            expand(arrived_at[d])
    for i in range(pieces):
        hops[i, i % 2, last].wait_recv()
    expand(ring_device(lax.rem(pos + n // 2, n), n))
    inverse = lax.rsqrt(state[0] / depth + 1e-05)
    gate = jax.nn.sigmoid(inverse * jnp.sum(state[1], axis=1, keepdims=True))
    inner = (jax.nn.silu(inverse * gate_sum[...]) * (inverse * up_sum[...])).astype(jnp.bfloat16)
    loads[2].wait()

    def partial(k, side):
        at = lax.rem(z + k, nz) * 2 + side
        return jnp.dot(inner, wd[:, cut(at * block, block)], preferred_element_type=jnp.float32)

    order = list(range(1, nz)) + [0]
    pairs = {}
    for k in order:
        p_buf[k] = partial(k, 1 - x).astype(jnp.bfloat16)
        pairs[k] = push(p_buf.at[k], x_buf.at[k], x_send.at[k], x_recv.at[k], partner)
    for k in order:
        mine[k] = partial(k, x)
    sent = []
    for k in order:
        pairs[k].wait_recv()
        if k:
            s_buf[k] = (mine[k] + x_buf[k].astype(jnp.float32)).astype(jnp.bfloat16)
            sent.append(push(s_buf.at[k], z_buf.at[k], z_send.at[k], z_recv.at[k], along[k - 1]))
    total = mine[0] + x_buf[0].astype(jnp.float32)
    for k in range(1, nz):
        sent[k - 1].wait_recv()
        total += z_buf[k].astype(jnp.float32)
    weighted = (gate * total).astype(jnp.bfloat16)
    w_buf[...] = crossed(pack, weighted).astype(jnp.bfloat16)

    def deliver(i):
        to = lax.rem(me + i, n)
        at = turn * ne + place
        return pltpu.make_async_remote_copy(
            src_ref=w_buf.at[cut(to * cap, cap), :],
            dst_ref=o_ref.at[cut(place * cap, cap), cut(turn * block, block)],
            send_sem=t_send.at[i], recv_sem=t_recv.at[at],
            device_id={"seq": to, "exp": target}, device_id_type=MESH,
        )

    home = pltpu.make_async_copy(
        w_buf.at[cut(me * cap, cap), :], o_ref.at[cut(place * cap, cap), cut(turn * block, block)], own.at[2]
    )
    for i in range(1, n):
        deliver(i).start()

    @pl.when(stays)
    def _():
        home.start()

    @pl.when(jnp.logical_not(stays))
    def _():
        deliver(0).start()

    for k in range(per):
        for e in range(ne):
            arrival = pltpu.make_async_remote_copy(
                src_ref=w_buf.at[cut(me * cap, cap), :],
                dst_ref=o_ref.at[e * cap : (e + 1) * cap, k * block : (k + 1) * block],
                send_sem=t_send.at[0], recv_sem=t_recv.at[k * ne + e],
                device_id=partner, device_id_type=MESH,
            )

            @pl.when(jnp.logical_not(to_self(k, e)))
            def _():
                arrival.wait_recv()

    @pl.when(stays)
    def _():
        home.wait()

    @pl.when(jnp.logical_not(stays))
    def _():
        deliver(0).wait_send()

    for i in range(1, n):
        deliver(i).wait_send()
    for k in range(share):
        for e in range(ne):
            handed = hand(k, e)

            @pl.when(jnp.logical_not(hand_self(k, e)))
            def _():
                handed.wait_send()

    for copy in scales + list(hops.values()) + list(pairs.values()) + sent:
        copy.wait_send()


def run_experts(hidden_state, picks, norm_gain, router, w_gate, w_up, w_down, n, ne, cap):
    tokens, width = hidden_state.shape
    count, slots = picks.shape[1], n * cap
    depth, hidden = w_gate.shape
    nz, block = n // 2, depth // n
    bf, f32 = jnp.bfloat16, jnp.float32
    inside = pl.BlockSpec(memory_space=pltpu.VMEM)
    outside = pl.BlockSpec(memory_space=pltpu.HBM)
    slab = pltpu.VMEM((nz, count, block), bf)
    sems = lambda size: pltpu.SemaphoreType.DMA((size,))
    return pl.pallas_call(
        functools.partial(experts_kernel, n, ne, cap),
        out_shape=(
            jax.ShapeDtypeStruct((ne * cap, width), bf),
            jax.ShapeDtypeStruct((ne * cap, tokens), bf),
        ),
        in_specs=[inside] * 4 + [outside] * 3,
        out_specs=(outside, inside),
        scratch_shapes=[
            pltpu.VMEM((depth, hidden), bf), pltpu.VMEM((depth, hidden), bf), pltpu.VMEM((hidden, depth), bf),
            pltpu.VMEM((ne * cap, width), bf), pltpu.VMEM((slots, block), bf),
            pltpu.VMEM((n, count, block), bf), pltpu.VMEM((1, depth), f32),
            pltpu.VMEM((count, hidden), f32), pltpu.VMEM((count, hidden), f32), pltpu.VMEM((nz, count, block), f32),
            slab, slab, slab, slab, pltpu.VMEM((slots, block), bf),
            sems(3), sems(ne * n), sems(ne * n), sems(ne), sems(ne), sems(4 * n), sems(4 * n),
            sems(nz), sems(nz), sems(nz), sems(nz), sems(n), sems(n), sems(3),
        ],
        compiler_params=pltpu.CompilerParams(
            collective_id=2, has_side_effects=True, vmem_limit_bytes=44 * 1024 * 1024
        ),
    )(hidden_state, picks, norm_gain, router.reshape(1, -1), w_gate, w_up, w_down)


def flash_kernel(block, border_ref, q_ref, k_ref, v_ref, o_ref):
    at = pl.program_id(1)
    border = border_ref[0]
    q_start = at * block
    rows = q_start + lax.broadcasted_iota(jnp.int32, (block, 1), 0)
    low = jnp.where(rows >= border, border, 0)
    steps = lax.broadcasted_iota(jnp.int32, (block, block), 1)
    q = q_ref[...]
    scale = math.log2(math.e) / math.sqrt(HD)

    def scored(j):
        start = pl.multiple_of(j * block, block)
        s = lax.dot_general(
            q, k_ref[pl.ds(start, block), :], (((1,), (1,)), ((), ())), preferred_element_type=jnp.float32
        )
        return s * scale, start

    def mix(p, start):
        return jnp.dot(
            p.astype(jnp.bfloat16), v_ref[pl.ds(start, block), :], preferred_element_type=jnp.float32
        )

    s, start = scored(at)
    s = jnp.where((steps >= low - start) & (steps <= rows - start), s, -jnp.inf)
    top = jnp.max(s, axis=1, keepdims=True)
    p = jnp.exp2(s - top)
    state = (top, jnp.sum(p, axis=1, keepdims=True), mix(p, start))

    def step(j, state):
        top, total, out = state
        s, start = scored(j)
        s = jnp.where(steps >= low - start, s, -jnp.inf)
        new_top = jnp.maximum(top, jnp.max(s, axis=1, keepdims=True))
        factor = jnp.exp2(top - new_top)
        p = jnp.exp2(s - new_top)
        return (
            new_top,
            total * factor + jnp.sum(p, axis=1, keepdims=True),
            out * factor + mix(p, start),
        )

    begin = jnp.where(q_start >= border, border // block, 0)
    top, total, out = lax.fori_loop(begin, at, step, state)
    o_ref[...] = (out / total).astype(o_ref.dtype)


def flash(queries, keys, values, border):
    rows, width = queries.shape
    block = block_rows
    return pl.pallas_call(
        functools.partial(flash_kernel, block),
        out_shape=jax.ShapeDtypeStruct((rows, width), queries.dtype),
        grid_spec=pltpu.PrefetchScalarGridSpec(
            num_scalar_prefetch=1,
            grid=(width // HD, rows // block),
            in_specs=[
                pl.BlockSpec((block, HD), lambda h, i, b: (i, h)),
                pl.BlockSpec((rows, HD), lambda h, i, b: (0, h)),
                pl.BlockSpec((rows, HD), lambda h, i, b: (0, h)),
            ],
            out_specs=pl.BlockSpec((block, HD), lambda h, i, b: (i, h)),
        ),
    )(border, queries, keys, values)


def attend_by_head(queries, keys, values, documents, n, n_exp):
    border = jnp.sum((documents == 0).astype(jnp.int32)).reshape(1)
    q_all, k_all, v_all = heads_out(queries, keys, values, n)
    return heads_back(flash(q_all, k_all, v_all, border), n, n_exp)


def chain_kernel(
    nz, ne, group, docs_ref, q_ref, k_ref, v_ref, res_ref, w_ref, o_ref,
    q0, q1, q2, kb, vb, o0, o1, c0, c1, s2, s1, p2, p1, back, att, proj, acc, res,
    load, x_send, x_recv, d0_send, d0_recv, d1_send, d1_recv, u2_send, u2_recv,
    u1_send, u1_recv, b_send, b_recv, y_send, y_recv, m_send, m_recv,
    r_send, r_recv, w_sem, res_sem,
):
    me = lax.axis_index("seq")
    place = lax.axis_index("exp")
    z, x = me // 2, lax.rem(me, 2)
    y, core = place // 2, lax.rem(place, 2)
    ny = ne // 2
    tokens = q_ref.shape[0]
    steps = 2 * group
    up = {"seq": lax.rem(z + 1, nz) * 2 + x}
    down = {"seq": lax.rem(z + nz - 1, nz) * 2 + x}
    partner = {"seq": z * 2 + 1 - x}
    sibling = {"exp": y * 2 + 1 - core}
    far_place = lax.rem(y + 1, ny) * 2 + core
    far = {"exp": far_place}
    has1, has2, low1 = z + 1 < nz, z + 2 < nz, z >= 1
    border = jnp.sum(
        jnp.sum((docs_ref[...] == 0).astype(jnp.int32), axis=1, keepdims=True), axis=0, keepdims=True
    )
    scale = math.log2(math.e) / math.sqrt(HD)
    greet([up, down, partner, sibling, far])

    def remote(src, dst, send, recv, peer):
        return pltpu.make_async_remote_copy(
            src_ref=src, dst_ref=dst, send_sem=send, recv_sem=recv, device_id=peer, device_id_type=MESH
        )

    def half(ref, h, side):
        return ref.at[h, cut(side * tokens, tokens), :]

    def columns(ref, h, side):
        return ref.at[:, cut((side * group + h) * HD, HD)]

    def loads(h):
        return (
            pltpu.make_async_copy(columns(q_ref, h, x), q0.at[2 * h], load.at[3 * h]),
            pltpu.make_async_copy(columns(k_ref, h, x), half(kb, h, x), load.at[3 * h + 1]),
            pltpu.make_async_copy(columns(v_ref, h, x), half(vb, h, x), load.at[3 * h + 2]),
        )

    def swaps(h):
        side = 1 - x
        return tuple(
            remote(columns(src, h, side), dst, x_send.at[3 * h + t], x_recv.at[3 * h + t], partner)
            for t, (src, dst) in enumerate(
                ((q_ref, q0.at[2 * h + 1]), (k_ref, half(kb, h, x)), (v_ref, half(vb, h, x)))
            )
        )

    def q_down(t):
        return remote(q0.at[t], q1.at[t], d0_send.at[t], d0_recv.at[t], down)

    def q_further(t):
        return remote(q1.at[t], q2.at[t], d1_send.at[t], d1_recv.at[t], down)

    def part2_up(t):
        return (
            remote(s2.at[t], p2.at[t], u2_send.at[t], u2_recv.at[t], up),
        )

    def part1_up(t):
        return (
            remote(s1.at[t], p1.at[t], u1_send.at[t], u1_recv.at[t], up),
        )

    def spot(at, t):
        return att.at[t, :, cut(at * HD, HD)]

    def give_back(t):
        return remote(back.at[t // 2], spot(place, t), b_send.at[t // 2], b_recv.at[t // 2], partner)

    def to_far(t):
        return remote(spot(place, t), spot(place, t), y_send.at[t], y_recv.at[t], far)

    def to_sibling(t):
        return remote(spot(place, t), spot(place, t), m_send.at[t], m_recv.at[t], sibling)

    def relay(t):
        return remote(spot(far_place, t), spot(far_place, t), r_send.at[t], r_recv.at[t], sibling)

    def proj_loads(t):
        side = x + (t % 2) * (1 - 2 * x)
        return [
            pltpu.make_async_copy(
                w_ref.at[cut(((e * 2 + side) * group + t // 2) * HD, HD), :],
                proj.at[t, e * HD : (e + 1) * HD, :],
                w_sem.at[t, e],
            )
            for e in range(ne)
        ]

    res_load = pltpu.make_async_copy(res_ref, res, res_sem)

    tile = HD
    tiles = tokens // tile
    span = kb.shape[1]
    key_base = z * span
    diagonal = lax.broadcasted_iota(jnp.int32, (tile, tile), 0) == lax.broadcasted_iota(
        jnp.int32, (tile, tile), 1
    )

    big = 2 * tile
    at = lax.broadcasted_iota(jnp.int32, (big, tokens), 1)

    def attend(q_of, level, t, put, blocks):
        h = t // 2
        side = x + lax.rem(t, 2) * (1 - 2 * x)
        base = ((z + level) * 2 + side) * tokens - key_base
        edge = border - key_base

        def score(r):
            rows = base + r * big + lax.broadcasted_iota(jnp.int32, (big, 1), 0)
            low = jnp.where(rows >= edge, edge, -key_base)
            out = []
            for b in range(blocks):
                s = lax.dot_general(
                    q_of[r * big : (r + 1) * big, :], kb[h, b * tokens : (b + 1) * tokens, :],
                    (((1,), (1,)), ((), ())), preferred_element_type=jnp.float32,
                )
                seen = at >= low - b * tokens
                if level == 0 and b == blocks - 1:
                    seen = seen & (at <= rows - b * tokens)
                out.append(jnp.where(seen, s, -1e30))
            return out

        later = score(0)
        for r in range(tokens // big):
            now = later
            if (r + 1) * big < tokens:
                later = score(r + 1)
            top = jnp.max(functools.reduce(jnp.maximum, now), axis=1, keepdims=True) * scale
            total = jnp.zeros((big, 1), jnp.float32)
            out = jnp.zeros((big, HD), jnp.float32)
            for b, s in enumerate(now):
                p = jnp.exp2(s * scale - top)
                total += jnp.sum(p, axis=1, keepdims=True)
                out += jnp.dot(
                    p.astype(jnp.bfloat16), vb[h, b * tokens : (b + 1) * tokens, :],
                    preferred_element_type=jnp.float32,
                )
            put(r * big, out / total, top + jnp.log2(total))

    lines_at = tokens // tile

    def note(ref, i, row, level):
        rest = jnp.sum(jnp.where(diagonal, level, 0.0), axis=0, keepdims=True)
        for k in range(3):
            at = tokens + k * lines_at + row
            part = rest.astype(jnp.bfloat16)
            ref[i, at : at + 1, :] = part
            rest = rest - part.astype(jnp.float32)

    def upright(ref, r):
        line = jnp.zeros((1, tile), jnp.float32)
        for k in range(3):
            at = tokens + k * lines_at + r
            line += ref[at : at + 1, :].astype(jnp.float32)
        return jnp.sum(jnp.where(diagonal, line, 0.0), axis=1, keepdims=True)

    def joined(out, level, p_of, r):
        other = upright(p_of, r)
        top = jnp.maximum(level, other)
        mine, theirs = jnp.exp2(level - top), jnp.exp2(other - top)
        both = mine + theirs
        out = (out * mine + p_of[r * tile : (r + 1) * tile, :].astype(jnp.float32) * theirs) / both
        return out, top + jnp.log2(both)

    for h in range(group):
        for copy in swaps(h):
            copy.start()
        for copy in loads(h):
            copy.start()

    for t in range(steps):
        for copy in proj_loads(t):
            copy.start()
    res_load.start()

    def send_own(t):
        @pl.when(lax.rem(t, 2) == 0)
        def _():
            loads(t // 2)[0].wait()

        @pl.when(lax.rem(t, 2) == 1)
        def _():
            swaps(t // 2)[0].wait_recv()

        @pl.when(low1)
        def _():
            q_down(t).start()

    def forward(t):
        @pl.when(has1)
        def _():
            q_down(t).wait_recv()

            @pl.when(low1)
            def _():
                q_further(t).start()

    def spread(t):
        to_far(t).start()
        to_sibling(t).start()

    send_own(jnp.int32(0))
    send_own(jnp.int32(1))
    forward(jnp.int32(0))

    def step(i, carry):
        live = i < steps

        @pl.when(i + 2 < steps)
        def _():
            send_own(i + 2)

        @pl.when(i + 1 < steps)
        def _():
            forward(i + 1)

        @pl.when(live & (lax.rem(i, 2) == 0))
        def _():
            for copy in loads(i // 2)[1:]:
                copy.wait()
            for copy in swaps(i // 2)[1:]:
                copy.wait_recv()

        @pl.when(live & has2)
        def _():
            q_further(i).wait_recv()

            def put(at, out, level):
                s2[i, at : at + big, :] = out.astype(jnp.bfloat16)
                for r in range(big // tile):
                    row = at // tile + r
                    note(s2, i, row, level[r * tile : (r + 1) * tile])

            attend(q2.at[i], 2, i, put, 2)
            for copy in part2_up(i):
                copy.start()

        @pl.when(i == 1)
        def _():
            res_load.wait()
            acc[...] = res[...].astype(jnp.float32)

        t1 = i - 1

        @pl.when((t1 >= 0) & (t1 < steps) & has1)
        def _():
            def put(r, out, level):
                s1[t1, r * tile : (r + 1) * tile, :] = out.astype(jnp.bfloat16)
                note(s1, t1, r, level)

            @pl.when(low1)
            def _():
                for copy in part2_up(t1):
                    copy.wait_recv()
                for r in range(tiles):
                    put(r, *joined(o1[t1, r * tile : (r + 1) * tile, :], c1[t1, r * tile : (r + 1) * tile, :], p2.at[t1], r))

            @pl.when(jnp.logical_not(low1))
            def _():
                for r in range(tiles):
                    put(r, o1[t1, r * tile : (r + 1) * tile, :], c1[t1, r * tile : (r + 1) * tile, :])

            for copy in part1_up(t1):
                copy.start()

        @pl.when(live & has1)
        def _():
            def put(at, out, level):
                o1[i, at : at + big, :] = out
                c1[i, at : at + big, :] = level

            attend(q1.at[i], 1, i, put, 2)

        t0 = i - 2

        @pl.when((t0 >= 0) & (t0 < steps))
        def _():
            def finish(put):
                @pl.when(low1)
                def _():
                    for copy in part1_up(t0):
                        copy.wait_recv()
                    for r in range(tiles):
                        out, level = joined(o0[t0, r * tile : (r + 1) * tile, :], c0[t0, r * tile : (r + 1) * tile, :], p1.at[t0], r)
                        put(r, out)

                @pl.when(jnp.logical_not(low1))
                def _():
                    for r in range(tiles):
                        put(r, o0[t0, r * tile : (r + 1) * tile, :])

            @pl.when(lax.rem(t0, 2) == 0)
            def _():
                def put(r, out):
                    att[t0, r * tile : (r + 1) * tile, cut(place * HD, HD)] = out.astype(jnp.bfloat16)

                finish(put)
                spread(t0)

            @pl.when(lax.rem(t0, 2) == 1)
            def _():
                def put(r, out):
                    back[t0 // 2, r * tile : (r + 1) * tile, :] = out.astype(jnp.bfloat16)

                finish(put)
                give_back(t0).start()

        @pl.when(live)
        def _():
            def put(at, out, level):
                o0[i, at : at + big, :] = out
                c0[i, at : at + big, :] = level

            first_half = lax.rem(i, 2) == x

            @pl.when(first_half)
            def _():
                attend(q0.at[i], 0, i, put, 1)

            @pl.when(jnp.logical_not(first_half))
            def _():
                attend(q0.at[i], 0, i, put, 2)

        t4 = i - 3

        @pl.when((t4 >= 0) & (t4 < steps) & (lax.rem(t4, 2) == 1))
        def _():
            give_back(t4).wait_recv()
            spread(t4)

        t5 = i - 5

        @pl.when((t5 >= 0) & (t5 < steps))
        def _():
            to_far(t5).wait_recv()
            relay(t5).start()

        t6 = i - 6

        @pl.when((t6 >= 0) & (t6 < steps))
        def _():
            to_sibling(t6).wait_recv()
            relay(t6).wait_recv()
            for copy in proj_loads(t6):
                copy.wait()

            acc[...] += jnp.dot(att[t6], proj[t6], preferred_element_type=jnp.float32)

        return carry

    lax.fori_loop(0, steps + 6, step, 0)
    o_ref[...] = acc[...].astype(o_ref.dtype)


    def settle(t, carry):
        to_far(t).wait_send()
        to_sibling(t).wait_send()
        relay(t).wait_send()

        @pl.when(low1)
        def _():
            q_down(t).wait_send()

            @pl.when(has1)
            def _():
                q_further(t).wait_send()

        @pl.when(has1)
        def _():
            for copy in part1_up(t):
                copy.wait_send()

        @pl.when(has2)
        def _():
            for copy in part2_up(t):
                copy.wait_send()

        @pl.when(lax.rem(t, 2) == 1)
        def _():
            give_back(t).wait_send()
            for copy in swaps(t // 2):
                copy.wait_send()

        return carry

    lax.fori_loop(0, steps, settle, 0)


def attend_by_chain(queries, keys, values, documents, residual, out_proj, n, n_exp):
    tokens, width = queries.shape
    group = width // HD // 2
    steps = 2 * group
    nz = n // 2
    features = out_proj.shape[1]
    outside = pl.BlockSpec(memory_space=pltpu.HBM)
    inside = pl.BlockSpec(memory_space=pltpu.VMEM)
    bf, f32 = jnp.bfloat16, jnp.float32
    chunks = pltpu.VMEM((steps, tokens, HD), bf)
    side = pltpu.VMEM((group, 2 * tokens, HD), bf)
    wide = pltpu.VMEM((steps, tokens, HD), f32)
    thin = pltpu.VMEM((steps, tokens, 1), f32)
    noted = pltpu.VMEM((steps, tokens + -(-3 * (tokens // HD) // 16) * 16, HD), bf)
    sems = lambda count: pltpu.SemaphoreType.DMA((count,))
    return pl.pallas_call(
        functools.partial(chain_kernel, nz, n_exp, group),
        out_shape=jax.ShapeDtypeStruct((tokens, features), queries.dtype),
        in_specs=[inside] + [outside] * 5,
        out_specs=inside,
        scratch_shapes=[chunks] * 3 + [side] * 2 + [wide] * 2 + [thin] * 2 + [noted] * 4
        + [pltpu.VMEM((group, tokens, HD), bf), pltpu.VMEM((steps, tokens, n_exp * HD), bf)]
        + [pltpu.VMEM((steps, n_exp * HD, features), bf), pltpu.VMEM((tokens, features), f32)]
        + [pltpu.VMEM((tokens, features), bf)]
        + [sems(3 * group)] * 3 + [sems(steps)] * 8 + [sems(group)] * 2 + [sems(steps)] * 6
        + [pltpu.SemaphoreType.DMA((steps, n_exp)), pltpu.SemaphoreType.DMA(())],
        compiler_params=pltpu.CompilerParams(
            collective_id=0, has_side_effects=True, vmem_limit_bytes=54 * 1024 * 1024
        ),
    )(documents.reshape(-1, HD), queries, keys, values, residual, out_proj)


def attend_by_token(queries, keys, values, documents):
    tokens = queries.shape[0]
    heads_here = queries.shape[1] // HD
    seq_pos = lax.axis_index("seq")
    start_row = seq_pos * tokens
    query_pos = start_row + jnp.arange(tokens, dtype=jnp.int32)
    query_doc = lax.dynamic_slice_in_dim(documents, start_row, tokens, 0)
    query_heads = queries.reshape(tokens, heads_here, HD)
    score_scale = 1.0 / math.sqrt(HD)

    def attend(state, key_rows, value_rows, key_start):
        row_count = key_rows.shape[0]
        key_pos = key_start + jnp.arange(row_count, dtype=jnp.int32)
        key_doc = lax.dynamic_slice_in_dim(documents, key_start, row_count, 0)
        scores = (
            jnp.einsum(
                "qhd,khd->qhk",
                query_heads,
                key_rows.reshape(row_count, heads_here, HD),
                preferred_element_type=jnp.float32,
            )
            * score_scale
        )
        allowed = (key_pos[None, :] <= query_pos[:, None]) & (
            key_doc[None, :] == query_doc[:, None]
        )
        scores = jnp.where(allowed[:, None, :], scores, -jnp.inf)
        running_max, running_sum, running_out = state
        new_max = jnp.maximum(running_max, jnp.max(scores, axis=2))
        factor = jnp.exp(running_max - new_max)
        weights = jnp.exp(scores - new_max[:, :, None])
        running_sum = running_sum * factor + jnp.sum(weights, axis=2)
        running_out = running_out * factor[:, :, None] + jnp.einsum(
            "qhk,khd->qhd",
            weights.astype(jnp.bfloat16),
            value_rows.reshape(row_count, heads_here, HD),
            preferred_element_type=jnp.float32,
        )
        return (new_max, running_sum, running_out)

    def visit_block(state, key_rows, value_rows, key_start):
        row_count = key_rows.shape[0]
        last_doc = lax.dynamic_index_in_dim(documents, key_start + row_count - 1, 0, keepdims=False)
        beyond = (key_start > query_pos[tokens - 1]) | (last_doc < query_doc[0])
        return lax.cond(
            beyond,
            lambda inner_state: inner_state,
            lambda inner_state: attend(inner_state, key_rows, value_rows, key_start),
            state,
        )

    initial = (
        jnp.full((tokens, heads_here), -1e30, jnp.float32),
        jnp.zeros((tokens, heads_here), jnp.float32),
        jnp.zeros((tokens, heads_here, HD), jnp.float32),
    )
    state = initial
    key_piece = lax.all_gather(keys, "seq", axis=0, tiled=True)
    value_piece = lax.all_gather(values, "seq", axis=0, tiled=True)
    row_count = key_piece.shape[0]
    blocks = row_count // block_rows
    key_stack = key_piece.reshape(blocks, block_rows, key_piece.shape[1])
    value_stack = value_piece.reshape(blocks, block_rows, value_piece.shape[1])

    def scan_step(inner_state, block_item):
        block_index, key_rows, value_rows = block_item
        return (visit_block(inner_state, key_rows, value_rows, block_index * block_rows), None)

    state, unused = lax.scan(
        scan_step, state, (jnp.arange(blocks, dtype=jnp.int32), key_stack, value_stack)
    )
    running_max, running_sum, running_out = state
    attended = (
        (running_out / running_sum[:, :, None])
        .reshape(tokens, heads_here * HD)
        .astype(jnp.bfloat16)
    )
    return lax.all_gather(attended, "exp", axis=1, tiled=True)


def shards(
    residual,
    queries,
    keys,
    values,
    documents,
    out_proj,
    modality,
    norm_gain,
    picks,
    router,
    w_gate,
    w_up,
    w_down,
):
    tokens = queries.shape[0]
    seq_pos = lax.axis_index("seq")
    start_row = seq_pos * tokens
    n_seq, n_exp = lax.axis_size("seq"), lax.axis_size("exp")
    if (queries.shape[1] // HD) % n_seq == 0 and n_exp == 4:
        hidden_state = attend_by_chain(
            queries, keys, values, documents, residual, out_proj, n_seq, n_exp
        )
    else:
        attended = attend_by_token(queries, keys, values, documents)
        mixed = jnp.dot(attended, out_proj, preferred_element_type=jnp.float32)
        hidden_state = (residual.astype(jnp.float32) + mixed).astype(jnp.bfloat16)
    returned, placing = run_experts(
        hidden_state, picks, norm_gain, router, w_gate[0], w_up[0], w_down[0], n_seq, n_exp, tokens // 32
    )
    expert_add = lax.dot_general(
        placing, returned, (((0,), (0,)), ((), ())), preferred_element_type=jnp.float32
    )
    return (hidden_state.astype(jnp.float32) + expert_add).astype(jnp.bfloat16)


def solution(mesh):
    return jax.shard_map(
        shards,
        mesh=mesh,
        in_specs=(
            P("seq", "exp"),
            P("seq", "exp"),
            P("seq", "exp"),
            P("seq", "exp"),
            P(),
            P(None, "exp"),
            P("seq"),
            P(None, "exp"),
            P(),
            P(None, "exp"),
            P("exp", None, "seq"),
            P("exp", None, "seq"),
            P("exp", "seq", None),
        ),
        out_specs=P("seq", "exp"),
        check_vma=False,
    )
```
